128 devices in a mesh: past: 8 (over y, z_lo), second: 16 (over x, z_hi, core).
Axes of the slice: x: 4, y: 4, z: 4 (z_hi: 2, z_lo: 2; z = z_hi * 2 + z_lo), core: 2. Of those that a mesh axis runs over, the one named last changes fastest.
Arguments:
- resident: bfloat16 [24576, 24576], P('past', 'second'), may hold values from -6 to 6
- memory: bfloat16 [2, 384, 24576], P(None, None, 'past'), may hold values from -0.0390625 to 0.0390625
- previous: bfloat16 [2, 384, 24576], P(None, None, 'second'), may hold values from -6 to 6
- inverse_part: float32 [2, 384, 384], replicated, may hold values from -0.3125 to 0.3125
- pair_coupling: float32 [32, 32], replicated, may hold values from 0.000318944 to 0.00318944
Outputs:
- fronts: bfloat16 [2, 384, 24576], P(None, None, 'second')
The draws below stay inside these ranges and needn't reach their ends.
All inputs are finite; a program needn't handle non-finite values.
Results may differ from the reference program's by a relative error of at most 0.017.
Values may be sent and summed in bfloat16 or wider, within the bound.
No kernel may reach another device: no remote copies, remote signals or barrier semaphores. Data moves between devices by JAX's collectives and lax.ppermute only.
A program may use at most 128 MiB of HBM per device.

```python
import math
import jax
import jax.numpy as jnp
from jax import lax

ORB = 32
ROWS = 384
COLS = 24576
PAST = 24576
N_PAST = 8


def block_scale(own_key, extent, shards, low, top_value):
    level = 1.0
    for dim, blocks in shards:
        draws = jax.random.uniform(jax.random.fold_in(jax.random.fold_in(own_key, 6), dim), (blocks,), jnp.float32, low / len(shards), top_value / len(shards))
        level = level * jnp.repeat(jnp.exp(draws), extent[dim] // blocks).reshape((-1,) + (1,) * (len(extent) - 1 - dim))
    return level


def centred(rng, dims, spread, reach, cuts=(), dtype=jnp.bfloat16):
    array = spread * jax.random.normal(rng, dims, jnp.float32)
    if cuts:
        array = array * block_scale(rng, dims, cuts, -0.22, 0.18)
    return jnp.clip(array, -reach, reach).astype(dtype)


def setup_inputs(seed: int = 0) -> dict:
    key_of = jax.random.split(jax.random.key(seed), 6)
    return {
        "resident": centred(key_of[0], (PAST, COLS), 1.0, 6.0, ((0, 8), (1, 16))),
        "memory": centred(key_of[1], (2, ROWS, PAST), PAST ** -0.5, 0.0390625, ((2, 8),)),
        "previous": centred(key_of[2], (2, ROWS, COLS), 1.0, 6.0, ((2, 16),)),
        "inverse_part": centred(key_of[3], (2, ROWS, ROWS), ROWS ** -0.5, 0.3125, (), jnp.float32),
        "pair_coupling": jnp.clip(jnp.exp(jax.random.uniform(key_of[4], (ORB, ORB), jnp.float32, math.log(0.000318944), math.log(0.00318944))), 0.000318944, 0.00318944),
    }


step_size = 0.5


def orbital_flip(block, orbitals):
    row_count, col_count = block.shape
    blocks = block.reshape(row_count // orbitals, orbitals, col_count // orbitals, orbitals)
    return blocks.transpose(0, 3, 2, 1).reshape(row_count, col_count)


def history(memory_row, resident):
    depth = PAST // N_PAST
    slabs = resident.reshape(N_PAST, depth, COLS)
    pieces = memory_row.reshape(ROWS, N_PAST, depth).transpose(1, 0, 2)

    def add_term(total, pair):
        term = jnp.dot(pair[0], pair[1], preferred_element_type=jnp.float32)
        rounded = lax.optimization_barrier(term.astype(jnp.bfloat16))
        return total + rounded.astype(jnp.float32), None

    total, _ = lax.scan(add_term, jnp.zeros((ROWS, COLS), jnp.float32), (pieces, slabs))
    return total


def solve_front(summed, prior, inverse_block):
    source = prior.astype(jnp.float32) - step_size * summed
    solved = source + jnp.dot(inverse_block, source, precision=lax.Precision.HIGHEST, preferred_element_type=jnp.float32)
    return solved.astype(jnp.bfloat16)


def self_energy(front, pair_coupling):
    values = front.astype(jnp.float32)
    mirror = orbital_flip(values, ORB)
    blocks = (values * values * mirror).reshape(ROWS // ORB, ORB, COLS // ORB, ORB)
    return (blocks * pair_coupling[None, :, None, :]).reshape(ROWS, COLS).astype(jnp.bfloat16)


def reference(resident, memory, previous, inverse_part, pair_coupling):
    front_one = solve_front(history(memory[0], resident), previous[0], inverse_part[0])
    energy = self_energy(front_one, pair_coupling)
    memory_next = (memory[1].astype(jnp.float32) + orbital_flip(energy, ORB).astype(jnp.float32)).astype(jnp.bfloat16)
    front_two = solve_front(history(memory_next, resident), previous[1], inverse_part[1])
    return jnp.stack([front_one, front_two])
```

```python
import functools

import jax
import jax.numpy as jnp
from jax import lax
from jax.experimental import pallas as pl
from jax.experimental.pallas import tpu as pltpu
from jax.sharding import Mesh, PartitionSpec as P

step_size = 0.5
ORB = 32
f32 = jnp.float32
bf16 = jnp.bfloat16
PASTS = ("y", "zl")
SECONDS = ("x", "zh", "c")
ALL = PASTS + SECONDS
VMEM = pl.BlockSpec(memory_space=pltpu.VMEM)
SMEM = pl.BlockSpec(memory_space=pltpu.SMEM)


def params(megabytes):
    return pltpu.CompilerParams(vmem_limit_bytes=megabytes << 20)


def first_product_kernel(memory_ref, resident_ref, out_ref):
    product = jnp.dot(memory_ref[...], resident_ref[...], preferred_element_type=f32)
    out_ref[...] = product.T.astype(bf16)


def first_product(memory, resident):
    _, rows, depth = memory.shape
    cols = resident.shape[1]
    tile = 512
    return pl.pallas_call(
        first_product_kernel,
        grid=(cols // tile,),
        in_specs=[
            pl.BlockSpec((None, rows, depth), lambda n: (0, 0, 0)),
            pl.BlockSpec((depth, tile), lambda n: (0, n)),
        ],
        out_specs=pl.BlockSpec((tile, rows), lambda n: (n, 0)),
        out_shape=jax.ShapeDtypeStruct((cols, rows), bf16),
        compiler_params=params(40),
        name="first_product",
    )(memory, resident)


def second_product_kernel(place_ref, memory_ref, own_ref, other_ref, resident_ref, out_ref, lhs_ref):
    @pl.when(pl.program_id(0) == 0)
    def _():
        z_high, core = place_ref[0], place_ref[1]
        half = memory_ref.shape[1] // 2
        for side, ref in enumerate((own_ref, other_ref)):
            start = (core ^ side) * half
            for x in range(4):
                near, far = ref[x, 0].astype(f32), ref[x, 1].astype(f32)
                low = jnp.where(z_high == 0, near, far)
                high = jnp.where(z_high == 0, far, near)
                pair = jnp.concatenate([low, high], axis=0).T
                width = pair.shape[1]
                at = pl.ds(pl.multiple_of(start + x * width, 128), width)
                lhs_ref[:, at] = (memory_ref[:, at].astype(f32) + pair).astype(bf16)

    product = jnp.dot(lhs_ref[...], resident_ref[...], preferred_element_type=f32)
    out_ref[...] = product.T.astype(bf16)


def second_product(place, memory, own, other, resident):
    _, rows, depth = memory.shape
    cols = resident.shape[1]
    tile = 512
    whole = lambda n: (0, 0, 0, 0)
    return pl.pallas_call(
        second_product_kernel,
        grid=(cols // tile,),
        in_specs=[
            SMEM,
            pl.BlockSpec((None, rows, depth), lambda n: (1, 0, 0)),
            pl.BlockSpec(own.shape, whole),
            pl.BlockSpec(other.shape, whole),
            pl.BlockSpec((depth, tile), lambda n: (0, n)),
        ],
        out_specs=pl.BlockSpec((tile, rows), lambda n: (n, 0)),
        out_shape=jax.ShapeDtypeStruct((cols, rows), bf16),
        scratch_shapes=[pltpu.VMEM((rows, depth), bf16)],
        compiler_params=params(48),
        name="second_product",
    )(place, memory, own, other, resident)


def solve_into(parts_ref, prior_ref, inverse_ref):
    summed = parts_ref[0].astype(f32)
    for i in range(1, parts_ref.shape[0]):
        summed = summed + parts_ref[i].astype(f32)
    source = prior_ref[...].astype(f32) - step_size * summed
    mixed = lax.dot_general(
        source,
        inverse_ref[...],
        (((1,), (1,)), ((), ())),
        precision=lax.Precision.HIGHEST,
        preferred_element_type=f32,
    )
    return (source + mixed).astype(bf16)


def flipped(values):
    rows, cols = values.shape
    strips = []
    pad = jnp.zeros((128 - ORB, 128), f32)
    for s in range(rows // ORB):
        pieces = []
        for q in range(cols // 128):
            block = values[s * ORB : (s + 1) * ORB, q * 128 : (q + 1) * 128]
            turned = jnp.concatenate([block, pad], axis=0).T
            piece = turned[:ORB]
            for t in range(1, 128 // ORB):
                piece = piece + pltpu.roll(turned[t * ORB : (t + 1) * ORB], t * ORB, 1)
            pieces.append(piece)
        strips.append(jnp.concatenate(pieces, axis=1))
    return jnp.concatenate(strips, axis=0)


def first_solve_kernel(parts_ref, prior_ref, inverse_ref, coupling_ref, front_ref, energy_ref):
    front = solve_into(parts_ref, prior_ref, inverse_ref)
    for i in range(front_ref.shape[0]):
        front_ref[i] = front
    values = front.astype(f32)
    mirror = flipped(values)
    energy_ref[...] = (mirror * mirror * values * coupling_ref[...]).astype(bf16)


def second_solve_kernel(parts_ref, prior_ref, inverse_ref, front_ref):
    front = solve_into(parts_ref, prior_ref, inverse_ref)
    for i in range(front_ref.shape[0]):
        front_ref[i] = front


def first_solve(parts, prior, inverse, coupling):
    return pl.pallas_call(
        first_solve_kernel,
        in_specs=[VMEM] * 4,
        out_specs=[VMEM] * 2,
        out_shape=[
            jax.ShapeDtypeStruct(parts.shape, bf16),
            jax.ShapeDtypeStruct(prior.shape, bf16),
        ],
        compiler_params=params(24),
        name="first_solve",
    )(parts, prior, inverse, coupling)


def second_solve(parts, prior, inverse):
    return pl.pallas_call(
        second_solve_kernel,
        in_specs=[VMEM] * 3,
        out_specs=VMEM,
        out_shape=jax.ShapeDtypeStruct(parts.shape, bf16),
        compiler_params=params(24),
        name="second_solve",
    )(parts, prior, inverse)


def join_kernel(one_ref, two_ref, out_ref):
    for front, ref in enumerate((one_ref, two_ref)):
        width = 2 * ref.shape[1]
        for m in range(ref.shape[0] // 2):
            pair = jnp.concatenate([ref[2 * m], ref[2 * m + 1]], axis=0)
            out_ref[front, :, m * width : (m + 1) * width] = pair.astype(f32).T.astype(bf16)


def join(one, two, rows, cols):
    return pl.pallas_call(
        join_kernel,
        in_specs=[VMEM] * 2,
        out_specs=VMEM,
        out_shape=jax.ShapeDtypeStruct((2, rows, cols), bf16),
        compiler_params=params(24),
        name="join",
    )(one, two)


def turn_pairs(size, flip):
    pairs = []
    for i in range(128):
        rest, c = divmod(i, 2)
        rest, zh = divmod(rest, 2)
        rest, x = divmod(rest, 4)
        y, zl = divmod(rest, 2)
        target = (((x * 2 + zh) * 4 + y) * 2 + (zl ^ flip)) * 2 + c
        pairs.append((i, target))
    return pairs


def per_device(resident, memory, previous, inverse_part, pair_coupling):
    rows = memory.shape[1]
    cols = resident.shape[1]
    width = cols // 8
    past = lax.axis_index("y") * 2 + lax.axis_index("zl")
    place = jnp.stack([lax.axis_index("zh"), lax.axis_index("c")]).astype(jnp.int32)
    priors = lax.dynamic_slice_in_dim(previous, past * width, width, 2).transpose(0, 2, 1)
    coupling = jnp.tile(pair_coupling, (width // ORB, rows // ORB))

    def scatter(partial):
        return lax.all_to_all(partial.reshape(8, width, rows), PASTS, 0, 0, tiled=True)

    parts = scatter(first_product(memory, resident))
    copies, energy = first_solve(parts, priors[0], inverse_part[0], coupling)
    near = lax.ppermute(energy, ALL, turn_pairs(128, 0))
    far = lax.ppermute(energy, ALL, turn_pairs(128, 1))
    both = jnp.broadcast_to(jnp.stack([near, far])[None], (4, 2, width, rows))
    own = lax.all_to_all(both, "x", 0, 0, tiled=True)
    other = lax.ppermute(own, "c", [(0, 1), (1, 0)])
    parts = scatter(second_product(place, memory, own, other, resident))
    front_one = lax.all_to_all(copies, PASTS, 0, 0, tiled=True)
    copies = second_solve(parts, priors[1], inverse_part[1])
    front_two = lax.all_to_all(copies, PASTS, 0, 0, tiled=True)
    return join(front_one, front_two, rows, cols)


def solution(mesh):
    fine = Mesh(mesh.devices.reshape(4, 2, 4, 2, 2), ALL)
    in_specs = (P(PASTS, SECONDS), P(None, None, PASTS), P(None, None, SECONDS), P(), P())
    out_specs = P(None, None, SECONDS)
    return jax.shard_map(
        per_device, mesh=fine, in_specs=in_specs, out_specs=out_specs, check_vma=False
    )
```

```python
import functools

import jax
import jax.numpy as jnp
from jax import lax
from jax.experimental import pallas as pl
from jax.experimental.pallas import tpu as pltpu
from jax.sharding import Mesh, PartitionSpec as P

step_size = 0.5
ORB = 32
f32 = jnp.float32
bf16 = jnp.bfloat16
PASTS = ("y", "zl")
SECONDS = ("x", "zh", "c")
ALL = PASTS + SECONDS
VMEM = pl.BlockSpec(memory_space=pltpu.VMEM)
SMEM = pl.BlockSpec(memory_space=pltpu.SMEM)


def params(megabytes):
    return pltpu.CompilerParams(vmem_limit_bytes=megabytes << 20)


def first_product_kernel(memory_ref, resident_ref, out_ref):
    product = jnp.dot(memory_ref[...], resident_ref[...], preferred_element_type=f32)
    out_ref[...] = product.T.astype(bf16)


def first_product(memory, resident):
    _, rows, depth = memory.shape
    cols = resident.shape[1]
    tile = 512
    return pl.pallas_call(
        first_product_kernel,
        grid=(cols // tile,),
        in_specs=[
            pl.BlockSpec((None, rows, depth), lambda n: (0, 0, 0)),
            pl.BlockSpec((depth, tile), lambda n: (0, n)),
        ],
        out_specs=pl.BlockSpec((tile, rows), lambda n: (n, 0)),
        out_shape=jax.ShapeDtypeStruct((cols, rows), bf16),
        compiler_params=params(56),
        name="first_product",
    )(memory, resident)


def place_pair(own, other, first, at, out_ref, base_ref):
    near, far = own.astype(f32), other.astype(f32)
    low = jnp.where(first == 0, near, far)
    high = jnp.where(first == 0, far, near)
    pair = jnp.concatenate([low, high], axis=0).T
    if base_ref is not None:
        pair = pair + base_ref[:, at].astype(f32)
    out_ref[:, at] = pair.astype(bf16)


def second_product_kernel(place_ref, memory_ref, *refs):
    chunk_refs, resident_ref, out_ref, lhs_ref = refs[:16], refs[16], refs[17], refs[18]

    @pl.when(pl.program_id(0) == 0)
    def _():
        x, z_high, core = place_ref[0], place_ref[1], place_ref[2]
        half = memory_ref.shape[1] // 2
        width = half // 4
        for side in range(2):
            for dx in range(4):
                own, other = chunk_refs[side * 8 + dx * 2], chunk_refs[side * 8 + dx * 2 + 1]
                start = (core ^ side) * half + ((x - dx) & 3) * width
                at = pl.ds(pl.multiple_of(start, 128), width)
                place_pair(own[...], other[...], z_high, at, lhs_ref, memory_ref)

    product = jnp.dot(lhs_ref[...], resident_ref[...], preferred_element_type=f32)
    out_ref[...] = product.T.astype(bf16)


def second_product(place, memory, chunks, resident):
    _, rows, depth = memory.shape
    cols = resident.shape[1]
    tile = 512
    return pl.pallas_call(
        second_product_kernel,
        grid=(cols // tile,),
        in_specs=[
            SMEM,
            pl.BlockSpec((None, rows, depth), lambda n: (1, 0, 0)),
            *[pl.BlockSpec(chunk.shape, lambda n: (0, 0)) for chunk in chunks],
            pl.BlockSpec((depth, tile), lambda n: (0, n)),
        ],
        out_specs=pl.BlockSpec((tile, rows), lambda n: (n, 0)),
        out_shape=jax.ShapeDtypeStruct((cols, rows), bf16),
        scratch_shapes=[pltpu.VMEM((rows, depth), bf16)],
        compiler_params=params(56),
        name="second_product",
    )(place, memory, *chunks, resident)


def solve_into(parts_ref, prior_ref, inverse_ref):
    summed = parts_ref[0].astype(f32)
    for i in range(1, parts_ref.shape[0]):
        summed = summed + parts_ref[i].astype(f32)
    source = prior_ref[...].astype(f32) - step_size * summed
    mixed = lax.dot_general(
        source,
        inverse_ref[...],
        (((1,), (1,)), ((), ())),
        precision=lax.Precision.HIGHEST,
        preferred_element_type=f32,
    )
    return (source + mixed).astype(bf16)


def flipped(values):
    rows, cols = values.shape
    strips = []
    pad = jnp.zeros((128 - ORB, 128), f32)
    for s in range(rows // ORB):
        pieces = []
        for q in range(cols // 128):
            block = values[s * ORB : (s + 1) * ORB, q * 128 : (q + 1) * 128]
            turned = jnp.concatenate([block, pad], axis=0).T
            piece = turned[:ORB]
            for t in range(1, 128 // ORB):
                piece = piece + pltpu.roll(turned[t * ORB : (t + 1) * ORB], t * ORB, 1)
            pieces.append(piece)
        strips.append(jnp.concatenate(pieces, axis=1))
    return jnp.concatenate(strips, axis=0)


def first_solve_kernel(parts_ref, prior_ref, inverse_ref, coupling_ref, front_ref, energy_ref):
    front = solve_into(parts_ref, prior_ref, inverse_ref)
    front_ref[...] = front
    values = front.astype(f32)
    mirror = flipped(values)
    energy_ref[...] = (mirror * mirror * values * coupling_ref[...]).astype(bf16)


def second_solve_kernel(parts_ref, prior_ref, inverse_ref, front_ref):
    front = solve_into(parts_ref, prior_ref, inverse_ref)
    front_ref[...] = front


def first_solve(parts, prior, inverse, coupling):
    return pl.pallas_call(
        first_solve_kernel,
        in_specs=[VMEM] * 4,
        out_specs=[VMEM] * 2,
        out_shape=[
            jax.ShapeDtypeStruct(prior.shape, bf16),
            jax.ShapeDtypeStruct(prior.shape, bf16),
        ],
        compiler_params=params(24),
        name="first_solve",
    )(parts, prior, inverse, coupling)


def second_solve(parts, prior, inverse):
    return pl.pallas_call(
        second_solve_kernel,
        in_specs=[VMEM] * 3,
        out_specs=VMEM,
        out_shape=jax.ShapeDtypeStruct(prior.shape, bf16),
        compiler_params=params(24),
        name="second_solve",
    )(parts, prior, inverse)


def join_one_kernel(front_ref, out_ref):
    width = front_ref.shape[0] // 4
    for m in range(4):
        at = slice(m * width, (m + 1) * width)
        out_ref[:, at] = front_ref[at, :].astype(f32).T.astype(bf16)


def join_one(front):
    cols, rows = front.shape
    return pl.pallas_call(
        join_one_kernel,
        grid=(1,),
        in_specs=[pl.BlockSpec((cols, rows), lambda i: (0, 0))],
        out_specs=pl.BlockSpec((None, rows, cols), lambda i: (0, 0, 0)),
        out_shape=jax.ShapeDtypeStruct((2, rows, cols), bf16),
        compiler_params=params(24),
        name="join_one",
    )(front)


def join_two_kernel(place_ref, *refs):
    chunk_refs, out_ref = refs[:8], refs[9]
    y, z_low = place_ref[3], place_ref[4]
    width = out_ref.shape[1] // 4
    for dy in range(4):
        at = pl.ds(pl.multiple_of(((y - dy) & 3) * width, 128), width)
        place_pair(chunk_refs[2 * dy][...], chunk_refs[2 * dy + 1][...], z_low, at, out_ref, None)


def join_two(place, chunks, fronts):
    _, rows, cols = fronts.shape
    return pl.pallas_call(
        join_two_kernel,
        grid=(1,),
        in_specs=[
            SMEM,
            *[pl.BlockSpec(chunk.shape, lambda i: (0, 0)) for chunk in chunks],
            pl.BlockSpec(memory_space=pl.ANY),
        ],
        out_specs=pl.BlockSpec((None, rows, cols), lambda i: (1, 0, 0)),
        out_shape=jax.ShapeDtypeStruct(fronts.shape, bf16),
        input_output_aliases={9: 0},
        compiler_params=params(24),
        name="join_two",
    )(place, *chunks, fronts)


def ring(shape, move):
    pairs = []
    for i in range(shape[0] * shape[1]):
        a, b = divmod(i, shape[1])
        c, d = (a + move[0]) % shape[0], b ^ move[1]
        pairs.append((i, c * shape[1] + d))
    return pairs


def spread(value, axes):
    moved = {}
    for move in ((2, 1), (2, 0), (1, 1), (3, 1), (1, 0), (3, 0), (0, 1)):
        moved[move] = lax.ppermute(value, axes, ring((4, 2), move))
    moved[0, 0] = value
    return [moved[a, b] for a in range(4) for b in range(2)]


def turn_pairs():
    pairs = []
    for i in range(128):
        rest, c = divmod(i, 2)
        rest, zh = divmod(rest, 2)
        rest, x = divmod(rest, 4)
        y, zl = divmod(rest, 2)
        pairs.append((i, (((x * 2 + zh) * 4 + y) * 2 + zl) * 2 + c))
    return pairs


def per_device(resident, memory, previous, inverse_part, pair_coupling):
    rows = memory.shape[1]
    cols = resident.shape[1]
    width = cols // 8
    past = lax.axis_index("y") * 2 + lax.axis_index("zl")
    place = jnp.stack([lax.axis_index(name) for name in ("x", "zh", "c", "y", "zl")]).astype(jnp.int32)
    priors = lax.dynamic_slice_in_dim(previous, past * width, width, 2).transpose(0, 2, 1)
    coupling = jnp.tile(pair_coupling, (width // ORB, rows // ORB))

    def scatter(partial):
        return lax.all_to_all(partial.reshape(8, width, rows), PASTS, 0, 0, tiled=True)

    parts = scatter(first_product(memory, resident))
    front_one, energy = first_solve(parts, priors[0], inverse_part[0], coupling)
    whole_one = lax.all_gather(front_one, PASTS, axis=0, tiled=True)
    turned = lax.ppermute(energy, ALL, turn_pairs())
    own = spread(turned, ("x", "zh"))
    other = [lax.ppermute(chunk, "c", [(0, 1), (1, 0)]) for chunk in own]
    parts = scatter(second_product(place, memory, own + other, resident))
    front_two = second_solve(parts, priors[1], inverse_part[1])
    chunks = spread(front_two, PASTS)
    return join_two(place, chunks, join_one(whole_one))


def solution(mesh):
    fine = Mesh(mesh.devices.reshape(4, 2, 4, 2, 2), ALL)
    in_specs = (P(PASTS, SECONDS), P(None, None, PASTS), P(None, None, SECONDS), P(), P())
    out_specs = P(None, None, SECONDS)
    return jax.shard_map(
        per_device, mesh=fine, in_specs=in_specs, out_specs=out_specs, check_vma=False
    )
```

```python
import functools

import jax
import jax.numpy as jnp
from jax import lax
from jax.experimental import pallas as pl
from jax.experimental.pallas import tpu as pltpu
from jax.sharding import Mesh, PartitionSpec as P

step_size = 0.5
ORB = 32
f32 = jnp.float32
bf16 = jnp.bfloat16
PASTS = ("y", "zl")
SECONDS = ("x", "zh", "c")
ALL = PASTS + SECONDS
SWAP = [(0, 1), (1, 0)]
X, ZH, C, Y, ZL = range(5)


VMEM = pl.BlockSpec(memory_space=pltpu.VMEM)
SMEM = pl.BlockSpec(memory_space=pltpu.SMEM)


def in_hbm(array):
    return pltpu.with_memory_space_constraint(array, pltpu.HBM)


def params(megabytes):
    return pltpu.CompilerParams(vmem_limit_bytes=megabytes << 20)


def cost(flops, nbytes):
    return pl.CostEstimate(flops=flops, bytes_accessed=nbytes, transcendentals=0)


def whole(shape):
    return pl.BlockSpec(shape, lambda i, place: (0,) * len(shape))


def placed_call(kernel, place, args, in_specs, out_specs, out_shape, name, limit, estimate, grid=1, scratch=(), aliases=None):
    return pl.pallas_call(
        kernel,
        grid_spec=pltpu.PrefetchScalarGridSpec(
            num_scalar_prefetch=1,
            grid=(grid,),
            in_specs=in_specs,
            out_specs=out_specs,
            scratch_shapes=list(scratch),
        ),
        out_shape=out_shape,
        input_output_aliases=aliases or {},
        compiler_params=params(limit),
        cost_estimate=cost(*estimate),
        name=name,
    )(place, *args)


def store_shares(place_ref, turned_ref, out_refs):
    width = out_refs[0].shape[0]
    for k, out_ref in enumerate(out_refs):
        share = ((place_ref[Y] & 1) ^ (k >> 1)) * 2 + (place_ref[ZL] ^ (k & 1))
        out_ref[...] = turned_ref[pl.ds(pl.multiple_of(share * width, width), width), :]


def first_half_kernel(place_ref, lhs_ref, resident_ref, *refs):
    out_refs, turned_ref = refs[:4], refs[4]
    step, tile = pl.program_id(0), resident_ref.shape[1]
    product = jnp.dot(lhs_ref[...], resident_ref[...], preferred_element_type=f32)
    turned_ref[pl.ds(pl.multiple_of(step * tile, tile), tile), :] = product.T.astype(bf16)

    @pl.when(step == pl.num_programs(0) - 1)
    def _():
        store_shares(place_ref, turned_ref, out_refs)


def first_half(place, memory, resident, far):
    _, rows, depth = memory.shape
    cols = resident.shape[1]
    width = cols // 8
    tile = 256
    steps = cols // 2 // tile
    return placed_call(
        first_half_kernel,
        place,
        (memory, resident),
        [
            pl.BlockSpec((None, rows, depth), lambda i, place: (0, 0, 0)),
            pl.BlockSpec((depth, tile), lambda i, place: (0, ((place[Y] >> 1) ^ far) * steps + i)),
        ],
        [whole((width, rows))] * 4,
        [jax.ShapeDtypeStruct((width, rows), bf16)] * 4,
        "first_half",
        16,
        (rows * depth * cols, depth * cols + 2 * rows * depth),
        grid=steps,
        scratch=[pltpu.VMEM((cols // 2, rows), bf16)],
    )


def second_half_kernel(far, place_ref, lhs_ref, resident_ref, *refs):
    out_refs, turned_ref = refs[:4], refs[4]
    cols = resident_ref.shape[1] // 2
    at = pl.ds(pl.multiple_of(((place_ref[Y] >> 1) ^ far) * cols, cols), cols)
    product = jnp.dot(lhs_ref[...], resident_ref[:, at], preferred_element_type=f32)
    turned_ref[...] = product.T.astype(bf16)
    store_shares(place_ref, turned_ref, out_refs)


def second_half(place, lhs, resident, far):
    rows, depth = lhs.shape
    cols = resident.shape[1]
    width = cols // 8
    return pl.pallas_call(
        functools.partial(second_half_kernel, far),
        in_specs=[SMEM, VMEM, VMEM],
        out_specs=[VMEM] * 4,
        out_shape=[jax.ShapeDtypeStruct((width, rows), bf16)] * 4,
        scratch_shapes=[pltpu.VMEM((cols // 2, rows), bf16)],
        compiler_params=params(6),
        cost_estimate=cost(rows * depth * cols, 4 * width * rows),
        name="second_half",
    )(place, lhs, resident)


def product(half, place, lhs, resident):
    far = half(place, lhs, resident, 1)
    near = half(place, lhs, resident, 0)
    moves = {}
    for k in range(4):
        moves[2 + (k >> 1), k & 1] = far[k]
        moves[k >> 1, k & 1] = near[k]
    return moves


def bring_kernel(place_ref, resident_ref, memory_ref, previous_ref, resident_out, memory_out, one_out, two_out, prior_ref, turned_ref, sems):
    width, rows = one_out.shape
    cols = pl.ds(pl.multiple_of(place_ref[Y] * 2 * width, 128), 2 * width)
    copies = [
        pltpu.make_async_copy(previous_ref.at[:, :, cols], prior_ref, sems.at[0]),
        pltpu.make_async_copy(memory_ref.at[1], memory_out, sems.at[1]),
        pltpu.make_async_copy(resident_ref, resident_out, sems.at[2]),
    ]
    for copy in copies:
        copy.start()
    copies[0].wait()
    for front, out_ref in enumerate((one_out, two_out)):
        turned_ref[...] = prior_ref[front].astype(f32).T
        share = turned_ref[pl.ds(pl.multiple_of(place_ref[ZL] * width, width), width), :]
        out_ref[...] = share.astype(bf16)
    copies[1].wait()
    copies[2].wait()


def bring(place, resident, memory, previous):
    _, rows, depth = memory.shape
    cols = resident.shape[1]
    width = cols // 8
    anywhere = pl.BlockSpec(memory_space=pltpu.HBM)
    return pl.pallas_call(
        bring_kernel,
        in_specs=[SMEM, anywhere, anywhere, anywhere],
        out_specs=[VMEM] * 4,
        out_shape=[
            jax.ShapeDtypeStruct(resident.shape, bf16),
            jax.ShapeDtypeStruct((rows, depth), bf16),
            jax.ShapeDtypeStruct((width, rows), bf16),
            jax.ShapeDtypeStruct((width, rows), bf16),
        ],
        scratch_shapes=[
            pltpu.VMEM((2, rows, 2 * width), bf16),
            pltpu.VMEM((2 * width, rows), f32),
            pltpu.SemaphoreType.DMA((3,)),
        ],
        compiler_params=params(6),
        cost_estimate=cost(0, 2 * depth * (rows + cols)),
        name="bring",
    )(place, resident, memory, previous)


def place_pair(own, other, first, at, out_ref, base_ref):
    near, far = own.astype(f32), other.astype(f32)
    low = jnp.where(first == 0, near, far)
    high = jnp.where(first == 0, far, near)
    pair = jnp.concatenate([low, high], axis=0).T
    if base_ref is not None:
        pair = pair + base_ref[:, at].astype(f32)
    out_ref[:, at] = pair.astype(bf16)


def next_memory_kernel(place_ref, memory_ref, *refs):
    pair_refs, out_ref = refs[:8], refs[8]
    half = memory_ref.shape[1] // 2
    width = half // 4
    for side in range(2):
        for dx in range(4):
            pair = pair_refs[side * 4 + dx]
            share = ((place_ref[X] - dx) & 3) ^ place_ref[Y]
            start = (place_ref[C] ^ side) * half + share * width
            at = pl.ds(pl.multiple_of(start, 128), width)
            place_pair(pair[0], pair[1], place_ref[ZH], at, out_ref, memory_ref)


def next_memory(place, memory, pairs):
    rows, depth = memory.shape
    return pl.pallas_call(
        next_memory_kernel,
        in_specs=[SMEM] + [VMEM] * 9,
        out_specs=VMEM,
        out_shape=jax.ShapeDtypeStruct((rows, depth), bf16),
        compiler_params=params(6),
        cost_estimate=cost(rows * depth, 6 * rows * depth),
        name="next_memory",
    )(place, memory, *pairs)


def solve_into(part_refs, prior_ref, inverse_ref):
    summed = part_refs[0][...].astype(f32)
    for part_ref in part_refs[1:]:
        summed = summed + part_ref[...].astype(f32)
    source = prior_ref[...].astype(f32) - step_size * summed
    mixed = lax.dot_general(
        source,
        inverse_ref[...],
        (((1,), (1,)), ((), ())),
        precision=lax.Precision.HIGHEST,
        preferred_element_type=f32,
    )
    return (source + mixed).astype(bf16)


def flipped(values):
    rows, cols = values.shape
    strips = []
    pad = jnp.zeros((128 - ORB, 128), f32)
    for s in range(rows // ORB):
        pieces = []
        for q in range(cols // 128):
            block = values[s * ORB : (s + 1) * ORB, q * 128 : (q + 1) * 128]
            turned = jnp.concatenate([block, pad], axis=0).T
            piece = turned[:ORB]
            for t in range(1, 128 // ORB):
                piece = piece + pltpu.roll(turned[t * ORB : (t + 1) * ORB], t * ORB, 1)
            pieces.append(piece)
        strips.append(jnp.concatenate(pieces, axis=1))
    return jnp.concatenate(strips, axis=0)


def first_solve_kernel(place_ref, *refs):
    front_ref, energy_ref = refs[11:]
    front = solve_into(refs[:8], refs[8], refs[9])
    front_ref[...] = front
    values = front.astype(f32)
    mirror = flipped(values)
    rows, cols = values.shape
    coupling = jnp.tile(refs[10][...], (rows // ORB, cols // 128))
    energy_ref[...] = (mirror * mirror * values * coupling).astype(bf16)


def second_solve_kernel(place_ref, *refs):
    refs[10][...] = solve_into(refs[:8], refs[8], refs[9])


def solve(kernel, front, place, parts, prior, inverse, extra, outputs, name):
    width, rows = prior.shape
    return placed_call(
        kernel,
        place,
        (*parts, prior, inverse, *extra),
        [
            *[whole(array.shape) for array in (*parts, prior)],
            pl.BlockSpec((None, rows, rows), lambda i, place: (front, 0, 0)),
            *[whole(array.shape) for array in extra],
        ],
        [whole((width, rows))] * outputs,
        [jax.ShapeDtypeStruct((width, rows), bf16)] * outputs,
        name,
        10,
        (12 * rows * rows * width, 24 * rows * width),
    )


def join_one_kernel(place_ref, *refs):
    pair_refs, out_ref = refs[:4], refs[4]
    width = out_ref.shape[1] // 4
    for dy in range(4):
        at = pl.ds(pl.multiple_of(((place_ref[Y] - dy) & 3) * width, 128), width)
        place_pair(pair_refs[dy][0], pair_refs[dy][1], place_ref[ZL], at, out_ref, None)


def join_one(place, pairs, rows, cols):
    return placed_call(
        join_one_kernel,
        place,
        pairs,
        [whole(pair.shape) for pair in pairs],
        pl.BlockSpec((None, rows, cols), lambda i, place: (0, 0, 0)),
        jax.ShapeDtypeStruct((2, rows, cols), bf16),
        "join_one",
        10,
        (rows * cols, 4 * rows * cols),
    )


def join_two_kernel(place_ref, *refs):
    chunk_refs, out_ref = refs[:8], refs[9]
    width = out_ref.shape[1] // 4
    for dy in range(4):
        at = pl.ds(pl.multiple_of(((place_ref[Y] - dy) & 3) * width, 128), width)
        own, other = chunk_refs[2 * dy][...], chunk_refs[2 * dy + 1][...]
        place_pair(own, other, place_ref[ZL], at, out_ref, None)


def join_two(place, chunks, fronts):
    _, rows, cols = fronts.shape
    return placed_call(
        join_two_kernel,
        place,
        (*chunks, fronts),
        [*[whole(chunk.shape) for chunk in chunks], pl.BlockSpec(memory_space=pl.ANY)],
        pl.BlockSpec((None, rows, cols), lambda i, place: (1, 0, 0)),
        jax.ShapeDtypeStruct(fronts.shape, bf16),
        "join_two",
        10,
        (rows * cols, 4 * rows * cols),
        aliases={9: 0},
    )


def move(value, target):
    pairs = []
    for i in range(128):
        rest, c = divmod(i, 2)
        rest, zh = divmod(rest, 2)
        rest, x = divmod(rest, 4)
        y, zl = divmod(rest, 2)
        y, zl, x, zh = target(y, zl, x, zh)
        pairs.append((i, (((y * 2 + zl) * 4 + x) * 2 + zh) * 2 + c))
    return lax.ppermute(value, ALL, pairs)


def turn(flip):
    return lambda y, zl, x, zh: (x, zh, x ^ y, zl ^ flip)


def scatter(shares):
    parts = []
    for dy, dz in ((2, 1), (2, 0), (3, 1), (3, 0), (1, 1), (1, 0), (0, 1)):
        parts.append(move(shares[dy, dz], lambda y, zl, x, zh: (y ^ dy, zl ^ dz, x, zh)))
    return [*parts, shares[0, 0]]


def spread_pairs(pair, axis):
    pairs = {0: pair}
    for d in (2, 1, 3):
        pairs[d] = lax.ppermute(pair, axis, [(i, (i + d) % 4) for i in range(4)])
    return [pairs[d] for d in range(4)]


def spread_chunks(value):
    chunks = {(0, 0): value}
    for dy, dz in ((2, 1), (2, 0), (1, 1), (3, 1), (1, 0), (3, 0), (0, 1)):
        chunks[dy, dz] = move(value, lambda y, zl, x, zh: ((y + dy) % 4, zl ^ dz, x, zh))
    return [chunks[dy, dz] for dy in range(4) for dz in range(2)]


def per_device(resident, memory, previous, inverse_part, pair_coupling):
    rows, cols = memory.shape[1], resident.shape[1]
    place = jnp.stack([lax.axis_index(name) for name in ("x", "zh", "c", "y", "zl")]).astype(jnp.int32)
    coupling = jnp.tile(pair_coupling, (1, 128 // ORB))

    resident, memory, previous = in_hbm(resident), in_hbm(memory), in_hbm(previous)
    shares = product(first_half, place, memory, resident)
    place, shares[0, 0] = lax.optimization_barrier((place, shares[0, 0]))
    resident, memory, prior_one, prior_two = bring(place, resident, memory, previous)
    parts = scatter(shares)
    front_one, energy = solve(
        first_solve_kernel, 0, place, parts, prior_one, inverse_part, [coupling], 2, "first_solve"
    )
    own = spread_pairs(jnp.stack([move(energy, turn(0)), move(energy, turn(1))]), "x")
    other = [lax.ppermute(pair, "c", SWAP) for pair in own]
    ones = spread_pairs(jnp.stack([front_one, lax.ppermute(front_one, "zl", SWAP)]), "y")
    own, other, ones = lax.optimization_barrier((own, other, ones))
    lhs = next_memory(place, memory, own + other)
    parts = scatter(product(second_half, place, lhs, resident))
    (front_two,) = solve(
        second_solve_kernel, 1, place, parts, prior_two, inverse_part, [], 1, "second_solve"
    )
    chunks = spread_chunks(front_two)
    return join_two(place, chunks, join_one(place, ones, rows, cols))


def solution(mesh):
    fine = Mesh(mesh.devices.reshape(4, 2, 4, 2, 2), ALL)
    in_specs = (P(PASTS, SECONDS), P(None, None, PASTS), P(None, None, SECONDS), P(), P())
    out_specs = P(None, None, SECONDS)
    return jax.shard_map(
        per_device, mesh=fine, in_specs=in_specs, out_specs=out_specs, check_vma=False
    )
```

```python
import functools

import jax
import jax.numpy as jnp
from jax import lax
from jax.experimental import pallas as pl
from jax.experimental.pallas import tpu as pltpu
from jax.sharding import Mesh, PartitionSpec as P

step_size = 0.5
ORB = 32
f32 = jnp.float32
bf16 = jnp.bfloat16
PASTS = ("y", "zl")
SECONDS = ("x", "zh", "c")
ALL = PASTS + SECONDS
SWAP = [(0, 1), (1, 0)]
X, ZH, C, Y, ZL = range(5)


VMEM = pl.BlockSpec(memory_space=pltpu.VMEM)
SMEM = pl.BlockSpec(memory_space=pltpu.SMEM)


def in_hbm(array):
    return pltpu.with_memory_space_constraint(array, pltpu.HBM)


def params(megabytes):
    return pltpu.CompilerParams(vmem_limit_bytes=megabytes << 20)


def cost(flops, nbytes):
    return pl.CostEstimate(flops=flops, bytes_accessed=nbytes, transcendentals=0)


def whole(shape):
    return pl.BlockSpec(shape, lambda i, place: (0,) * len(shape))


def placed_call(kernel, place, args, in_specs, out_specs, out_shape, name, limit, estimate, grid=1, scratch=(), aliases=None):
    return pl.pallas_call(
        kernel,
        grid_spec=pltpu.PrefetchScalarGridSpec(
            num_scalar_prefetch=1,
            grid=(grid,),
            in_specs=in_specs,
            out_specs=out_specs,
            scratch_shapes=list(scratch),
        ),
        out_shape=out_shape,
        input_output_aliases=aliases or {},
        compiler_params=params(limit),
        cost_estimate=cost(*estimate),
        name=name,
    )(place, *args)


def position(y):
    return (y & 1) * 2 + (y >> 1)


def store_shares(place_ref, turned_ref, out_refs):
    width = out_refs[0].shape[0]
    for k, out_ref in enumerate(out_refs):
        share = ((place_ref[Y] >> 1) ^ (k >> 1)) * 2 + (place_ref[ZL] ^ (k & 1))
        out_ref[...] = turned_ref[pl.ds(pl.multiple_of(share * width, width), width), :]


def half_product_kernel(place_ref, lhs_ref, resident_ref, *refs):
    out_refs, turned_ref = refs[:4], refs[4]
    product = jnp.dot(lhs_ref[...], resident_ref[...], preferred_element_type=f32)
    turned_ref[...] = product.T.astype(bf16)
    store_shares(place_ref, turned_ref, out_refs)


def half_product(place, lhs, resident):
    rows, depth = lhs.shape
    cols = resident.shape[1]
    width = cols // 4
    return pl.pallas_call(
        half_product_kernel,
        in_specs=[SMEM, VMEM, VMEM],
        out_specs=[VMEM] * 4,
        out_shape=[jax.ShapeDtypeStruct((width, rows), bf16)] * 4,
        scratch_shapes=[pltpu.VMEM((cols, rows), bf16)],
        compiler_params=params(6),
        cost_estimate=cost(2 * rows * depth * cols, 4 * width * rows),
        name="half_product",
    )(place, lhs, resident)


TILES = 3


def first_product_kernel(place_ref, memory_ref, resident_ref, *refs):
    out_refs, lhs_ref, even_ref, odd_ref, turned_ref, sems = refs[:4], *refs[4:]
    depth, cols = odd_ref.shape
    tile = cols // TILES
    parity = place_ref[Y] & 1

    def tile_copy(half_ref, side, i):
        start = pl.multiple_of((parity ^ side) * cols + i * tile, tile)
        return pltpu.make_async_copy(
            resident_ref.at[:, pl.ds(start, tile)],
            half_ref.at[:, i * tile : (i + 1) * tile],
            sems.at[side * TILES + i],
        )

    memory_copy = pltpu.make_async_copy(memory_ref.at[0], lhs_ref, sems.at[2 * TILES])
    odd = [tile_copy(odd_ref, 1, i) for i in range(TILES)]
    even = [tile_copy(even_ref, 0, i) for i in range(TILES)]
    for copy in (memory_copy, *odd, *even):
        copy.start()
    memory_copy.wait()
    for i, copy in enumerate(odd):
        copy.wait()
        at = slice(i * tile, (i + 1) * tile)
        product = jnp.dot(lhs_ref[...], odd_ref[:, at], preferred_element_type=f32)
        turned_ref[at, :] = product.T.astype(bf16)
    store_shares(place_ref, turned_ref, out_refs)
    for copy in even:
        copy.wait()


def first_product(place, memory, resident):
    _, rows, depth = memory.shape
    cols = resident.shape[1]
    width = cols // 8
    outs = [((width, rows), 4), ((rows, depth), 1), ((depth, cols // 2), 1)]
    shapes = [jax.ShapeDtypeStruct(shape, bf16) for shape, count in outs for _ in range(count)]
    *odd, lhs, even_resident = pl.pallas_call(
        first_product_kernel,
        in_specs=[SMEM] + [pl.BlockSpec(memory_space=pltpu.HBM)] * 2,
        out_specs=[VMEM] * 6,
        out_shape=shapes,
        scratch_shapes=[
            pltpu.VMEM((depth, cols // 2), bf16),
            pltpu.VMEM((cols // 2, rows), bf16),
            pltpu.SemaphoreType.DMA((2 * TILES + 1,)),
        ],
        compiler_params=params(12),
        cost_estimate=cost(rows * depth * cols, 4 * depth * cols),
        name="first_product",
    )(place, memory, resident)
    return odd, lhs, even_resident


def bring_kernel(
    place_ref, memory_ref, previous_ref, resident_ref, memory_out, one_out, two_out, odd_out, even_out, prior_ref, turned_ref, sems
):
    width, rows = one_out.shape
    start = position(place_ref[Y]) * 2 * width
    cols = pl.ds(pl.multiple_of(start, 128), 2 * width)
    copies = [
        pltpu.make_async_copy(previous_ref.at[:, :, cols], prior_ref, sems.at[0]),
        pltpu.make_async_copy(memory_ref.at[1], memory_out, sems.at[1]),
    ]
    half = odd_out.shape[1]
    for side, out_ref in ((1, odd_out), (0, even_out)):
        start = pl.multiple_of(((place_ref[Y] & 1) ^ side) * half, half)
        copies.append(
            pltpu.make_async_copy(resident_ref.at[:, pl.ds(start, half)], out_ref, sems.at[2 + side])
        )
    for copy in copies:
        copy.start()
    copies[0].wait()
    for front, out_ref in enumerate((one_out, two_out)):
        turned_ref[...] = prior_ref[front].astype(f32).T
        share = turned_ref[pl.ds(pl.multiple_of(place_ref[ZL] * width, width), width), :]
        out_ref[...] = share.astype(bf16)
    for copy in copies[1:]:
        copy.wait()


def bring(place, memory, previous, resident):
    _, rows, depth = memory.shape
    cols = resident.shape[1]
    width = previous.shape[2] // 8
    return pl.pallas_call(
        bring_kernel,
        in_specs=[SMEM] + [pl.BlockSpec(memory_space=pltpu.HBM)] * 3,
        out_specs=[VMEM] * 5,
        out_shape=[
            jax.ShapeDtypeStruct((rows, depth), bf16),
            jax.ShapeDtypeStruct((width, rows), bf16),
            jax.ShapeDtypeStruct((width, rows), bf16),
            jax.ShapeDtypeStruct((depth, cols // 2), bf16),
            jax.ShapeDtypeStruct((depth, cols // 2), bf16),
        ],
        scratch_shapes=[
            pltpu.VMEM((2, rows, 2 * width), bf16),
            pltpu.VMEM((2 * width, rows), f32),
            pltpu.SemaphoreType.DMA((4,)),
        ],
        compiler_params=params(6),
        cost_estimate=cost(0, 2 * depth * (rows + cols)),
        name="bring",
    )(place, memory, previous, resident)


def place_pair(own, other, first, at, out_ref, base_ref):
    near, far = own.astype(f32), other.astype(f32)
    low = jnp.where(first == 0, near, far)
    high = jnp.where(first == 0, far, near)
    pair = jnp.concatenate([low, high], axis=0).T
    if base_ref is not None:
        pair = pair + base_ref[:, at].astype(f32)
    out_ref[:, at] = pair.astype(bf16)


def next_memory_kernel(place_ref, memory_ref, *refs):
    pair_refs, out_ref = refs[:8], refs[8]
    half = memory_ref.shape[1] // 2
    width = half // 4
    for side in range(2):
        for dx in range(4):
            pair = pair_refs[side * 4 + dx]
            share = position(((place_ref[X] - dx) & 3) ^ place_ref[Y])
            start = (place_ref[C] ^ side) * half + share * width
            at = pl.ds(pl.multiple_of(start, 128), width)
            place_pair(pair[0], pair[1], place_ref[ZH], at, out_ref, memory_ref)


def next_memory(place, memory, pairs):
    rows, depth = memory.shape
    return pl.pallas_call(
        next_memory_kernel,
        in_specs=[SMEM] + [VMEM] * 9,
        out_specs=VMEM,
        out_shape=jax.ShapeDtypeStruct((rows, depth), bf16),
        compiler_params=params(6),
        cost_estimate=cost(rows * depth, 6 * rows * depth),
        name="next_memory",
    )(place, memory, *pairs)


def solve_into(part_refs, prior_ref, inverse_ref):
    summed = part_refs[0][...].astype(f32)
    for part_ref in part_refs[1:]:
        summed = summed + part_ref[...].astype(f32)
    source = prior_ref[...].astype(f32) - step_size * summed
    mixed = lax.dot_general(
        source,
        inverse_ref[...],
        (((1,), (1,)), ((), ())),
        precision=lax.Precision.HIGHEST,
        preferred_element_type=f32,
    )
    return (source + mixed).astype(bf16)


def flipped(values):
    rows, cols = values.shape
    strips = []
    pad = jnp.zeros((128 - ORB, 128), f32)
    for s in range(rows // ORB):
        pieces = []
        for q in range(cols // 128):
            block = values[s * ORB : (s + 1) * ORB, q * 128 : (q + 1) * 128]
            turned = jnp.concatenate([block, pad], axis=0).T
            piece = turned[:ORB]
            for t in range(1, 128 // ORB):
                piece = piece + pltpu.roll(turned[t * ORB : (t + 1) * ORB], t * ORB, 1)
            pieces.append(piece)
        strips.append(jnp.concatenate(pieces, axis=1))
    return jnp.concatenate(strips, axis=0)


def first_solve_kernel(place_ref, *refs):
    front_ref, energy_ref = refs[11:]
    front = solve_into(refs[:8], refs[8], refs[9])
    front_ref[...] = front
    values = front.astype(f32)
    mirror = flipped(values)
    rows, cols = values.shape
    coupling = jnp.tile(refs[10][...], (rows // ORB, cols // 128))
    energy_ref[...] = (mirror * mirror * values * coupling).astype(bf16)


def second_solve_kernel(place_ref, *refs):
    refs[10][...] = solve_into(refs[:8], refs[8], refs[9])


def solve(kernel, front, place, parts, prior, inverse, extra, outputs, name):
    width, rows = prior.shape
    return placed_call(
        kernel,
        place,
        (*parts, prior, inverse, *extra),
        [
            *[whole(array.shape) for array in (*parts, prior)],
            pl.BlockSpec((None, rows, rows), lambda i, place: (front, 0, 0)),
            *[whole(array.shape) for array in extra],
        ],
        [whole((width, rows))] * outputs,
        [jax.ShapeDtypeStruct((width, rows), bf16)] * outputs,
        name,
        10,
        (12 * rows * rows * width, 24 * rows * width),
    )


def join_one_kernel(place_ref, *refs):
    pair_refs, out_ref = refs[:4], refs[4]
    width = out_ref.shape[1] // 4
    for dy in range(4):
        at = pl.ds(pl.multiple_of(position((place_ref[Y] - dy) & 3) * width, 128), width)
        place_pair(pair_refs[dy][0], pair_refs[dy][1], place_ref[ZL], at, out_ref, None)


def join_one(place, pairs, rows, cols):
    return placed_call(
        join_one_kernel,
        place,
        pairs,
        [whole(pair.shape) for pair in pairs],
        pl.BlockSpec((None, rows, cols), lambda i, place: (0, 0, 0)),
        jax.ShapeDtypeStruct((2, rows, cols), bf16),
        "join_one",
        10,
        (rows * cols, 4 * rows * cols),
    )


def join_two_kernel(place_ref, *refs):
    chunk_refs, out_ref = refs[:8], refs[9]
    width = out_ref.shape[1] // 4
    for dy in range(4):
        at = pl.ds(pl.multiple_of(position((place_ref[Y] - dy) & 3) * width, 128), width)
        own, other = chunk_refs[2 * dy][...], chunk_refs[2 * dy + 1][...]
        place_pair(own, other, place_ref[ZL], at, out_ref, None)


def join_two(place, chunks, fronts):
    _, rows, cols = fronts.shape
    return placed_call(
        join_two_kernel,
        place,
        (*chunks, fronts),
        [*[whole(chunk.shape) for chunk in chunks], pl.BlockSpec(memory_space=pl.ANY)],
        pl.BlockSpec((None, rows, cols), lambda i, place: (1, 0, 0)),
        jax.ShapeDtypeStruct(fronts.shape, bf16),
        "join_two",
        10,
        (rows * cols, 4 * rows * cols),
        aliases={9: 0},
    )


def move(value, target):
    pairs = []
    for i in range(128):
        rest, c = divmod(i, 2)
        rest, zh = divmod(rest, 2)
        rest, x = divmod(rest, 4)
        y, zl = divmod(rest, 2)
        y, zl, x, zh = target(y, zl, x, zh)
        pairs.append((i, (((y * 2 + zl) * 4 + x) * 2 + zh) * 2 + c))
    return lax.ppermute(value, ALL, pairs)


def turn(flip):
    return lambda y, zl, x, zh: (x, zh, x ^ y, zl ^ flip)


def scatter(shares, first):
    parts = []
    for k in (3, 2, 1, 0) if first == 0 else (1, 0, 3, 2):
        dy, dz = first + 2 * (k >> 1), k & 1
        if (dy, dz) == (0, 0):
            parts.append(shares[k])
        else:
            parts.append(move(shares[k], lambda y, zl, x, zh: (y ^ dy, zl ^ dz, x, zh)))
    return parts


def spread_pairs(pair, axis):
    pairs = {0: pair}
    for d in (2, 1, 3):
        pairs[d] = lax.ppermute(pair, axis, [(i, (i + d) % 4) for i in range(4)])
    return [pairs[d] for d in range(4)]


def spread_chunks(value):
    chunks = {(0, 0): value}
    for dy, dz in ((2, 1), (2, 0), (1, 1), (3, 1), (1, 0), (3, 0), (0, 1)):
        chunks[dy, dz] = move(value, lambda y, zl, x, zh: ((y + dy) % 4, zl ^ dz, x, zh))
    return [chunks[dy, dz] for dy in range(4) for dz in range(2)]


def per_device(resident, memory, previous, inverse_part, pair_coupling):
    rows, cols = memory.shape[1], resident.shape[1]
    place = jnp.stack([lax.axis_index(name) for name in ("x", "zh", "c", "y", "zl")]).astype(jnp.int32)
    coupling = jnp.tile(pair_coupling, (1, 128 // ORB))

    resident, memory, previous = in_hbm(resident), in_hbm(memory), in_hbm(previous)
    odd, lhs, even_resident = first_product(place, memory, resident)
    odd_parts = scatter(odd, 1)
    lhs, odd = lax.optimization_barrier((lhs, odd))
    even = half_product(place, lhs, even_resident)
    even_parts = scatter(even, 0)
    place, _, odd_parts = lax.optimization_barrier((place, even[0], odd_parts))
    memory, prior_one, prior_two, odd_resident, even_resident = bring(place, memory, previous, resident)
    parts = odd_parts + even_parts
    front_one, energy = solve(
        first_solve_kernel, 0, place, parts, prior_one, inverse_part, [coupling], 2, "first_solve"
    )
    own = spread_pairs(jnp.stack([move(energy, turn(0)), move(energy, turn(1))]), "x")
    other = [lax.ppermute(pair, "c", SWAP) for pair in own]
    ones = spread_pairs(jnp.stack([front_one, lax.ppermute(front_one, "zl", SWAP)]), "y")
    own, other, ones = lax.optimization_barrier((own, other, ones))
    lhs = next_memory(place, memory, own + other)
    odd = half_product(place, lhs, odd_resident)
    lhs, odd = lax.optimization_barrier((lhs, odd))
    even = half_product(place, lhs, even_resident)
    parts = scatter(odd, 1) + scatter(even, 0)
    (front_two,) = solve(
        second_solve_kernel, 1, place, parts, prior_two, inverse_part, [], 1, "second_solve"
    )
    chunks = spread_chunks(front_two)
    return join_two(place, chunks, join_one(place, ones, rows, cols))


def solution(mesh):
    fine = Mesh(mesh.devices.reshape(4, 2, 4, 2, 2), ALL)
    in_specs = (P(PASTS, SECONDS), P(None, None, PASTS), P(None, None, SECONDS), P(), P())
    out_specs = P(None, None, SECONDS)
    return jax.shard_map(
        per_device, mesh=fine, in_specs=in_specs, out_specs=out_specs, check_vma=False
    )
```

```python
import functools

import jax
import jax.numpy as jnp
from jax import lax
from jax.experimental import pallas as pl
from jax.experimental.pallas import tpu as pltpu
from jax.sharding import Mesh, PartitionSpec as P

step_size = 0.5
ORB = 32
f32 = jnp.float32
bf16 = jnp.bfloat16
PASTS = ("y", "zl")
SECONDS = ("x", "zh", "c")
ALL = PASTS + SECONDS
SWAP = [(0, 1), (1, 0)]
X, ZH, C, Y, ZL = range(5)


VMEM = pl.BlockSpec(memory_space=pltpu.VMEM)
SMEM = pl.BlockSpec(memory_space=pltpu.SMEM)


def in_hbm(array):
    return pltpu.with_memory_space_constraint(array, pltpu.HBM)


def params(megabytes):
    return pltpu.CompilerParams(vmem_limit_bytes=megabytes << 20)


def cost(flops, nbytes):
    return pl.CostEstimate(flops=flops, bytes_accessed=nbytes, transcendentals=0)


def position(y):
    return (y & 1) * 2 + (y >> 1)


def store_shares(place_ref, turned_ref, out_refs):
    width = out_refs[0].shape[0]
    for k, out_ref in enumerate(out_refs):
        share = ((place_ref[Y] >> 1) ^ (k >> 1)) * 2 + (place_ref[ZL] ^ (k & 1))
        out_ref[...] = turned_ref[pl.ds(pl.multiple_of(share * width, width), width), :]


def half_product_kernel(place_ref, lhs_ref, resident_ref, *refs):
    out_refs, turned_ref = refs[:4], refs[4]
    product = jnp.dot(lhs_ref[...], resident_ref[...], preferred_element_type=f32)
    turned_ref[...] = product.T.astype(bf16)
    store_shares(place_ref, turned_ref, out_refs)


def half_product(place, lhs, resident):
    rows, depth = lhs.shape
    cols = resident.shape[1]
    width = cols // 4
    return pl.pallas_call(
        half_product_kernel,
        in_specs=[SMEM, VMEM, VMEM],
        out_specs=[VMEM] * 4,
        out_shape=[jax.ShapeDtypeStruct((width, rows), bf16)] * 4,
        scratch_shapes=[pltpu.VMEM((cols, rows), bf16)],
        compiler_params=params(6),
        cost_estimate=cost(2 * rows * depth * cols, 4 * width * rows),
        name="half_product",
    )(place, lhs, resident)


TILES = 3


def first_product_kernel(place_ref, memory_ref, resident_ref, *refs):
    out_refs, lhs_ref, even_ref, odd_ref, turned_ref, sems = refs[:4], *refs[4:]
    depth, cols = odd_ref.shape
    tile = cols // TILES
    parity = place_ref[Y] & 1

    def tile_copy(half_ref, side, i):
        start = pl.multiple_of((parity ^ side) * cols + i * tile, tile)
        return pltpu.make_async_copy(
            resident_ref.at[:, pl.ds(start, tile)],
            half_ref.at[:, i * tile : (i + 1) * tile],
            sems.at[side * TILES + i],
        )

    memory_copy = pltpu.make_async_copy(memory_ref.at[0], lhs_ref, sems.at[2 * TILES])
    odd = [tile_copy(odd_ref, 1, i) for i in range(TILES)]
    even = [tile_copy(even_ref, 0, i) for i in range(TILES)]
    for copy in (memory_copy, *odd):
        copy.start()
    memory_copy.wait()
    for i, copy in enumerate(odd):
        copy.wait()
        even[i].start()
        at = slice(i * tile, (i + 1) * tile)
        product = jnp.dot(lhs_ref[...], odd_ref[:, at], preferred_element_type=f32)
        turned_ref[at, :] = product.T.astype(bf16)
    store_shares(place_ref, turned_ref, out_refs)
    for copy in even:
        copy.wait()


def first_product(place, memory, resident):
    _, rows, depth = memory.shape
    cols = resident.shape[1]
    width = cols // 8
    outs = [((width, rows), 4), ((rows, depth), 1), ((depth, cols // 2), 1)]
    shapes = [jax.ShapeDtypeStruct(shape, bf16) for shape, count in outs for _ in range(count)]
    *odd, lhs, even_resident = pl.pallas_call(
        first_product_kernel,
        in_specs=[SMEM] + [pl.BlockSpec(memory_space=pltpu.HBM)] * 2,
        out_specs=[VMEM] * 6,
        out_shape=shapes,
        scratch_shapes=[
            pltpu.VMEM((depth, cols // 2), bf16),
            pltpu.VMEM((cols // 2, rows), bf16),
            pltpu.SemaphoreType.DMA((2 * TILES + 1,)),
        ],
        compiler_params=params(12),
        cost_estimate=cost(rows * depth * cols, 4 * depth * cols),
        name="first_product",
    )(place, memory, resident)
    return odd, lhs, even_resident


def bring_kernel(
    place_ref, memory_ref, previous_ref, resident_ref, memory_out, one_out, two_out, odd_out, even_out, prior_ref, turned_ref, sems
):
    width, rows = one_out.shape
    start = position(place_ref[Y]) * 2 * width
    cols = pl.ds(pl.multiple_of(start, 128), 2 * width)
    copies = [
        pltpu.make_async_copy(previous_ref.at[:, :, cols], prior_ref, sems.at[0]),
        pltpu.make_async_copy(memory_ref.at[1], memory_out, sems.at[1]),
    ]
    half = odd_out.shape[1]
    for side, out_ref in ((1, odd_out), (0, even_out)):
        start = pl.multiple_of(((place_ref[Y] & 1) ^ side) * half, half)
        copies.append(
            pltpu.make_async_copy(resident_ref.at[:, pl.ds(start, half)], out_ref, sems.at[2 + side])
        )
    for copy in copies:
        copy.start()
    copies[0].wait()
    for front, out_ref in enumerate((one_out, two_out)):
        turned_ref[...] = prior_ref[front].astype(f32).T
        share = turned_ref[pl.ds(pl.multiple_of(place_ref[ZL] * width, width), width), :]
        out_ref[...] = share.astype(bf16)
    for copy in copies[1:]:
        copy.wait()


def bring(place, memory, previous, resident):
    _, rows, depth = memory.shape
    cols = resident.shape[1]
    width = previous.shape[2] // 8
    return pl.pallas_call(
        bring_kernel,
        in_specs=[SMEM] + [pl.BlockSpec(memory_space=pltpu.HBM)] * 3,
        out_specs=[VMEM] * 5,
        out_shape=[
            jax.ShapeDtypeStruct((rows, depth), bf16),
            jax.ShapeDtypeStruct((width, rows), bf16),
            jax.ShapeDtypeStruct((width, rows), bf16),
            jax.ShapeDtypeStruct((depth, cols // 2), bf16),
            jax.ShapeDtypeStruct((depth, cols // 2), bf16),
        ],
        scratch_shapes=[
            pltpu.VMEM((2, rows, 2 * width), bf16),
            pltpu.VMEM((2 * width, rows), f32),
            pltpu.SemaphoreType.DMA((4,)),
        ],
        compiler_params=params(6),
        cost_estimate=cost(0, 2 * depth * (rows + cols)),
        name="bring",
    )(place, memory, previous, resident)


def place_pair(own, other, first, at, out_ref, base_ref):
    near, far = own.astype(f32), other.astype(f32)
    low = jnp.where(first == 0, near, far)
    high = jnp.where(first == 0, far, near)
    pair = jnp.concatenate([low, high], axis=0).T
    if base_ref is not None:
        pair = pair + base_ref[:, at].astype(f32)
    out_ref[:, at] = pair.astype(bf16)


def next_memory_kernel(place_ref, memory_ref, *refs):
    pair_refs, out_ref = refs[:8], refs[8]
    half = memory_ref.shape[1] // 2
    width = half // 4
    for side in range(2):
        for dx in range(4):
            near, far = pair_refs[side * 4 + dx], pair_refs[side * 4 + (dx ^ 2)]
            share = position(((place_ref[X] - dx) & 3) ^ place_ref[Y])
            start = (place_ref[C] ^ side) * half + share * width
            at = pl.ds(pl.multiple_of(start, 128), width)
            place_pair(near[0], far[1], place_ref[ZH], at, out_ref, memory_ref)


def next_memory(place, memory, pairs):
    rows, depth = memory.shape
    return pl.pallas_call(
        next_memory_kernel,
        in_specs=[SMEM] + [VMEM] * 9,
        out_specs=VMEM,
        out_shape=jax.ShapeDtypeStruct((rows, depth), bf16),
        compiler_params=params(6),
        cost_estimate=cost(rows * depth, 6 * rows * depth),
        name="next_memory",
    )(place, memory, *pairs)


def solve_into(part_refs, prior_ref, inverse_ref):
    summed = part_refs[0][...].astype(f32)
    for part_ref in part_refs[1:]:
        summed = summed + part_ref[...].astype(f32)
    source = prior_ref[...].astype(f32) - step_size * summed
    mixed = lax.dot_general(
        source,
        inverse_ref[...],
        (((1,), (1,)), ((), ())),
        precision=lax.Precision.HIGHEST,
        preferred_element_type=f32,
    )
    return (source + mixed).astype(bf16)


def flipped(values):
    rows, cols = values.shape
    strips = []
    pad = jnp.zeros((128 - ORB, 128), f32)
    for s in range(rows // ORB):
        pieces = []
        for q in range(cols // 128):
            block = values[s * ORB : (s + 1) * ORB, q * 128 : (q + 1) * 128]
            turned = jnp.concatenate([block, pad], axis=0).T
            piece = turned[:ORB]
            for t in range(1, 128 // ORB):
                piece = piece + pltpu.roll(turned[t * ORB : (t + 1) * ORB], t * ORB, 1)
            pieces.append(piece)
        strips.append(jnp.concatenate(pieces, axis=1))
    return jnp.concatenate(strips, axis=0)


def first_solve_kernel(place_ref, *refs):
    front_ref, energy_ref = refs[11:]
    front = solve_into(refs[:8], refs[8], refs[9])
    front_ref[...] = front
    values = front.astype(f32)
    mirror = flipped(values)
    rows, cols = values.shape
    coupling = jnp.tile(refs[10][...], (rows // ORB, cols // 128))
    energy_ref[...] = (mirror * mirror * values * coupling).astype(bf16)


def second_solve_kernel(place_ref, *refs):
    refs[10][...] = solve_into(refs[:8], refs[8], refs[9])


def solve(kernel, place, parts, prior, inverse, extra, outputs, name):
    width, rows = prior.shape
    return pl.pallas_call(
        kernel,
        in_specs=[SMEM] + [VMEM] * (len(parts) + 2 + len(extra)),
        out_specs=[VMEM] * outputs,
        out_shape=[jax.ShapeDtypeStruct((width, rows), bf16)] * outputs,
        compiler_params=params(8),
        cost_estimate=cost(12 * rows * rows * width, 24 * rows * width),
        name=name,
    )(place, *parts, prior, inverse, *extra)


def join_kernel(front, moves, pairs, place_ref, *refs):
    chunk_refs, (out_ref, block_ref, sems) = refs[: 2 * len(moves)] if not pairs else refs[: len(moves)], refs[-3:]
    width = block_ref.shape[2]
    copies = []
    for i, dy in enumerate(moves):
        own, other = (chunk_refs[i][0], chunk_refs[i][1]) if pairs else (chunk_refs[2 * i][...], chunk_refs[2 * i + 1][...])
        if i >= 2:
            copies[i - 2].wait()
        place_pair(own, other, place_ref[ZL], slice(None), block_ref.at[i % 2], None)
        at = pl.ds(pl.multiple_of(position((place_ref[Y] - dy) & 3) * width, 128), width)
        copies.append(pltpu.make_async_copy(block_ref.at[i % 2], out_ref.at[front, :, at], sems.at[i % 2]))
        copies[i].start()
    for copy in copies[-2:]:
        copy.wait()


def join(front, moves, pairs, place, chunks, fronts, shape):
    _, rows, cols = shape
    hbm = pl.BlockSpec(memory_space=pltpu.HBM)
    before = [] if fronts is None else [fronts]
    return pl.pallas_call(
        functools.partial(join_kernel, front, moves, pairs),
        in_specs=[SMEM] + [VMEM] * len(chunks) + [hbm] * len(before),
        out_specs=hbm,
        out_shape=jax.ShapeDtypeStruct(shape, bf16),
        scratch_shapes=[pltpu.VMEM((2, rows, cols // 4), bf16), pltpu.SemaphoreType.DMA((2,))],
        input_output_aliases={1 + len(chunks): 0} if before else {},
        compiler_params=params(6),
        cost_estimate=cost(rows * cols, len(moves) * rows * cols),
        name="join",
    )(place, *chunks, *before)


def move(value, target):
    pairs = []
    for i in range(128):
        rest, c = divmod(i, 2)
        rest, zh = divmod(rest, 2)
        rest, x = divmod(rest, 4)
        y, zl = divmod(rest, 2)
        y, zl, x, zh = target(y, zl, x, zh)
        pairs.append((i, (((y * 2 + zl) * 4 + x) * 2 + zh) * 2 + c))
    return lax.ppermute(value, ALL, pairs)


def turn(flip):
    return lambda y, zl, x, zh: (x, zh, x ^ y ^ (2 * flip), zl ^ flip)


def scatter(shares, first):
    parts = []
    for k in (3, 2, 1, 0) if first == 0 else (1, 0, 3, 2):
        dy, dz = first + 2 * (k >> 1), k & 1
        if (dy, dz) == (0, 0):
            parts.append(shares[k])
        else:
            parts.append(move(shares[k], lambda y, zl, x, zh: (y ^ dy, zl ^ dz, x, zh)))
    return parts


def spread_pairs(pair, axis):
    pairs = {0: pair}
    for d in (2, 1, 3):
        pairs[d] = lax.ppermute(pair, axis, [(i, (i + d) % 4) for i in range(4)])
    return [pairs[d] for d in range(4)]


def spread_chunks(value):
    chunks = {(0, 0): value}
    for dy, dz in ((2, 1), (2, 0), (0, 1), (1, 1), (3, 1), (1, 0), (3, 0)):
        chunks[dy, dz] = move(value, lambda y, zl, x, zh: ((y + dy) % 4, zl ^ dz, x, zh))
    return chunks


def per_device(resident, memory, previous, inverse_part, pair_coupling):
    place = jnp.stack([lax.axis_index(name) for name in ("x", "zh", "c", "y", "zl")]).astype(jnp.int32)
    coupling = jnp.tile(pair_coupling, (1, 128 // ORB))

    resident, memory, previous = in_hbm(resident), in_hbm(memory), in_hbm(previous)
    odd, lhs, even_resident = first_product(place, memory, resident)
    odd_parts = scatter(odd, 1)
    lhs, odd = lax.optimization_barrier((lhs, odd))
    even = half_product(place, lhs, even_resident)
    even_parts = scatter(even, 0)
    place, _, odd_parts = lax.optimization_barrier((place, even[0], odd_parts))
    memory, prior_one, prior_two, odd_resident, even_resident = bring(place, memory, previous, resident)
    parts = odd_parts + even_parts
    front_one, energy = solve(
        first_solve_kernel, place, parts, prior_one, inverse_part[0], [coupling], 2, "first_solve"
    )
    own = spread_pairs(jnp.stack([move(energy, turn(0)), move(energy, turn(1))]), "x")
    other = [lax.ppermute(pair, "c", SWAP) for pair in own]
    ones = spread_pairs(jnp.stack([front_one, lax.ppermute(front_one, "zl", SWAP)]), "y")
    own, other, ones = lax.optimization_barrier((own, other, ones))
    lhs = next_memory(place, memory, own + other)
    odd = half_product(place, lhs, odd_resident)
    lhs, odd = lax.optimization_barrier((lhs, odd))
    even = half_product(place, lhs, even_resident)
    parts = scatter(odd, 1) + scatter(even, 0)
    (front_two,) = solve(
        second_solve_kernel, place, parts, prior_two, inverse_part[1], [], 1, "second_solve"
    )
    chunks = spread_chunks(front_two)
    fronts = join(0, (0, 1, 2, 3), True, place, ones, None, previous.shape)
    for moves in ((0, 2), (1, 3)):
        some = [chunks[dy, dz] for dy in moves for dz in range(2)]
        fronts = join(1, moves, False, place, some, fronts, previous.shape)
    return fronts


def solution(mesh):
    fine = Mesh(mesh.devices.reshape(4, 2, 4, 2, 2), ALL)
    in_specs = (P(PASTS, SECONDS), P(None, None, PASTS), P(None, None, SECONDS), P(), P())
    out_specs = P(None, None, SECONDS)
    return jax.shard_map(
        per_device, mesh=fine, in_specs=in_specs, out_specs=out_specs, check_vma=False
    )
```

```python
import functools

import jax
import jax.numpy as jnp
from jax import lax
from jax.experimental import pallas as pl
from jax.experimental.pallas import tpu as pltpu
from jax.sharding import Mesh, PartitionSpec as P

step_size = 0.5
ORB = 32
f32 = jnp.float32
bf16 = jnp.bfloat16
PASTS = ("y", "zl")
SECONDS = ("x", "zh", "c")
ALL = PASTS + SECONDS
SWAP = [(0, 1), (1, 0)]
X, ZH, C, Y, ZL = range(5)


VMEM = pl.BlockSpec(memory_space=pltpu.VMEM)
SMEM = pl.BlockSpec(memory_space=pltpu.SMEM)
HBM = pl.BlockSpec(memory_space=pltpu.HBM)


def in_hbm(array):
    return pltpu.with_memory_space_constraint(array, pltpu.HBM)


def params(megabytes):
    return pltpu.CompilerParams(vmem_limit_bytes=megabytes << 20)


def cost(flops, nbytes):
    return pl.CostEstimate(flops=flops, bytes_accessed=nbytes, transcendentals=0)


def part_of(place_ref, dy, dz):
    return (place_ref[Y] ^ dy) * 2 + (place_ref[ZL] ^ dz)


def rows_at(part, width):
    return pl.ds(pl.multiple_of(part * width, width), width)


def store_shares(place_ref, turned_ref, out_refs):
    width = out_refs[0].shape[0]
    for k, out_ref in enumerate(out_refs):
        out_ref[...] = turned_ref[rows_at(part_of(place_ref, k >> 1, k & 1), width), :]


TILES = 3


def first_product_kernel(place_ref, memory_ref, resident_ref, *refs):
    out_refs, lhs_ref, next_ref, tile_ref, turned_ref, sems = refs[:8], *refs[8:]
    cols = next_ref.shape[1]
    tile = cols // TILES

    def tile_copy(half, half_ref, i):
        at = slice(half * cols + i * tile, half * cols + (i + 1) * tile)
        return pltpu.make_async_copy(
            resident_ref.at[:, at], half_ref.at[:, i * tile : (i + 1) * tile], sems.at[half * TILES + i]
        )

    memory_copy = pltpu.make_async_copy(memory_ref.at[0], lhs_ref, sems.at[2 * TILES])
    first = [tile_copy(0, tile_ref, i) for i in range(TILES)]
    second = [tile_copy(1, next_ref, i) for i in range(TILES)]
    for copy in (memory_copy, *first):
        copy.start()
    memory_copy.wait()
    for i, copy in enumerate(first):
        copy.wait()
        second[i].start()
        at = slice(i * tile, (i + 1) * tile)
        product = jnp.dot(lhs_ref[...], tile_ref[:, at], preferred_element_type=f32)
        turned_ref[at, :] = product.T.astype(bf16)
    store_shares(place_ref, turned_ref, out_refs)
    for copy in second:
        copy.wait()


def first_product(place, memory, resident):
    _, rows, depth = memory.shape
    half = resident.shape[1] // 2
    outs = [(half // 8, rows)] * 8 + [(rows, depth), (depth, half)]
    *shares, lhs, resident_half = pl.pallas_call(
        first_product_kernel,
        in_specs=[SMEM] + [HBM] * 2,
        out_specs=[VMEM] * 10,
        out_shape=[jax.ShapeDtypeStruct(shape, bf16) for shape in outs],
        scratch_shapes=[
            pltpu.VMEM((depth, half), bf16),
            pltpu.VMEM((half, rows), bf16),
            pltpu.SemaphoreType.DMA((2 * TILES + 1,)),
        ],
        compiler_params=params(12),
        cost_estimate=cost(rows * depth * half * 2, 4 * depth * half),
        name="first_product",
    )(place, memory, resident)
    return shares, lhs, resident_half


def half_product_kernel(place_ref, lhs_ref, resident_ref, *refs):
    out_refs, turned_ref = refs[:8], refs[8]
    product = jnp.dot(lhs_ref[...], resident_ref[...], preferred_element_type=f32)
    turned_ref[...] = product.T.astype(bf16)
    store_shares(place_ref, turned_ref, out_refs)


def half_product(place, lhs, resident):
    rows, depth = lhs.shape
    cols = resident.shape[1]
    return pl.pallas_call(
        half_product_kernel,
        in_specs=[SMEM, VMEM, VMEM],
        out_specs=[VMEM] * 8,
        out_shape=[jax.ShapeDtypeStruct((cols // 8, rows), bf16)] * 8,
        scratch_shapes=[pltpu.VMEM((cols, rows), bf16)],
        compiler_params=params(6),
        cost_estimate=cost(2 * rows * depth * cols, 4 * cols * rows),
        name="half_product",
    )(place, lhs, resident)


def depth_rows(resident_ref, half, core):
    depth = resident_ref.shape[0]
    start = core * (depth // 2) + half * (depth // 4)
    return slice(start, start + depth // 4)


def early_product_kernel(lhs_ref, resident_ref, out_ref):
    quarter = lhs_ref.shape[1] // 2
    for n in range(2):
        at = slice(n * out_ref.shape[1] // 2, (n + 1) * out_ref.shape[1] // 2)
        out_ref[:, at] = sum(
            jnp.dot(
                lhs_ref[:, core * quarter : (core + 1) * quarter],
                resident_ref[depth_rows(resident_ref, 0, core), at],
                preferred_element_type=f32,
            )
            for core in range(2)
        )


def early_product(lhs, resident):
    rows, depth = lhs.shape
    cols = resident.shape[1]
    return pl.pallas_call(
        early_product_kernel,
        in_specs=[VMEM] * 2,
        out_specs=VMEM,
        out_shape=jax.ShapeDtypeStruct((rows, cols), f32),
        compiler_params=params(6),
        cost_estimate=cost(2 * rows * depth * cols, 4 * cols * rows),
        name="early_product",
    )(lhs, resident)


def late_product_kernel(n, place_ref, early_ref, lhs_ref, resident_ref, *refs):
    out_refs, turned_ref = refs[:8], refs[8]
    quarter, half = lhs_ref.shape[1] // 2, resident_ref.shape[1] // 2
    at = slice(n * half, (n + 1) * half)
    product = early_ref[:, at]
    for core in range(2):
        product = product + jnp.dot(
            lhs_ref[:, core * quarter : (core + 1) * quarter],
            resident_ref[depth_rows(resident_ref, 1, core), at],
            preferred_element_type=f32,
        )
    turned_ref[...] = product.T.astype(bf16)
    store_shares(place_ref, turned_ref, out_refs)


def late_product(n, place, early, lhs, resident):
    rows, depth = lhs.shape
    half = resident.shape[1] // 2
    return pl.pallas_call(
        functools.partial(late_product_kernel, n),
        in_specs=[SMEM] + [VMEM] * 3,
        out_specs=[VMEM] * 8,
        out_shape=[jax.ShapeDtypeStruct((half // 8, rows), bf16)] * 8,
        scratch_shapes=[pltpu.VMEM((half, rows), bf16)],
        compiler_params=params(6),
        cost_estimate=cost(2 * rows * depth * half, 4 * half * rows),
        name="late_product",
    )(place, early, lhs, resident)


def priors_kernel(place_ref, previous_ref, *refs):
    out_refs, block_ref, turned_ref, sems = refs[:4], *refs[4:]
    width = out_refs[0].shape[0]
    half = previous_ref.shape[2] // 2
    copies = []
    for k in range(4):
        start = (k & 1) * half + (place_ref[Y] >> 1) * 4 * width
        at = pl.ds(pl.multiple_of(start, 128), 4 * width)
        copies.append(pltpu.make_async_copy(previous_ref.at[k >> 1, :, at], block_ref.at[k], sems.at[k]))
        copies[k].start()
    for k, out_ref in enumerate(out_refs):
        copies[k].wait()
        turned_ref[...] = block_ref[k].astype(f32).T
        part = (place_ref[Y] & 1) * 2 + place_ref[ZL]
        out_ref[...] = turned_ref[rows_at(part, width), :].astype(bf16)


def priors(place, previous):
    _, rows, cols = previous.shape
    width = cols // 16
    return pl.pallas_call(
        priors_kernel,
        in_specs=[SMEM, HBM],
        out_specs=[VMEM] * 4,
        out_shape=[jax.ShapeDtypeStruct((width, rows), bf16)] * 4,
        scratch_shapes=[
            pltpu.VMEM((4, rows, 4 * width), bf16),
            pltpu.VMEM((4 * width, rows), f32),
            pltpu.SemaphoreType.DMA((4,)),
        ],
        compiler_params=params(6),
        cost_estimate=cost(0, 32 * width * rows),
        name="priors",
    )(place, previous)


def bring_kernel(after_ref, memory_ref, resident_ref, memory_out, resident_out, sems):
    copies = [
        pltpu.make_async_copy(memory_ref.at[1], memory_out, sems.at[0]),
        pltpu.make_async_copy(resident_ref, resident_out, sems.at[1]),
    ]
    for copy in copies:
        copy.start()
    for copy in copies:
        copy.wait()


def bring(after, memory, resident):
    _, rows, depth = memory.shape
    return pl.pallas_call(
        bring_kernel,
        in_specs=[SMEM] + [HBM] * 2,
        out_specs=[VMEM] * 2,
        out_shape=[
            jax.ShapeDtypeStruct((rows, depth), bf16),
            jax.ShapeDtypeStruct(resident.shape, bf16),
        ],
        scratch_shapes=[pltpu.SemaphoreType.DMA((2,))],
        compiler_params=params(6),
        cost_estimate=cost(0, 2 * (rows * depth + resident.size)),
        name="bring",
    )(after, memory, resident)


def next_memory_kernel(half, place_ref, memory_ref, *refs):
    pair_refs, out_ref, energy_ref = refs[:8], refs[8], refs[9]
    depth = memory_ref.shape[1]
    width = pair_refs[0].shape[1]
    shift = place_ref[X] ^ place_ref[Y]
    for side in range(2):
        core = place_ref[C] ^ side
        for d in range(4):
            pair = pair_refs[side * 4 + d]
            near = core * 8 + (shift ^ d) * 2 + place_ref[ZH]
            far = core * 8 + (shift ^ d ^ 2) * 2 + (place_ref[ZH] ^ 1)
            energy_ref[rows_at(near, width), :] = pair[0]
            energy_ref[rows_at(far, width), :] = pair[1]
    block = depth // 8
    for i in range(4):
        at = slice(i * block, (i + 1) * block)
        start = (i // 2) * (depth // 2) + half * (depth // 4) + (i % 2) * block
        old = memory_ref[:, start : start + block].astype(f32)
        out_ref[:, at] = (old + energy_ref[at, :].astype(f32).T).astype(bf16)


def next_memory(half, place, memory, pairs):
    rows, depth = memory.shape
    return pl.pallas_call(
        functools.partial(next_memory_kernel, half),
        in_specs=[SMEM] + [VMEM] * 9,
        out_specs=VMEM,
        out_shape=jax.ShapeDtypeStruct((rows, depth // 2), bf16),
        scratch_shapes=[pltpu.VMEM((depth // 2, rows), bf16)],
        compiler_params=params(6),
        cost_estimate=cost(rows * depth, 3 * rows * depth),
        name="next_memory",
    )(place, memory, *pairs)


def solve_into(part_refs, prior_ref, inverse_ref):
    summed = part_refs[0][...].astype(f32)
    for part_ref in part_refs[1:]:
        summed = summed + part_ref[...].astype(f32)
    source = prior_ref[...].astype(f32) - step_size * summed
    mixed = lax.dot_general(
        source,
        inverse_ref[...],
        (((1,), (1,)), ((), ())),
        precision=lax.Precision.HIGHEST,
        preferred_element_type=f32,
    )
    return (source + mixed).astype(bf16)


def flipped(values):
    rows, cols = values.shape
    strips = []
    pad = jnp.zeros((128 - ORB, 128), f32)
    for s in range(rows // ORB):
        pieces = []
        for q in range(cols // 128):
            block = values[s * ORB : (s + 1) * ORB, q * 128 : (q + 1) * 128]
            turned = jnp.concatenate([block, pad], axis=0).T
            piece = turned[:ORB]
            for t in range(1, 128 // ORB):
                piece = piece + pltpu.roll(turned[t * ORB : (t + 1) * ORB], t * ORB, 1)
            pieces.append(piece)
        strips.append(jnp.concatenate(pieces, axis=1))
    return jnp.concatenate(strips, axis=0)


def first_solve_kernel(*refs):
    front_ref, energy_ref = refs[11:]
    front = solve_into(refs[:8], refs[8], refs[9])
    front_ref[...] = front
    values = front.astype(f32)
    mirror = flipped(values)
    rows, cols = values.shape
    coupling = jnp.tile(refs[10][...], (rows // ORB, cols // 128))
    energy_ref[...] = (mirror * mirror * values * coupling).astype(bf16)


def second_solve_kernel(*refs):
    refs[10][...] = solve_into(refs[:8], refs[8], refs[9])


def solve(kernel, parts, prior, inverse, extra, outputs, name):
    width, rows = prior.shape
    return pl.pallas_call(
        kernel,
        in_specs=[VMEM] * (len(parts) + 2 + len(extra)),
        out_specs=[VMEM] * outputs,
        out_shape=[jax.ShapeDtypeStruct((width, rows), bf16)] * outputs,
        compiler_params=params(8),
        cost_estimate=cost(12 * rows * rows * width, 24 * rows * width),
        name=name,
    )(*parts, prior, inverse, *extra)


def put_blocks(turned_ref, block_ref, sems, out_ref, front, start):
    width = block_ref.shape[2]
    copies = []
    for i in range(turned_ref.shape[0] // width):
        at = slice(i * width, (i + 1) * width)
        block_ref[i] = turned_ref[at, :].astype(f32).T.astype(bf16)
        to = slice(start + i * width, start + (i + 1) * width)
        copies.append(pltpu.make_async_copy(block_ref.at[i], out_ref.at[front, :, to], sems.at[i]))
        copies[i].start()
    for copy in copies:
        copy.wait()


def join_one_kernel(front_ref, out_ref, turned_ref, block_ref, sems):
    cols = front_ref.shape[0]
    width = cols // 16
    for part in range(8):
        for half in range(2):
            to, at = (half * 8 + part) * width, (part * 2 + half) * width
            turned_ref[to : to + width, :] = front_ref[at : at + width, :]
    put_blocks(turned_ref, block_ref, sems, out_ref, 0, 0)


def join_one(front):
    cols, rows = front.shape
    return pl.pallas_call(
        join_one_kernel,
        in_specs=[VMEM],
        out_specs=HBM,
        out_shape=jax.ShapeDtypeStruct((2, rows, cols), bf16),
        scratch_shapes=[
            pltpu.VMEM((cols, rows), bf16),
            pltpu.VMEM((4, rows, cols // 4), bf16),
            pltpu.SemaphoreType.DMA((4,)),
        ],
        compiler_params=params(6),
        cost_estimate=cost(rows * cols, 4 * rows * cols),
        name="join_one",
    )(front)


def join_half_kernel(half, place_ref, *refs):
    chunk_refs, (out_ref, turned_ref, block_ref, sems) = refs[:8], refs[9:]
    width = chunk_refs[0].shape[0]
    for k, chunk_ref in enumerate(chunk_refs):
        turned_ref[rows_at(part_of(place_ref, k >> 1, k & 1), width), :] = chunk_ref[...]
    put_blocks(turned_ref, block_ref, sems, out_ref, 1, half * 8 * width)


def join_half(half, place, chunks, fronts):
    _, rows, cols = fronts.shape
    return pl.pallas_call(
        functools.partial(join_half_kernel, half),
        in_specs=[SMEM] + [VMEM] * 8 + [HBM],
        out_specs=HBM,
        out_shape=jax.ShapeDtypeStruct(fronts.shape, bf16),
        scratch_shapes=[
            pltpu.VMEM((cols // 2, rows), bf16),
            pltpu.VMEM((2, rows, cols // 4), bf16),
            pltpu.SemaphoreType.DMA((2,)),
        ],
        input_output_aliases={9: 0},
        compiler_params=params(6),
        cost_estimate=cost(rows * cols, 2 * rows * cols),
        name="join_half",
    )(place, *chunks, fronts)


def move(value, target):
    pairs = []
    for i in range(128):
        rest, c = divmod(i, 2)
        rest, zh = divmod(rest, 2)
        rest, x = divmod(rest, 4)
        y, zl = divmod(rest, 2)
        y, zl, x, zh = target(y, zl, x, zh)
        pairs.append((i, (((y * 2 + zl) * 4 + x) * 2 + zh) * 2 + c))
    return lax.ppermute(value, ALL, pairs)


ROUNDS = ((2, 1), (2, 0), (1, 1), (3, 1), (1, 0), (3, 0), (0, 1))


def exchange(shares):
    parts = [None] * 8
    for dy, dz in ROUNDS:
        k = dy * 2 + dz
        value = shares[k] if isinstance(shares, (list, tuple)) else shares
        parts[k] = move(value, lambda y, zl, x, zh: (y ^ dy, zl ^ dz, x, zh))
    parts[0] = shares[0] if isinstance(shares, (list, tuple)) else shares
    return parts


def after(value, others):
    return lax.optimization_barrier((value, others))


def turned(energy):
    near = move(energy, lambda y, zl, x, zh: (x, zh, x ^ y, zl))
    far = move(energy, lambda y, zl, x, zh: (x, zh, x ^ y ^ 2, zl ^ 1))
    return [near, far]


def spread(pair):
    own = [pair, None, None, None]
    for d in (2, 1, 3):
        own[d] = lax.ppermute(pair, "x", [(i, i ^ d) for i in range(4)])
    return own


def swapped(own):
    return [lax.ppermute(one, "c", SWAP) for one in own]


def per_device(resident, memory, previous, inverse_part, pair_coupling):
    place = jnp.stack([lax.axis_index(name) for name in ("x", "zh", "c", "y", "zl")]).astype(jnp.int32)
    coupling = jnp.tile(pair_coupling, (1, 128 // ORB))
    resident, memory, previous = in_hbm(resident), in_hbm(memory), in_hbm(previous)

    shares_a, lhs, resident_half = first_product(place, memory, resident)
    parts_a = exchange(shares_a)
    lhs, parts_a[4:6] = after(lhs, parts_a[4:6])
    shares_b = half_product(place, lhs, resident_half)
    parts_b = exchange(shares_b)
    later, parts_a = after(place, parts_a)
    prior_one_a, prior_one_b, prior_two_a, prior_two_b = priors(later, previous)
    front_a, energy_a = solve(
        first_solve_kernel, parts_a, prior_one_a, inverse_part[0], [coupling], 2, "first_solve"
    )
    turned_a = turned(energy_a)
    parts_b, turned_a = after(parts_b, turned_a)
    front_b, energy_b = solve(
        first_solve_kernel, parts_b, prior_one_b, inverse_part[0], [coupling], 2, "first_solve"
    )
    whole_one = lax.all_gather(jnp.concatenate([front_a, front_b]), PASTS, axis=0, tiled=True)
    turned_b = turned(energy_b)
    own_a = spread(jnp.stack(turned_a))
    later, _ = after(place, energy_b)
    memory, resident = bring(later, memory, resident)
    turned_b, (own_a, memory) = after(turned_b, (own_a, memory))
    own_b = spread(jnp.stack(turned_b))
    early = early_product(next_memory(0, place, memory, own_a + swapped(own_a)), resident)
    own_b, early = after(own_b, early)
    lhs = next_memory(1, place, memory, own_b + swapped(own_b))
    parts_a = exchange(late_product(0, place, early, lhs, resident))
    lhs, parts_a[4:6] = after(lhs, parts_a[4:6])
    parts_b = exchange(late_product(1, place, early, lhs, resident))
    (front_a,) = solve(
        second_solve_kernel, parts_a, prior_two_a, inverse_part[1], [], 1, "second_solve"
    )
    chunks_a = exchange(front_a)
    parts_b, chunks_a[4:6] = after(parts_b, chunks_a[4:6])
    (front_b,) = solve(
        second_solve_kernel, parts_b, prior_two_b, inverse_part[1], [], 1, "second_solve"
    )
    chunks_b = exchange(front_b)
    fronts = join_half(0, place, chunks_a, join_one(whole_one))
    chunks_b[4:6], fronts = after(chunks_b[4:6], fronts)
    return join_half(1, place, chunks_b, fronts)


def solution(mesh):
    fine = Mesh(mesh.devices.reshape(4, 2, 4, 2, 2), ALL)
    in_specs = (P(PASTS, SECONDS), P(None, None, PASTS), P(None, None, SECONDS), P(), P())
    out_specs = P(None, None, SECONDS)
    return jax.shard_map(
        per_device, mesh=fine, in_specs=in_specs, out_specs=out_specs, check_vma=False
    )
```

```python
import functools

import jax
import jax.numpy as jnp
from jax import lax
from jax.experimental import pallas as pl
from jax.experimental.pallas import tpu as pltpu
from jax.sharding import Mesh, PartitionSpec as P

step_size = 0.5
ORB = 32
f32 = jnp.float32
bf16 = jnp.bfloat16
PASTS = ("y", "zl")
SECONDS = ("x", "zh", "c")
ALL = PASTS + SECONDS
SWAP = [(0, 1), (1, 0)]
X, ZH, C, Y, ZL = range(5)


VMEM = pl.BlockSpec(memory_space=pltpu.VMEM)
SMEM = pl.BlockSpec(memory_space=pltpu.SMEM)
HBM = pl.BlockSpec(memory_space=pltpu.HBM)


def in_hbm(array):
    return pltpu.with_memory_space_constraint(array, pltpu.HBM)


def params(megabytes):
    return pltpu.CompilerParams(vmem_limit_bytes=megabytes << 20)


def cost(flops, nbytes):
    return pl.CostEstimate(flops=flops, bytes_accessed=nbytes, transcendentals=0)


def position(y):
    return (y & 1) * 2 + (y >> 1)


def block_at(place_ref, dy, width):
    start = position(place_ref[Y] ^ dy) * width
    return pl.ds(pl.multiple_of(start, 128), width)


def store_shares(place_ref, turned_ref, out_refs):
    width = out_refs[0].shape[0]
    for k, out_ref in enumerate(out_refs):
        share = (k >> 1) * 2 + (place_ref[ZL] ^ (k & 1))
        out_ref[...] = turned_ref[pl.ds(pl.multiple_of(share * width, width), width), :]


STEPS = 3


def first_piece_kernel(moves, bring_lhs, place_ref, memory_ref, resident_ref, *refs):
    count = 2 * len(moves)
    if bring_lhs:
        out_refs, (lhs_ref, block_ref, turned_ref, sems) = refs[:count], refs[count:]
    else:
        lhs_ref, out_refs, (block_ref, turned_ref, sems) = memory_ref, refs[:count], refs[count:]
    depth = lhs_ref.shape[1]
    width = block_ref.shape[1] // len(moves)
    step = depth // STEPS
    copies = []
    for k in range(STEPS):
        at = slice(k * step, (k + 1) * step)
        some = [
            pltpu.make_async_copy(
                resident_ref.at[at, block_at(place_ref, dy, width)],
                block_ref.at[at, i * width : (i + 1) * width],
                sems.at[i, k],
            )
            for i, dy in enumerate(moves)
        ]
        if bring_lhs:
            some.append(pltpu.make_async_copy(memory_ref.at[0, :, at], lhs_ref.at[:, at], sems.at[len(moves), k]))
        for copy in some:
            copy.start()
        copies.append(some)
    product = None
    for k in range(STEPS):
        at = slice(k * step, (k + 1) * step)
        for copy in copies[k]:
            copy.wait()
        term = jnp.dot(lhs_ref[:, at], block_ref[at, :], preferred_element_type=f32)
        product = term if product is None else product + term
    turned_ref[...] = product.T.astype(bf16)
    store_shares(place_ref, turned_ref, out_refs)


def first_piece(moves, place, memory, resident):
    rows, depth = memory.shape[-2:]
    cols = resident.shape[1]
    width = cols // 8
    bring_lhs = memory.ndim == 3
    shapes = [(width, rows)] * 2 * len(moves) + [(rows, depth)] * bring_lhs
    return pl.pallas_call(
        functools.partial(first_piece_kernel, moves, bring_lhs),
        in_specs=[SMEM, HBM if bring_lhs else VMEM, HBM],
        out_specs=[VMEM] * len(shapes),
        out_shape=[jax.ShapeDtypeStruct(shape, bf16) for shape in shapes],
        scratch_shapes=[
            pltpu.VMEM((depth, 2 * width * len(moves)), bf16),
            pltpu.VMEM((2 * width * len(moves), rows), bf16),
            pltpu.SemaphoreType.DMA((len(moves) + bring_lhs, STEPS)),
        ],
        compiler_params=params(12),
        cost_estimate=cost(4 * rows * depth * width * len(moves), 4 * depth * width * len(moves)),
        name="first_piece",
    )(place, memory, resident)


def second_piece_kernel(moves, place_ref, lhs_ref, resident_ref, *refs):
    out_refs, turned_ref = refs[: 2 * len(moves)], refs[2 * len(moves)]
    width = turned_ref.shape[0] // len(moves)
    for i, dy in enumerate(moves):
        block = resident_ref[:, block_at(place_ref, dy, width)]
        product = jnp.dot(lhs_ref[...], block, preferred_element_type=f32)
        turned_ref[i * width : (i + 1) * width, :] = product.T.astype(bf16)
    store_shares(place_ref, turned_ref, out_refs)


def second_piece(moves, place, lhs, resident):
    rows, depth = lhs.shape
    width = resident.shape[1] // 8
    return pl.pallas_call(
        functools.partial(second_piece_kernel, moves),
        in_specs=[SMEM, VMEM, VMEM],
        out_specs=[VMEM] * 2 * len(moves),
        out_shape=[jax.ShapeDtypeStruct((width, rows), bf16)] * 2 * len(moves),
        scratch_shapes=[pltpu.VMEM((2 * width * len(moves), rows), bf16)],
        compiler_params=params(6),
        cost_estimate=cost(4 * rows * depth * width * len(moves), 4 * width * rows * len(moves)),
        name="second_piece",
    )(place, lhs, resident)


def priors_kernel(place_ref, previous_ref, one_out, two_out, prior_ref, turned_ref, sem):
    width, rows = one_out.shape
    cols = block_at(place_ref, 0, 2 * width)
    copy = pltpu.make_async_copy(previous_ref.at[:, :, cols], prior_ref, sem)
    copy.start()
    copy.wait()
    for front, out_ref in enumerate((one_out, two_out)):
        turned_ref[...] = prior_ref[front].astype(f32).T
        share = turned_ref[pl.ds(pl.multiple_of(place_ref[ZL] * width, width), width), :]
        out_ref[...] = share.astype(bf16)


def priors(place, previous):
    _, rows, cols = previous.shape
    width = cols // 8
    return pl.pallas_call(
        priors_kernel,
        in_specs=[SMEM, HBM],
        out_specs=[VMEM] * 2,
        out_shape=[jax.ShapeDtypeStruct((width, rows), bf16)] * 2,
        scratch_shapes=[
            pltpu.VMEM((2, rows, 2 * width), bf16),
            pltpu.VMEM((2 * width, rows), f32),
            pltpu.SemaphoreType.DMA,
        ],
        compiler_params=params(6),
        cost_estimate=cost(0, 32 * width * rows),
        name="priors",
    )(place, previous)


def bring_kernel(place_ref, memory_ref, resident_ref, memory_out, resident_out, sems):
    copies = [
        pltpu.make_async_copy(memory_ref.at[1], memory_out, sems.at[0]),
        pltpu.make_async_copy(resident_ref, resident_out, sems.at[1]),
    ]
    for copy in copies:
        copy.start()
    for copy in copies:
        copy.wait()


def bring(place, memory, resident):
    _, rows, depth = memory.shape
    return pl.pallas_call(
        bring_kernel,
        in_specs=[SMEM] + [HBM] * 2,
        out_specs=[VMEM] * 2,
        out_shape=[
            jax.ShapeDtypeStruct((rows, depth), bf16),
            jax.ShapeDtypeStruct(resident.shape, bf16),
        ],
        scratch_shapes=[pltpu.SemaphoreType.DMA((2,))],
        compiler_params=params(6),
        cost_estimate=cost(0, 2 * (rows * depth + resident.size)),
        name="bring",
    )(place, memory, resident)


def place_pair(own, other, first, at, out_ref, base_ref):
    near, far = own.astype(f32), other.astype(f32)
    low = jnp.where(first == 0, near, far)
    high = jnp.where(first == 0, far, near)
    pair = jnp.concatenate([low, high], axis=0).T
    if base_ref is not None:
        pair = pair + base_ref[:, at].astype(f32)
    out_ref[:, at] = pair.astype(bf16)


def next_memory_kernel(place_ref, memory_ref, *refs):
    pair_refs, out_ref = refs[:8], refs[8]
    half = memory_ref.shape[1] // 2
    width = half // 4
    for side in range(2):
        for dx in range(4):
            near, far = pair_refs[side * 4 + dx], pair_refs[side * 4 + (dx ^ 2)]
            share = position(((place_ref[X] - dx) & 3) ^ place_ref[Y])
            start = (place_ref[C] ^ side) * half + share * width
            at = pl.ds(pl.multiple_of(start, 128), width)
            place_pair(near[0], far[1], place_ref[ZH], at, out_ref, memory_ref)


def next_memory(place, memory, pairs):
    rows, depth = memory.shape
    return pl.pallas_call(
        next_memory_kernel,
        in_specs=[SMEM] + [VMEM] * 9,
        out_specs=VMEM,
        out_shape=jax.ShapeDtypeStruct((rows, depth), bf16),
        compiler_params=params(6),
        cost_estimate=cost(rows * depth, 6 * rows * depth),
        name="next_memory",
    )(place, memory, *pairs)


def solve_into(part_refs, prior_ref, inverse_ref):
    summed = part_refs[0][...].astype(f32)
    for part_ref in part_refs[1:]:
        summed = summed + part_ref[...].astype(f32)
    source = prior_ref[...].astype(f32) - step_size * summed
    mixed = lax.dot_general(
        source,
        inverse_ref[...],
        (((1,), (1,)), ((), ())),
        precision=lax.Precision.HIGHEST,
        preferred_element_type=f32,
    )
    return (source + mixed).astype(bf16)


def flipped(values):
    rows, cols = values.shape
    strips = []
    pad = jnp.zeros((128 - ORB, 128), f32)
    for s in range(rows // ORB):
        pieces = []
        for q in range(cols // 128):
            block = values[s * ORB : (s + 1) * ORB, q * 128 : (q + 1) * 128]
            turned = jnp.concatenate([block, pad], axis=0).T
            piece = turned[:ORB]
            for t in range(1, 128 // ORB):
                piece = piece + pltpu.roll(turned[t * ORB : (t + 1) * ORB], t * ORB, 1)
            pieces.append(piece)
        strips.append(jnp.concatenate(pieces, axis=1))
    return jnp.concatenate(strips, axis=0)


def first_solve_kernel(place_ref, *refs):
    front_ref, energy_ref = refs[11:]
    front = solve_into(refs[:8], refs[8], refs[9])
    front_ref[...] = front
    values = front.astype(f32)
    mirror = flipped(values)
    rows, cols = values.shape
    coupling = jnp.tile(refs[10][...], (rows // ORB, cols // 128))
    energy_ref[...] = (mirror * mirror * values * coupling).astype(bf16)


def second_solve_kernel(place_ref, *refs):
    refs[10][...] = solve_into(refs[:8], refs[8], refs[9])


def solve(kernel, place, parts, prior, inverse, extra, outputs, name):
    width, rows = prior.shape
    return pl.pallas_call(
        kernel,
        in_specs=[SMEM] + [VMEM] * (len(parts) + 2 + len(extra)),
        out_specs=[VMEM] * outputs,
        out_shape=[jax.ShapeDtypeStruct((width, rows), bf16)] * outputs,
        compiler_params=params(8),
        cost_estimate=cost(12 * rows * rows * width, 24 * rows * width),
        name=name,
    )(place, *parts, prior, inverse, *extra)


def put_blocks(blocks, block_ref, sems, out_ref, front):
    width = block_ref.shape[2]
    copies = []
    for i, (start, write) in enumerate(blocks):
        write(block_ref.at[i])
        at = pl.ds(pl.multiple_of(start, 128), width)
        copies.append(pltpu.make_async_copy(block_ref.at[i], out_ref.at[front, :, at], sems.at[i]))
        copies[i].start()
    for copy in copies:
        copy.wait()


def join_one_kernel(front_ref, out_ref, block_ref, sems):
    width = block_ref.shape[2]

    def block(y):
        def write(ref):
            ref[...] = front_ref[y * width : (y + 1) * width, :].astype(f32).T.astype(bf16)

        return position(y) * width, write

    put_blocks([block(y) for y in range(4)], block_ref, sems, out_ref, 0)


def join_two_kernel(place_ref, *refs):
    chunk_refs, (out_ref, block_ref, sems) = refs[:8], refs[9:]
    width = block_ref.shape[2]

    def block(dy):
        def write(ref):
            own, other = chunk_refs[2 * dy][...], chunk_refs[2 * dy + 1][...]
            place_pair(own, other, place_ref[ZL], slice(None), ref, None)

        return position((place_ref[Y] - dy) & 3) * width, write

    put_blocks([block(dy) for dy in (0, 2, 1, 3)], block_ref, sems, out_ref, 1)


def join(kernel, args, in_specs, shape, aliases, name):
    _, rows, cols = shape
    return pl.pallas_call(
        kernel,
        in_specs=in_specs,
        out_specs=HBM,
        out_shape=jax.ShapeDtypeStruct(shape, bf16),
        scratch_shapes=[pltpu.VMEM((4, rows, cols // 4), bf16), pltpu.SemaphoreType.DMA((4,))],
        input_output_aliases=aliases,
        compiler_params=params(6),
        cost_estimate=cost(rows * cols, 4 * rows * cols),
        name=name,
    )(*args)


def move(value, target):
    pairs = []
    for i in range(128):
        rest, c = divmod(i, 2)
        rest, zh = divmod(rest, 2)
        rest, x = divmod(rest, 4)
        y, zl = divmod(rest, 2)
        y, zl, x, zh = target(y, zl, x, zh)
        pairs.append((i, (((y * 2 + zl) * 4 + x) * 2 + zh) * 2 + c))
    return lax.ppermute(value, ALL, pairs)


def turn(flip):
    return lambda y, zl, x, zh: (x, zh, x ^ y ^ (2 * flip), zl ^ flip)


def after(value, others):
    return lax.optimization_barrier((value, others))


def scatter(shares, moves):
    parts = []
    for i, dy in enumerate(moves):
        for dz in (1, 0):
            share = shares[2 * i + dz]
            if (dy, dz) != (0, 0):
                share = move(share, lambda y, zl, x, zh: (y ^ dy, zl ^ dz, x, zh))
            parts.append(share)
    return parts


def spread_pairs(pair, axis):
    pairs = {0: pair}
    for d in (2, 1, 3):
        pairs[d] = lax.ppermute(pair, axis, [(i, (i + d) % 4) for i in range(4)])
    return [pairs[d] for d in range(4)]


def spread_chunks(value):
    chunks = {(0, 0): value}
    for dy, dz in ((2, 1), (2, 0), (0, 1), (1, 1), (3, 1), (1, 0), (3, 0)):
        chunks[dy, dz] = move(value, lambda y, zl, x, zh: ((y + dy) % 4, zl ^ dz, x, zh))
    return chunks


def per_device(resident, memory, previous, inverse_part, pair_coupling):
    place = jnp.stack([lax.axis_index(name) for name in ("x", "zh", "c", "y", "zl")]).astype(jnp.int32)
    coupling = jnp.tile(pair_coupling, (1, 128 // ORB))

    resident, memory, previous = in_hbm(resident), in_hbm(memory), in_hbm(previous)

    *shares, lhs = first_piece((1,), place, memory, resident)
    parts = scatter(shares, (1,))
    lhs, shares = after(lhs, shares)
    shares = first_piece((3,), place, lhs, resident)
    parts += scatter(shares, (3,))
    lhs, shares = after(lhs, shares)
    shares = first_piece((2, 0), place, lhs, resident)
    later, _ = after(place, (shares, parts))
    parts += scatter(shares, (2, 0))
    prior_one, prior_two = priors(later, previous)
    front_one, energy = solve(
        first_solve_kernel, place, parts, prior_one, inverse_part[0], [coupling], 2, "first_solve"
    )
    whole_one = lax.all_gather(front_one, PASTS, axis=0, tiled=True)
    pair = [move(energy, turn(0)), move(energy, turn(1))]
    later, _ = after(place, energy)
    memory, resident = bring(later, memory, resident)
    pair, memory = after(pair, memory)
    own = spread_pairs(jnp.stack(pair), "x")
    other = [lax.ppermute(pair, "c", SWAP) for pair in own]
    lhs = next_memory(place, memory, own + other)
    shares = second_piece((1,), place, lhs, resident)
    parts = scatter(shares, (1,))
    lhs, shares = after(lhs, shares)
    shares = second_piece((3,), place, lhs, resident)
    more = scatter(shares, (3,))
    lhs, parts = after(lhs, parts)
    parts += more + scatter(second_piece((2, 0), place, lhs, resident), (2, 0))
    (front_two,) = solve(
        second_solve_kernel, place, parts, prior_two, inverse_part[1], [], 1, "second_solve"
    )
    chunks = spread_chunks(front_two)
    chunks = [chunks[dy, dz] for dy in range(4) for dz in range(2)]
    fronts = join(join_one_kernel, (whole_one,), [VMEM], previous.shape, {}, "join_one")
    return join(
        join_two_kernel, (place, *chunks, fronts), [SMEM] + [VMEM] * 8 + [HBM], previous.shape, {9: 0}, "join_two"
    )


def solution(mesh):
    fine = Mesh(mesh.devices.reshape(4, 2, 4, 2, 2), ALL)
    in_specs = (P(PASTS, SECONDS), P(None, None, PASTS), P(None, None, SECONDS), P(), P())
    out_specs = P(None, None, SECONDS)
    return jax.shard_map(
        per_device, mesh=fine, in_specs=in_specs, out_specs=out_specs, check_vma=False
    )
```

```python
import functools

import jax
import jax.numpy as jnp
from jax import lax
from jax.experimental import pallas as pl
from jax.experimental.pallas import tpu as pltpu
from jax.sharding import Mesh, PartitionSpec as P

step_size = 0.5
ORB = 32
f32 = jnp.float32
bf16 = jnp.bfloat16
PASTS = ("y", "zl")
SECONDS = ("x", "zh", "c")
ALL = PASTS + SECONDS
SWAP = [(0, 1), (1, 0)]
X, ZH, C, Y, ZL = range(5)


VMEM = pl.BlockSpec(memory_space=pltpu.VMEM)
SMEM = pl.BlockSpec(memory_space=pltpu.SMEM)
HBM = pl.BlockSpec(memory_space=pltpu.HBM)


def in_hbm(array):
    return pltpu.with_memory_space_constraint(array, pltpu.HBM)


def params(megabytes):
    return pltpu.CompilerParams(vmem_limit_bytes=megabytes << 20)


def cost(flops, nbytes):
    return pl.CostEstimate(flops=flops, bytes_accessed=nbytes, transcendentals=0)


def position(y):
    return (y & 1) * 2 + (y >> 1)


def store_shares(place_ref, turned_ref, out_refs):
    width = out_refs[0].shape[0]
    for k, out_ref in enumerate(out_refs):
        share = ((place_ref[Y] >> 1) ^ (k >> 1)) * 2 + (place_ref[ZL] ^ (k & 1))
        out_ref[...] = turned_ref[pl.ds(pl.multiple_of(share * width, width), width), :]


def half_product_kernel(place_ref, lhs_ref, resident_ref, *refs):
    out_refs, turned_ref = refs[:4], refs[4]
    product = jnp.dot(lhs_ref[...], resident_ref[...], preferred_element_type=f32)
    turned_ref[...] = product.T.astype(bf16)
    store_shares(place_ref, turned_ref, out_refs)


def half_product(place, lhs, resident):
    rows, depth = lhs.shape
    cols = resident.shape[1]
    width = cols // 4
    return pl.pallas_call(
        half_product_kernel,
        in_specs=[SMEM, VMEM, VMEM],
        out_specs=[VMEM] * 4,
        out_shape=[jax.ShapeDtypeStruct((width, rows), bf16)] * 4,
        scratch_shapes=[pltpu.VMEM((cols, rows), bf16)],
        compiler_params=params(6),
        cost_estimate=cost(2 * rows * depth * cols, 4 * width * rows),
        name="half_product",
    )(place, lhs, resident)


TILES = 3


def first_product_kernel(place_ref, memory_ref, resident_ref, *refs):
    out_refs, lhs_ref, even_ref, odd_ref, turned_ref, sems = refs[:4], *refs[4:]
    depth, cols = odd_ref.shape
    tile = cols // TILES
    parity = place_ref[Y] & 1

    def tile_copy(half_ref, side, i):
        start = pl.multiple_of((parity ^ side) * cols + i * tile, tile)
        return pltpu.make_async_copy(
            resident_ref.at[:, pl.ds(start, tile)],
            half_ref.at[:, i * tile : (i + 1) * tile],
            sems.at[side * TILES + i],
        )

    memory_copy = pltpu.make_async_copy(memory_ref.at[0], lhs_ref, sems.at[2 * TILES])
    odd = [tile_copy(odd_ref, 1, i) for i in range(TILES)]
    even = [tile_copy(even_ref, 0, i) for i in range(TILES)]
    for copy in (memory_copy, *odd):
        copy.start()
    memory_copy.wait()
    for i, copy in enumerate(odd):
        copy.wait()
        even[i].start()
        at = slice(i * tile, (i + 1) * tile)
        product = jnp.dot(lhs_ref[...], odd_ref[:, at], preferred_element_type=f32)
        turned_ref[at, :] = product.T.astype(bf16)
    store_shares(place_ref, turned_ref, out_refs)
    for copy in even:
        copy.wait()


def first_product(place, memory, resident):
    _, rows, depth = memory.shape
    cols = resident.shape[1]
    width = cols // 8
    outs = [((width, rows), 4), ((rows, depth), 1), ((depth, cols // 2), 1)]
    shapes = [jax.ShapeDtypeStruct(shape, bf16) for shape, count in outs for _ in range(count)]
    *odd, lhs, even_resident = pl.pallas_call(
        first_product_kernel,
        in_specs=[SMEM] + [pl.BlockSpec(memory_space=pltpu.HBM)] * 2,
        out_specs=[VMEM] * 6,
        out_shape=shapes,
        scratch_shapes=[
            pltpu.VMEM((depth, cols // 2), bf16),
            pltpu.VMEM((cols // 2, rows), bf16),
            pltpu.SemaphoreType.DMA((2 * TILES + 1,)),
        ],
        compiler_params=params(12),
        cost_estimate=cost(rows * depth * cols, 4 * depth * cols),
        name="first_product",
    )(place, memory, resident)
    return odd, lhs, even_resident


def bring_kernel(
    place_ref, memory_ref, previous_ref, resident_ref, memory_out, one_out, two_out, odd_out, even_out, prior_ref, turned_ref, sems
):
    width, rows = one_out.shape
    start = position(place_ref[Y]) * 2 * width
    cols = pl.ds(pl.multiple_of(start, 128), 2 * width)
    copies = [
        pltpu.make_async_copy(previous_ref.at[:, :, cols], prior_ref, sems.at[0]),
        pltpu.make_async_copy(memory_ref.at[1], memory_out, sems.at[1]),
    ]
    half = odd_out.shape[1]
    for side, out_ref in ((1, odd_out), (0, even_out)):
        start = pl.multiple_of(((place_ref[Y] & 1) ^ side) * half, half)
        copies.append(
            pltpu.make_async_copy(resident_ref.at[:, pl.ds(start, half)], out_ref, sems.at[2 + side])
        )
    for copy in copies:
        copy.start()
    copies[0].wait()
    for front, out_ref in enumerate((one_out, two_out)):
        turned_ref[...] = prior_ref[front].astype(f32).T
        share = turned_ref[pl.ds(pl.multiple_of(place_ref[ZL] * width, width), width), :]
        out_ref[...] = share.astype(bf16)
    for copy in copies[1:]:
        copy.wait()


def bring(place, memory, previous, resident):
    _, rows, depth = memory.shape
    cols = resident.shape[1]
    width = previous.shape[2] // 8
    return pl.pallas_call(
        bring_kernel,
        in_specs=[SMEM] + [pl.BlockSpec(memory_space=pltpu.HBM)] * 3,
        out_specs=[VMEM] * 5,
        out_shape=[
            jax.ShapeDtypeStruct((rows, depth), bf16),
            jax.ShapeDtypeStruct((width, rows), bf16),
            jax.ShapeDtypeStruct((width, rows), bf16),
            jax.ShapeDtypeStruct((depth, cols // 2), bf16),
            jax.ShapeDtypeStruct((depth, cols // 2), bf16),
        ],
        scratch_shapes=[
            pltpu.VMEM((2, rows, 2 * width), bf16),
            pltpu.VMEM((2 * width, rows), f32),
            pltpu.SemaphoreType.DMA((4,)),
        ],
        compiler_params=params(6),
        cost_estimate=cost(0, 2 * depth * (rows + cols)),
        name="bring",
    )(place, memory, previous, resident)


def place_pair(own, other, first, at, out_ref, base_ref):
    near, far = own.astype(f32), other.astype(f32)
    low = jnp.where(first == 0, near, far)
    high = jnp.where(first == 0, far, near)
    pair = jnp.concatenate([low, high], axis=0).T
    if base_ref is not None:
        pair = pair + base_ref[:, at].astype(f32)
    out_ref[:, at] = pair.astype(bf16)


def next_memory_kernel(place_ref, memory_ref, *refs):
    pair_refs, out_ref = refs[:8], refs[8]
    half = memory_ref.shape[1] // 2
    width = half // 4
    for side in range(2):
        for dx in range(4):
            near, far = pair_refs[side * 4 + dx], pair_refs[side * 4 + (dx ^ 2)]
            share = position(((place_ref[X] - dx) & 3) ^ place_ref[Y])
            start = (place_ref[C] ^ side) * half + share * width
            at = pl.ds(pl.multiple_of(start, 128), width)
            place_pair(near[0], far[1], place_ref[ZH], at, out_ref, memory_ref)


def next_memory(place, memory, pairs):
    rows, depth = memory.shape
    return pl.pallas_call(
        next_memory_kernel,
        in_specs=[SMEM] + [VMEM] * 9,
        out_specs=VMEM,
        out_shape=jax.ShapeDtypeStruct((rows, depth), bf16),
        compiler_params=params(6),
        cost_estimate=cost(rows * depth, 6 * rows * depth),
        name="next_memory",
    )(place, memory, *pairs)


def solve_into(part_refs, prior_ref, inverse_ref):
    summed = part_refs[0][...].astype(f32)
    for part_ref in part_refs[1:]:
        summed = summed + part_ref[...].astype(f32)
    source = prior_ref[...].astype(f32) - step_size * summed
    mixed = lax.dot_general(
        source,
        inverse_ref[...],
        (((1,), (1,)), ((), ())),
        precision=lax.Precision.HIGHEST,
        preferred_element_type=f32,
    )
    return (source + mixed).astype(bf16)


def flipped(values):
    rows, cols = values.shape
    strips = []
    pad = jnp.zeros((128 - ORB, 128), f32)
    for s in range(rows // ORB):
        pieces = []
        for q in range(cols // 128):
            block = values[s * ORB : (s + 1) * ORB, q * 128 : (q + 1) * 128]
            turned = jnp.concatenate([block, pad], axis=0).T
            piece = turned[:ORB]
            for t in range(1, 128 // ORB):
                piece = piece + pltpu.roll(turned[t * ORB : (t + 1) * ORB], t * ORB, 1)
            pieces.append(piece)
        strips.append(jnp.concatenate(pieces, axis=1))
    return jnp.concatenate(strips, axis=0)


def first_solve_kernel(place_ref, *refs):
    front_ref, energy_ref = refs[11:]
    front = solve_into(refs[:8], refs[8], refs[9])
    front_ref[...] = front
    values = front.astype(f32)
    mirror = flipped(values)
    rows, cols = values.shape
    coupling = jnp.tile(refs[10][...], (rows // ORB, cols // 128))
    energy_ref[...] = (mirror * mirror * values * coupling).astype(bf16)


def second_solve_kernel(place_ref, *refs):
    refs[10][...] = solve_into(refs[:8], refs[8], refs[9])


def solve(kernel, place, parts, prior, inverse, extra, outputs, name):
    width, rows = prior.shape
    return pl.pallas_call(
        kernel,
        in_specs=[SMEM] + [VMEM] * (len(parts) + 2 + len(extra)),
        out_specs=[VMEM] * outputs,
        out_shape=[jax.ShapeDtypeStruct((width, rows), bf16)] * outputs,
        compiler_params=params(8),
        cost_estimate=cost(12 * rows * rows * width, 24 * rows * width),
        name=name,
    )(place, *parts, prior, inverse, *extra)


def put_blocks(blocks, block_ref, sems, out_ref, front):
    width = block_ref.shape[2]
    copies = []
    for i, (start, write) in enumerate(blocks):
        write(block_ref.at[i])
        at = pl.ds(pl.multiple_of(start, 128), width)
        copies.append(pltpu.make_async_copy(block_ref.at[i], out_ref.at[front, :, at], sems.at[i]))
        copies[i].start()
    for copy in copies:
        copy.wait()


def join_one_kernel(place_ref, own_ref, other_ref, out_ref, block_ref, sems):
    def block(dy):
        def write(ref):
            place_pair(own_ref[dy], other_ref[dy], place_ref[ZL], slice(None), ref, None)

        return position((place_ref[Y] - dy) & 3) * block_ref.shape[2], write

    put_blocks([block(dy) for dy in range(4)], block_ref, sems, out_ref, 0)


def join_two_kernel(place_ref, *refs):
    chunk_refs, (out_ref, block_ref, sems) = refs[:8], refs[9:]

    def block(dy):
        def write(ref):
            own, other = chunk_refs[2 * dy][...], chunk_refs[2 * dy + 1][...]
            place_pair(own, other, place_ref[ZL], slice(None), ref, None)

        return position((place_ref[Y] - dy) & 3) * block_ref.shape[2], write

    put_blocks([block(dy) for dy in (0, 2, 1, 3)], block_ref, sems, out_ref, 1)


def join(kernel, args, in_specs, shape, aliases, name):
    _, rows, cols = shape
    return pl.pallas_call(
        kernel,
        in_specs=in_specs,
        out_specs=HBM,
        out_shape=jax.ShapeDtypeStruct(shape, bf16),
        scratch_shapes=[pltpu.VMEM((4, rows, cols // 4), bf16), pltpu.SemaphoreType.DMA((4,))],
        input_output_aliases=aliases,
        compiler_params=params(6),
        cost_estimate=cost(rows * cols, 4 * rows * cols),
        name=name,
    )(*args)


def move(value, target):
    pairs = []
    for i in range(128):
        rest, c = divmod(i, 2)
        rest, zh = divmod(rest, 2)
        rest, x = divmod(rest, 4)
        y, zl = divmod(rest, 2)
        y, zl, x, zh = target(y, zl, x, zh)
        pairs.append((i, (((y * 2 + zl) * 4 + x) * 2 + zh) * 2 + c))
    return lax.ppermute(value, ALL, pairs)


def turn(flip):
    return lambda y, zl, x, zh: (x, zh, x ^ y ^ (2 * flip), zl ^ flip)


def scatter(shares, first):
    parts = []
    for k in (3, 2, 1, 0) if first == 0 else (1, 0, 3, 2):
        dy, dz = first + 2 * (k >> 1), k & 1
        if (dy, dz) == (0, 0):
            parts.append(shares[k])
        else:
            parts.append(move(shares[k], lambda y, zl, x, zh: (y ^ dy, zl ^ dz, x, zh)))
    return parts


def spread(pair, axis):
    pairs = {0: pair}
    for d in (2, 1, 3):
        pairs[d] = lax.ppermute(pair, axis, [(i, (i + d) % 4) for i in range(4)])
    return [pairs[d] for d in range(4)]


def spread_chunks(value):
    chunks = {(0, 0): value}
    for dy, dz in ((2, 1), (2, 0), (0, 1), (1, 1), (3, 1), (1, 0), (3, 0)):
        chunks[dy, dz] = move(value, lambda y, zl, x, zh: ((y + dy) % 4, zl ^ dz, x, zh))
    return chunks


def per_device(resident, memory, previous, inverse_part, pair_coupling):
    place = jnp.stack([lax.axis_index(name) for name in ("x", "zh", "c", "y", "zl")]).astype(jnp.int32)
    coupling = jnp.tile(pair_coupling, (1, 128 // ORB))

    resident, memory, previous = in_hbm(resident), in_hbm(memory), in_hbm(previous)
    odd, lhs, even_resident = first_product(place, memory, resident)
    odd_parts = scatter(odd, 1)
    lhs, odd = lax.optimization_barrier((lhs, odd))
    even = half_product(place, lhs, even_resident)
    even_parts = scatter(even, 0)
    place, _, odd_parts = lax.optimization_barrier((place, even[0], odd_parts))
    memory, prior_one, prior_two, odd_resident, even_resident = bring(place, memory, previous, resident)
    parts = odd_parts + even_parts
    front_one, energy = solve(
        first_solve_kernel, place, parts, prior_one, inverse_part[0], [coupling], 2, "first_solve"
    )
    pair = [move(energy, turn(0)), move(energy, turn(1))]
    ones = spread(front_one, "y")
    pair, ones = lax.optimization_barrier((pair, ones))
    own = spread(jnp.stack(pair), "x")
    ones = jnp.stack(ones)
    others = lax.ppermute(ones, "zl", SWAP)
    other = [lax.ppermute(pair, "c", SWAP) for pair in own]
    own, other, others = lax.optimization_barrier((own, other, others))
    lhs = next_memory(place, memory, own + other)
    odd = half_product(place, lhs, odd_resident)
    lhs, odd = lax.optimization_barrier((lhs, odd))
    even = half_product(place, lhs, even_resident)
    parts = scatter(odd, 1) + scatter(even, 0)
    (front_two,) = solve(
        second_solve_kernel, place, parts, prior_two, inverse_part[1], [], 1, "second_solve"
    )
    chunks = spread_chunks(front_two)
    chunks = [chunks[dy, dz] for dy in range(4) for dz in range(2)]
    fronts = join(join_one_kernel, (place, ones, others), [SMEM, VMEM, VMEM], previous.shape, {}, "join_one")
    return join(
        join_two_kernel, (place, *chunks, fronts), [SMEM] + [VMEM] * 8 + [HBM], previous.shape, {9: 0}, "join_two"
    )


def solution(mesh):
    fine = Mesh(mesh.devices.reshape(4, 2, 4, 2, 2), ALL)
    in_specs = (P(PASTS, SECONDS), P(None, None, PASTS), P(None, None, SECONDS), P(), P())
    out_specs = P(None, None, SECONDS)
    return jax.shard_map(
        per_device, mesh=fine, in_specs=in_specs, out_specs=out_specs, check_vma=False
    )
```

```python
import functools

import jax
import jax.numpy as jnp
from jax import lax
from jax.experimental import pallas as pl
from jax.experimental.pallas import tpu as pltpu
from jax.sharding import Mesh, PartitionSpec as P

step_size = 0.5
ORB = 32
f32 = jnp.float32
bf16 = jnp.bfloat16
PASTS = ("y", "zl")
SECONDS = ("x", "zh", "c")
ALL = PASTS + SECONDS
SWAP = [(0, 1), (1, 0)]
X, ZH, C, Y, ZL = range(5)


VMEM = pl.BlockSpec(memory_space=pltpu.VMEM)
SMEM = pl.BlockSpec(memory_space=pltpu.SMEM)
HBM = pl.BlockSpec(memory_space=pltpu.HBM)


def in_hbm(array):
    return pltpu.with_memory_space_constraint(array, pltpu.HBM)


def params(megabytes):
    return pltpu.CompilerParams(vmem_limit_bytes=megabytes << 20)


def cost(flops, nbytes):
    return pl.CostEstimate(flops=flops, bytes_accessed=nbytes, transcendentals=0)


def position(y):
    return (y & 1) * 2 + (y >> 1)


def store_shares(place_ref, turned_ref, out_refs):
    width = out_refs[0].shape[0]
    for k, out_ref in enumerate(out_refs):
        share = ((place_ref[Y] >> 1) ^ (k >> 1)) * 2 + (place_ref[ZL] ^ (k & 1))
        out_ref[...] = turned_ref[pl.ds(pl.multiple_of(share * width, width), width), :]


TILES = 3


def tiled_product(start, lhs_ref, resident_ref, tile_ref, turned_ref, sems, before):
    tile = tile_ref.shape[1] // TILES
    copies = []
    for i in range(TILES):
        at = pl.ds(pl.multiple_of(start + i * tile, tile), tile)
        to = tile_ref.at[:, i * tile : (i + 1) * tile]
        copies.append(pltpu.make_async_copy(resident_ref.at[:, at], to, sems.at[i]))
    for copy in (*before, *copies):
        copy.start()
    for copy in before:
        copy.wait()
    for i, copy in enumerate(copies):
        copy.wait()
        at = slice(i * tile, (i + 1) * tile)
        product = jnp.dot(lhs_ref[...], tile_ref[:, at], preferred_element_type=f32)
        turned_ref[at, :] = product.T.astype(bf16)


def odd_product_kernel(place_ref, memory_ref, resident_ref, *refs):
    out_refs, (lhs_ref, tile_ref, turned_ref, sems) = refs[:4], refs[4:]
    start = ((place_ref[Y] & 1) ^ 1) * tile_ref.shape[1]
    copy = pltpu.make_async_copy(memory_ref.at[0], lhs_ref, sems.at[TILES])
    tiled_product(start, lhs_ref, resident_ref, tile_ref, turned_ref, sems, [copy])
    store_shares(place_ref, turned_ref, out_refs)


def even_product_kernel(place_ref, lhs_ref, resident_ref, *refs):
    out_refs, (tile_ref, turned_ref, sems) = refs[:4], refs[4:]
    start = (place_ref[Y] & 1) * tile_ref.shape[1]
    tiled_product(start, lhs_ref, resident_ref, tile_ref, turned_ref, sems, [])
    store_shares(place_ref, turned_ref, out_refs)


def first_product(kernel, place, left, resident, lhs_shape, name):
    depth, cols = resident.shape
    rows, half = left.shape[-2], cols // 2
    shapes = [(half // 4, rows)] * 4 + lhs_shape
    return pl.pallas_call(
        kernel,
        in_specs=[SMEM, HBM if lhs_shape else VMEM, HBM],
        out_specs=[VMEM] * len(shapes),
        out_shape=[jax.ShapeDtypeStruct(shape, bf16) for shape in shapes],
        scratch_shapes=[
            pltpu.VMEM((depth, half), bf16),
            pltpu.VMEM((half, rows), bf16),
            pltpu.SemaphoreType.DMA((TILES + 1,)),
        ],
        compiler_params=params(12),
        cost_estimate=cost(2 * rows * depth * half, 2 * depth * half),
        name=name,
    )(place, left, resident)


def depth_half(place_ref, side, resident_ref):
    half = resident_ref.shape[0] // 2
    return pl.ds(pl.multiple_of((place_ref[C] ^ side) * half, half), half)


def early_product_kernel(place_ref, lhs_ref, resident_ref, out_ref):
    right = resident_ref[depth_half(place_ref, 0, resident_ref), :]
    out_ref[...] = jnp.dot(lhs_ref[...], right, preferred_element_type=f32)


def early_product(place, lhs, resident):
    rows, depth = lhs.shape
    cols = resident.shape[1]
    return pl.pallas_call(
        early_product_kernel,
        in_specs=[SMEM, VMEM, VMEM],
        out_specs=VMEM,
        out_shape=jax.ShapeDtypeStruct((rows, cols), f32),
        compiler_params=params(6),
        cost_estimate=cost(2 * rows * depth * cols, 4 * rows * cols),
        name="early_product",
    )(place, lhs, resident)


def late_product_kernel(place_ref, early_ref, lhs_ref, resident_ref, *refs):
    out_refs, turned_ref = refs[:4], refs[4]
    right = resident_ref[depth_half(place_ref, 1, resident_ref), :]
    product = early_ref[...] + jnp.dot(lhs_ref[...], right, preferred_element_type=f32)
    turned_ref[...] = product.T.astype(bf16)
    store_shares(place_ref, turned_ref, out_refs)


def both_product_kernel(place_ref, own_ref, other_ref, resident_ref, *refs):
    out_refs, turned_ref = refs[:4], refs[4]
    product = None
    for side, lhs_ref in enumerate((own_ref, other_ref)):
        right = resident_ref[depth_half(place_ref, side, resident_ref), :]
        term = jnp.dot(lhs_ref[...], right, preferred_element_type=f32)
        product = term if product is None else product + term
    turned_ref[...] = product.T.astype(bf16)
    store_shares(place_ref, turned_ref, out_refs)


def second_product(kernel, place, left, lhs, resident, name):
    rows, depth = lhs.shape
    cols = resident.shape[1]
    return pl.pallas_call(
        kernel,
        in_specs=[SMEM] + [VMEM] * 3,
        out_specs=[VMEM] * 4,
        out_shape=[jax.ShapeDtypeStruct((cols // 4, rows), bf16)] * 4,
        scratch_shapes=[pltpu.VMEM((cols, rows), bf16)],
        compiler_params=params(6),
        cost_estimate=cost(2 * rows * depth * cols, 4 * cols * rows),
        name=name,
    )(place, left, lhs, resident)


def half_copy(side, place_ref, resident_ref, out_ref, sem):
    half = out_ref.shape[1]
    at = pl.ds(pl.multiple_of(((place_ref[Y] & 1) ^ side) * half, half), half)
    return pltpu.make_async_copy(resident_ref.at[:, at], out_ref, sem)


def bring_odd_kernel(
    place_ref, memory_ref, previous_ref, resident_ref, memory_out, one_out, two_out, odd_out, prior_ref, turned_ref, sems
):
    width, rows = one_out.shape
    start = position(place_ref[Y]) * 2 * width
    cols = pl.ds(pl.multiple_of(start, 128), 2 * width)
    copies = [
        pltpu.make_async_copy(previous_ref.at[:, :, cols], prior_ref, sems.at[0]),
        pltpu.make_async_copy(memory_ref.at[1], memory_out, sems.at[1]),
        half_copy(1, place_ref, resident_ref, odd_out, sems.at[2]),
    ]
    for copy in copies:
        copy.start()
    copies[0].wait()
    for front, out_ref in enumerate((one_out, two_out)):
        turned_ref[...] = prior_ref[front].astype(f32).T
        share = turned_ref[pl.ds(pl.multiple_of(place_ref[ZL] * width, width), width), :]
        out_ref[...] = share.astype(bf16)
    for copy in copies[1:]:
        copy.wait()


def bring_odd(place, memory, previous, resident):
    _, rows, depth = memory.shape
    cols = resident.shape[1]
    width = previous.shape[2] // 8
    shapes = [(rows, depth), (width, rows), (width, rows), (depth, cols // 2)]
    return pl.pallas_call(
        bring_odd_kernel,
        in_specs=[SMEM] + [HBM] * 3,
        out_specs=[VMEM] * 4,
        out_shape=[jax.ShapeDtypeStruct(shape, bf16) for shape in shapes],
        scratch_shapes=[
            pltpu.VMEM((2, rows, 2 * width), bf16),
            pltpu.VMEM((2 * width, rows), f32),
            pltpu.SemaphoreType.DMA((3,)),
        ],
        compiler_params=params(6),
        cost_estimate=cost(0, depth * (2 * rows + cols)),
        name="bring_odd",
    )(place, memory, previous, resident)


def bring_even_kernel(place_ref, resident_ref, even_out, sem):
    copy = half_copy(0, place_ref, resident_ref, even_out, sem)
    copy.start()
    copy.wait()


def bring_even(place, resident):
    depth, cols = resident.shape
    return pl.pallas_call(
        bring_even_kernel,
        in_specs=[SMEM, HBM],
        out_specs=VMEM,
        out_shape=jax.ShapeDtypeStruct((depth, cols // 2), bf16),
        scratch_shapes=[pltpu.SemaphoreType.DMA],
        compiler_params=params(4),
        cost_estimate=cost(0, depth * cols),
        name="bring_even",
    )(place, resident)


def place_pair(own, other, first, out_ref):
    near, far = own.astype(f32), other.astype(f32)
    low = jnp.where(first == 0, near, far)
    high = jnp.where(first == 0, far, near)
    out_ref[...] = jnp.concatenate([low, high], axis=0).T.astype(bf16)


def next_memory_kernel(side, place_ref, memory_ref, *refs):
    pair_refs, out_ref = refs[:4], refs[4]
    half = out_ref.shape[1]
    width = half // 4
    for dx in range(4):
        near, far = pair_refs[dx][0].astype(f32), pair_refs[dx ^ 2][1].astype(f32)
        start = position(((place_ref[X] - dx) & 3) ^ place_ref[Y]) * width
        low = jnp.where(place_ref[ZH] == 0, near, far)
        high = jnp.where(place_ref[ZH] == 0, far, near)
        pair = jnp.concatenate([low, high], axis=0).T
        at = pl.ds(pl.multiple_of((place_ref[C] ^ side) * half + start, 128), width)
        to = pl.ds(pl.multiple_of(start, 128), width)
        out_ref[:, to] = (memory_ref[:, at].astype(f32) + pair).astype(bf16)


def next_memory(side, place, memory, pairs):
    rows, depth = memory.shape
    return pl.pallas_call(
        functools.partial(next_memory_kernel, side),
        in_specs=[SMEM] + [VMEM] * 5,
        out_specs=VMEM,
        out_shape=jax.ShapeDtypeStruct((rows, depth // 2), bf16),
        compiler_params=params(6),
        cost_estimate=cost(rows * depth, 3 * rows * depth),
        name="next_memory",
    )(place, memory, *pairs)


def solve_into(part_refs, prior_ref, inverse_ref):
    summed = part_refs[0][...].astype(f32)
    for part_ref in part_refs[1:]:
        summed = summed + part_ref[...].astype(f32)
    source = prior_ref[...].astype(f32) - step_size * summed
    mixed = lax.dot_general(
        source,
        inverse_ref[...],
        (((1,), (1,)), ((), ())),
        precision=lax.Precision.HIGHEST,
        preferred_element_type=f32,
    )
    return (source + mixed).astype(bf16)


def flipped(values):
    rows, cols = values.shape
    strips = []
    pad = jnp.zeros((128 - ORB, 128), f32)
    for s in range(rows // ORB):
        pieces = []
        for q in range(cols // 128):
            block = values[s * ORB : (s + 1) * ORB, q * 128 : (q + 1) * 128]
            turned = jnp.concatenate([block, pad], axis=0).T
            piece = turned[:ORB]
            for t in range(1, 128 // ORB):
                piece = piece + pltpu.roll(turned[t * ORB : (t + 1) * ORB], t * ORB, 1)
            pieces.append(piece)
        strips.append(jnp.concatenate(pieces, axis=1))
    return jnp.concatenate(strips, axis=0)


def first_solve_kernel(place_ref, *refs):
    front_ref, energy_ref = refs[11:]
    front = solve_into(refs[:8], refs[8], refs[9])
    front_ref[...] = front
    values = front.astype(f32)
    mirror = flipped(values)
    rows, cols = values.shape
    coupling = jnp.tile(refs[10][...], (rows // ORB, cols // 128))
    energy_ref[...] = (mirror * mirror * values * coupling).astype(bf16)


def second_solve_kernel(place_ref, *refs):
    refs[10][...] = solve_into(refs[:8], refs[8], refs[9])


def solve(kernel, place, parts, prior, inverse, extra, outputs, name):
    width, rows = prior.shape
    return pl.pallas_call(
        kernel,
        in_specs=[SMEM] + [VMEM] * (len(parts) + 2 + len(extra)),
        out_specs=[VMEM] * outputs,
        out_shape=[jax.ShapeDtypeStruct((width, rows), bf16)] * outputs,
        compiler_params=params(8),
        cost_estimate=cost(12 * rows * rows * width, 24 * rows * width),
        name=name,
    )(place, *parts, prior, inverse, *extra)


def put_blocks(blocks, block_ref, sems, out_ref, front):
    width = block_ref.shape[2]
    copies = []
    for i, (start, write) in enumerate(blocks):
        write(block_ref.at[i])
        at = pl.ds(pl.multiple_of(start, 128), width)
        copies.append(pltpu.make_async_copy(block_ref.at[i], out_ref.at[front, :, at], sems.at[i]))
        copies[i].start()
    for copy in copies:
        copy.wait()


def join_one_kernel(place_ref, own_ref, other_ref, out_ref, block_ref, sems):
    def block(dy):
        def write(ref):
            place_pair(own_ref[dy], other_ref[dy], place_ref[ZL], ref)

        return position((place_ref[Y] - dy) & 3) * block_ref.shape[2], write

    put_blocks([block(dy) for dy in range(4)], block_ref, sems, out_ref, 0)


def join_two_kernel(moves, place_ref, *refs):
    chunk_refs, (out_ref, block_ref, sems) = refs[:4], refs[5:]

    def block(i):
        def write(ref):
            own, other = chunk_refs[2 * i][...], chunk_refs[2 * i + 1][...]
            place_pair(own, other, place_ref[ZL], ref)

        return position((place_ref[Y] - moves[i]) & 3) * block_ref.shape[2], write

    put_blocks([block(i) for i in range(2)], block_ref, sems, out_ref, 1)


def join(kernel, args, in_specs, shape, aliases, name):
    _, rows, cols = shape
    return pl.pallas_call(
        kernel,
        in_specs=in_specs,
        out_specs=HBM,
        out_shape=jax.ShapeDtypeStruct(shape, bf16),
        scratch_shapes=[pltpu.VMEM((4, rows, cols // 4), bf16), pltpu.SemaphoreType.DMA((4,))],
        input_output_aliases=aliases,
        compiler_params=params(6),
        cost_estimate=cost(rows * cols, 4 * rows * cols),
        name=name,
    )(*args)


def move(value, target):
    pairs = []
    for i in range(128):
        rest, c = divmod(i, 2)
        rest, zh = divmod(rest, 2)
        rest, x = divmod(rest, 4)
        y, zl = divmod(rest, 2)
        y, zl, x, zh = target(y, zl, x, zh)
        pairs.append((i, (((y * 2 + zl) * 4 + x) * 2 + zh) * 2 + c))
    return lax.ppermute(value, ALL, pairs)


def turn(flip):
    return lambda y, zl, x, zh: (x, zh, x ^ y ^ (2 * flip), zl ^ flip)


def scatter(shares, first):
    parts = []
    for k in (3, 2, 1, 0) if first == 0 else (1, 0, 3, 2):
        dy, dz = first + 2 * (k >> 1), k & 1
        if (dy, dz) == (0, 0):
            parts.append(shares[k])
        else:
            parts.append(move(shares[k], lambda y, zl, x, zh: (y ^ dy, zl ^ dz, x, zh)))
    return parts


def spread(pair, axis):
    pairs = {0: pair}
    for d in (2, 1, 3):
        pairs[d] = lax.ppermute(pair, axis, [(i, (i + d) % 4) for i in range(4)])
    return [pairs[d] for d in range(4)]


def spread_chunks(value):
    chunks = {(0, 0): value}
    for dy, dz in ((2, 1), (2, 0), (0, 1), (1, 1), (3, 1), (1, 0), (3, 0)):
        chunks[dy, dz] = move(value, lambda y, zl, x, zh: ((y + dy) % 4, zl ^ dz, x, zh))
    return chunks


def per_device(resident, memory, previous, inverse_part, pair_coupling):
    place = jnp.stack([lax.axis_index(name) for name in ("x", "zh", "c", "y", "zl")]).astype(jnp.int32)
    coupling = jnp.tile(pair_coupling, (1, 128 // ORB))

    resident, memory, previous = in_hbm(resident), in_hbm(memory), in_hbm(previous)
    *odd, lhs = first_product(odd_product_kernel, place, memory, resident, [memory.shape[1:]], "odd_product")
    odd_parts = scatter(odd, 1)
    lhs, odd = lax.optimization_barrier((lhs, odd))
    even = first_product(even_product_kernel, place, lhs, resident, [], "even_product")
    even_parts = scatter(even, 0)
    place, _, odd_parts = lax.optimization_barrier((place, even[0], odd_parts))
    memory, prior_one, prior_two, odd_resident = bring_odd(place, memory, previous, resident)
    parts = odd_parts + even_parts
    front_one, energy = solve(
        first_solve_kernel, place, parts, prior_one, inverse_part[0], [coupling], 2, "first_solve"
    )
    pair = [move(energy, turn(0)), move(energy, turn(1))]
    ones = spread(front_one, "y")
    later, _ = lax.optimization_barrier((place, energy))
    even_resident = bring_even(later, resident)
    pair, ones, even_resident = lax.optimization_barrier((pair, ones, even_resident))
    own = spread(jnp.stack(pair), "x")
    ones = jnp.stack(ones)
    others = lax.ppermute(ones, "zl", SWAP)
    other = [lax.ppermute(pair, "c", SWAP) for pair in own]
    own_lhs = next_memory(0, place, memory, own)
    early = early_product(place, own_lhs, odd_resident)
    other, others, early = lax.optimization_barrier((other, others, early))
    other_lhs = next_memory(1, place, memory, other)
    odd = second_product(late_product_kernel, place, early, other_lhs, odd_resident, "late_product")
    own_lhs, odd = lax.optimization_barrier((own_lhs, odd))
    even = second_product(both_product_kernel, place, own_lhs, other_lhs, even_resident, "both_product")
    parts = scatter(odd, 1) + scatter(even, 0)
    (front_two,) = solve(
        second_solve_kernel, place, parts, prior_two, inverse_part[1], [], 1, "second_solve"
    )
    chunks = spread_chunks(front_two)
    fronts = join(join_one_kernel, (place, ones, others), [SMEM, VMEM, VMEM], previous.shape, {}, "join_one")
    for moves in ((0, 2), (1, 3)):
        some = [chunks[dy, dz] for dy in moves for dz in range(2)]
        some, fronts = lax.optimization_barrier((some, fronts))
        fronts = join(
            functools.partial(join_two_kernel, moves),
            (place, *some, fronts),
            [SMEM] + [VMEM] * 4 + [HBM],
            previous.shape,
            {5: 0},
            "join_two",
        )
    return fronts


def solution(mesh):
    fine = Mesh(mesh.devices.reshape(4, 2, 4, 2, 2), ALL)
    in_specs = (P(PASTS, SECONDS), P(None, None, PASTS), P(None, None, SECONDS), P(), P())
    out_specs = P(None, None, SECONDS)
    return jax.shard_map(
        per_device, mesh=fine, in_specs=in_specs, out_specs=out_specs, check_vma=False
    )
```

```python
import functools

import jax
import jax.numpy as jnp
from jax import lax
from jax.experimental import pallas as pl
from jax.experimental.pallas import tpu as pltpu
from jax.sharding import Mesh, PartitionSpec as P

step_size = 0.5
ORB = 32
f32 = jnp.float32
bf16 = jnp.bfloat16
PASTS = ("y", "zl")
SECONDS = ("x", "zh", "c")
ALL = PASTS + SECONDS
SWAP = [(0, 1), (1, 0)]
X, ZH, C, Y, ZL = range(5)


VMEM = pl.BlockSpec(memory_space=pltpu.VMEM)
SMEM = pl.BlockSpec(memory_space=pltpu.SMEM)
HBM = pl.BlockSpec(memory_space=pltpu.HBM)


def in_hbm(array):
    return pltpu.with_memory_space_constraint(array, pltpu.HBM)


def params(megabytes):
    return pltpu.CompilerParams(vmem_limit_bytes=megabytes << 20)


def cost(flops, nbytes):
    return pl.CostEstimate(flops=flops, bytes_accessed=nbytes, transcendentals=0)


def position(y):
    return (y & 1) * 2 + (y >> 1)


def store_shares(place_ref, turned_ref, out_refs):
    width = out_refs[0].shape[0]
    for k, out_ref in enumerate(out_refs):
        share = ((place_ref[Y] >> 1) ^ (k >> 1)) * 2 + (place_ref[ZL] ^ (k & 1))
        out_ref[...] = turned_ref[pl.ds(pl.multiple_of(share * width, width), width), :]


def half_product_kernel(place_ref, lhs_ref, resident_ref, *refs):
    out_refs, turned_ref = refs[:4], refs[4]
    product = jnp.dot(lhs_ref[...], resident_ref[...], preferred_element_type=f32)
    turned_ref[...] = product.T.astype(bf16)
    store_shares(place_ref, turned_ref, out_refs)


def half_product(place, lhs, resident):
    rows, depth = lhs.shape
    cols = resident.shape[1]
    width = cols // 4
    return pl.pallas_call(
        half_product_kernel,
        in_specs=[SMEM, VMEM, VMEM],
        out_specs=[VMEM] * 4,
        out_shape=[jax.ShapeDtypeStruct((width, rows), bf16)] * 4,
        scratch_shapes=[pltpu.VMEM((cols, rows), bf16)],
        compiler_params=params(6),
        cost_estimate=cost(2 * rows * depth * cols, 4 * width * rows),
        name="half_product",
    )(place, lhs, resident)


TILES = 3


def first_product_kernel(place_ref, memory_ref, resident_ref, *refs):
    out_refs, lhs_ref, odd_ref, even_ref, turned_ref, sems = refs[:4], *refs[4:]
    depth, cols = odd_ref.shape
    tile = cols // TILES
    parity = place_ref[Y] & 1

    def tile_copy(half_ref, side, i):
        start = pl.multiple_of((parity ^ side) * cols + i * tile, tile)
        return pltpu.make_async_copy(
            resident_ref.at[:, pl.ds(start, tile)],
            half_ref.at[:, i * tile : (i + 1) * tile],
            sems.at[side * TILES + i],
        )

    memory_copy = pltpu.make_async_copy(memory_ref.at[0], lhs_ref, sems.at[2 * TILES])
    odd = [tile_copy(odd_ref, 1, i) for i in range(TILES)]
    even = [tile_copy(even_ref, 0, i) for i in range(TILES)]
    for copy in (memory_copy, *even):
        copy.start()
    memory_copy.wait()
    for i, copy in enumerate(even):
        copy.wait()
        odd[i].start()
        at = slice(i * tile, (i + 1) * tile)
        product = jnp.dot(lhs_ref[...], even_ref[:, at], preferred_element_type=f32)
        turned_ref[at, :] = product.T.astype(bf16)
    store_shares(place_ref, turned_ref, out_refs)
    for copy in odd:
        copy.wait()


def first_product(place, memory, resident):
    _, rows, depth = memory.shape
    cols = resident.shape[1]
    width = cols // 8
    outs = [((width, rows), 4), ((rows, depth), 1), ((depth, cols // 2), 1)]
    shapes = [jax.ShapeDtypeStruct(shape, bf16) for shape, count in outs for _ in range(count)]
    *even, lhs, odd_resident = pl.pallas_call(
        first_product_kernel,
        in_specs=[SMEM] + [pl.BlockSpec(memory_space=pltpu.HBM)] * 2,
        out_specs=[VMEM] * 6,
        out_shape=shapes,
        scratch_shapes=[
            pltpu.VMEM((depth, cols // 2), bf16),
            pltpu.VMEM((cols // 2, rows), bf16),
            pltpu.SemaphoreType.DMA((2 * TILES + 1,)),
        ],
        compiler_params=params(12),
        cost_estimate=cost(rows * depth * cols, 4 * depth * cols),
        name="first_product",
    )(place, memory, resident)
    return even, lhs, odd_resident


def depth_half(place_ref, side, resident_ref):
    half = resident_ref.shape[0] // 2
    return pl.ds(pl.multiple_of((place_ref[C] ^ side) * half, half), half)


def early_product_kernel(place_ref, lhs_ref, resident_ref, out_ref):
    right = resident_ref[depth_half(place_ref, 0, resident_ref), :]
    out_ref[...] = jnp.dot(lhs_ref[...], right, preferred_element_type=f32)


def early_product(place, lhs, resident):
    rows, depth = lhs.shape
    cols = resident.shape[1]
    return pl.pallas_call(
        early_product_kernel,
        in_specs=[SMEM, VMEM, VMEM],
        out_specs=VMEM,
        out_shape=jax.ShapeDtypeStruct((rows, cols), f32),
        compiler_params=params(6),
        cost_estimate=cost(2 * rows * depth * cols, 4 * rows * cols),
        name="early_product",
    )(place, lhs, resident)


def late_product_kernel(place_ref, early_ref, lhs_ref, resident_ref, *refs):
    out_refs, turned_ref = refs[:4], refs[4]
    right = resident_ref[depth_half(place_ref, 1, resident_ref), :]
    product = early_ref[...] + jnp.dot(lhs_ref[...], right, preferred_element_type=f32)
    turned_ref[...] = product.T.astype(bf16)
    store_shares(place_ref, turned_ref, out_refs)


def both_product_kernel(place_ref, own_ref, other_ref, resident_ref, *refs):
    out_refs, turned_ref = refs[:4], refs[4]
    product = None
    for side, lhs_ref in enumerate((own_ref, other_ref)):
        right = resident_ref[depth_half(place_ref, side, resident_ref), :]
        term = jnp.dot(lhs_ref[...], right, preferred_element_type=f32)
        product = term if product is None else product + term
    turned_ref[...] = product.T.astype(bf16)
    store_shares(place_ref, turned_ref, out_refs)


def second_product(kernel, place, left, lhs, resident, name):
    rows, depth = lhs.shape
    cols = resident.shape[1]
    return pl.pallas_call(
        kernel,
        in_specs=[SMEM] + [VMEM] * 3,
        out_specs=[VMEM] * 4,
        out_shape=[jax.ShapeDtypeStruct((cols // 4, rows), bf16)] * 4,
        scratch_shapes=[pltpu.VMEM((cols, rows), bf16)],
        compiler_params=params(6),
        cost_estimate=cost(2 * rows * depth * cols, 4 * cols * rows),
        name=name,
    )(place, left, lhs, resident)


def half_copy(side, place_ref, resident_ref, out_ref, sem):
    half = out_ref.shape[1]
    at = pl.ds(pl.multiple_of(((place_ref[Y] & 1) ^ side) * half, half), half)
    return pltpu.make_async_copy(resident_ref.at[:, at], out_ref, sem)


def bring_soon_kernel(
    place_ref, memory_ref, previous_ref, resident_ref, memory_out, one_out, two_out, even_out, prior_ref, turned_ref, sems
):
    width, rows = one_out.shape
    start = position(place_ref[Y]) * 2 * width
    cols = pl.ds(pl.multiple_of(start, 128), 2 * width)
    copies = [
        pltpu.make_async_copy(previous_ref.at[:, :, cols], prior_ref, sems.at[0]),
        pltpu.make_async_copy(memory_ref.at[1], memory_out, sems.at[1]),
        half_copy(0, place_ref, resident_ref, even_out, sems.at[2]),
    ]
    for copy in copies:
        copy.start()
    copies[0].wait()
    for front, out_ref in enumerate((one_out, two_out)):
        turned_ref[...] = prior_ref[front].astype(f32).T
        share = turned_ref[pl.ds(pl.multiple_of(place_ref[ZL] * width, width), width), :]
        out_ref[...] = share.astype(bf16)
    for copy in copies[1:]:
        copy.wait()


def bring_soon(place, memory, previous, resident):
    _, rows, depth = memory.shape
    cols = resident.shape[1]
    width = previous.shape[2] // 8
    shapes = [(rows, depth), (width, rows), (width, rows), (depth, cols // 2)]
    return pl.pallas_call(
        bring_soon_kernel,
        in_specs=[SMEM] + [HBM] * 3,
        out_specs=[VMEM] * 4,
        out_shape=[jax.ShapeDtypeStruct(shape, bf16) for shape in shapes],
        scratch_shapes=[
            pltpu.VMEM((2, rows, 2 * width), bf16),
            pltpu.VMEM((2 * width, rows), f32),
            pltpu.SemaphoreType.DMA((3,)),
        ],
        compiler_params=params(6),
        cost_estimate=cost(0, depth * (2 * rows + cols)),
        name="bring_soon",
    )(place, memory, previous, resident)


def bring_late_kernel(place_ref, resident_ref, odd_out, sem):
    copy = half_copy(1, place_ref, resident_ref, odd_out, sem)
    copy.start()
    copy.wait()


def bring_late(place, resident):
    depth, cols = resident.shape
    return pl.pallas_call(
        bring_late_kernel,
        in_specs=[SMEM, HBM],
        out_specs=VMEM,
        out_shape=jax.ShapeDtypeStruct((depth, cols // 2), bf16),
        scratch_shapes=[pltpu.SemaphoreType.DMA],
        compiler_params=params(4),
        cost_estimate=cost(0, depth * cols),
        name="bring_late",
    )(place, resident)


def place_pair(own, other, first, out_ref):
    near, far = own.astype(f32), other.astype(f32)
    low = jnp.where(first == 0, near, far)
    high = jnp.where(first == 0, far, near)
    out_ref[...] = jnp.concatenate([low, high], axis=0).T.astype(bf16)


def next_memory_kernel(side, place_ref, memory_ref, *refs):
    pair_refs, out_ref = refs[:4], refs[4]
    half = out_ref.shape[1]
    width = half // 4
    for dx in range(4):
        near, far = pair_refs[dx][0].astype(f32), pair_refs[dx ^ 2][1].astype(f32)
        start = position(((place_ref[X] - dx) & 3) ^ place_ref[Y]) * width
        low = jnp.where(place_ref[ZH] == 0, near, far)
        high = jnp.where(place_ref[ZH] == 0, far, near)
        pair = jnp.concatenate([low, high], axis=0).T
        at = pl.ds(pl.multiple_of((place_ref[C] ^ side) * half + start, 128), width)
        to = pl.ds(pl.multiple_of(start, 128), width)
        out_ref[:, to] = (memory_ref[:, at].astype(f32) + pair).astype(bf16)


def next_memory(side, place, memory, pairs):
    rows, depth = memory.shape
    return pl.pallas_call(
        functools.partial(next_memory_kernel, side),
        in_specs=[SMEM] + [VMEM] * 5,
        out_specs=VMEM,
        out_shape=jax.ShapeDtypeStruct((rows, depth // 2), bf16),
        compiler_params=params(6),
        cost_estimate=cost(rows * depth, 3 * rows * depth),
        name="next_memory",
    )(place, memory, *pairs)


def solve_into(part_refs, prior_ref, inverse_ref):
    summed = part_refs[0][...].astype(f32)
    for part_ref in part_refs[1:]:
        summed = summed + part_ref[...].astype(f32)
    source = prior_ref[...].astype(f32) - step_size * summed
    mixed = lax.dot_general(
        source,
        inverse_ref[...],
        (((1,), (1,)), ((), ())),
        precision=lax.Precision.HIGHEST,
        preferred_element_type=f32,
    )
    return (source + mixed).astype(bf16)


def flipped(values):
    rows, cols = values.shape
    strips = []
    pad = jnp.zeros((128 - ORB, 128), f32)
    for s in range(rows // ORB):
        pieces = []
        for q in range(cols // 128):
            block = values[s * ORB : (s + 1) * ORB, q * 128 : (q + 1) * 128]
            turned = jnp.concatenate([block, pad], axis=0).T
            piece = turned[:ORB]
            for t in range(1, 128 // ORB):
                piece = piece + pltpu.roll(turned[t * ORB : (t + 1) * ORB], t * ORB, 1)
            pieces.append(piece)
        strips.append(jnp.concatenate(pieces, axis=1))
    return jnp.concatenate(strips, axis=0)


def first_solve_kernel(place_ref, *refs):
    front_ref, energy_ref = refs[8:]
    front = solve_into(refs[:5], refs[5], refs[6])
    front_ref[...] = front
    values = front.astype(f32)
    mirror = flipped(values)
    rows, cols = values.shape
    coupling = jnp.tile(refs[7][...], (rows // ORB, cols // 128))
    energy_ref[...] = (mirror * mirror * values * coupling).astype(bf16)


def second_solve_kernel(place_ref, *refs):
    refs[7][...] = solve_into(refs[:5], refs[5], refs[6])


def solve(kernel, place, parts, prior, inverse, extra, outputs, name):
    width, rows = prior.shape
    return pl.pallas_call(
        kernel,
        in_specs=[SMEM] + [VMEM] * (len(parts) + 2 + len(extra)),
        out_specs=[VMEM] * outputs,
        out_shape=[jax.ShapeDtypeStruct((width, rows), bf16)] * outputs,
        compiler_params=params(8),
        cost_estimate=cost(12 * rows * rows * width, 24 * rows * width),
        name=name,
    )(place, *parts, prior, inverse, *extra)


def put_blocks(blocks, block_ref, sems, out_ref, front):
    width = block_ref.shape[2]
    copies = []
    for i, (start, write) in enumerate(blocks):
        write(block_ref.at[i])
        at = pl.ds(pl.multiple_of(start, 128), width)
        copies.append(pltpu.make_async_copy(block_ref.at[i], out_ref.at[front, :, at], sems.at[i]))
        copies[i].start()
    for copy in copies:
        copy.wait()


def join_one_kernel(place_ref, own_ref, other_ref, out_ref, block_ref, sems):
    def block(dy):
        def write(ref):
            place_pair(own_ref[dy], other_ref[dy], place_ref[ZL], ref)

        return position((place_ref[Y] - dy) & 3) * block_ref.shape[2], write

    put_blocks([block(dy) for dy in range(4)], block_ref, sems, out_ref, 0)


def join_two_kernel(place_ref, *refs):
    own_refs, twin_refs, (out_ref, block_ref, sems) = refs[:4], refs[4:8], refs[9:]

    def block(dy):
        def write(ref):
            place_pair(own_refs[dy][...], twin_refs[dy][...], place_ref[ZL], ref)

        return position((place_ref[Y] - dy) & 3) * block_ref.shape[2], write

    put_blocks([block(dy) for dy in range(4)], block_ref, sems, out_ref, 1)


def join(kernel, args, in_specs, shape, aliases, name):
    _, rows, cols = shape
    return pl.pallas_call(
        kernel,
        in_specs=in_specs,
        out_specs=HBM,
        out_shape=jax.ShapeDtypeStruct(shape, bf16),
        scratch_shapes=[pltpu.VMEM((4, rows, cols // 4), bf16), pltpu.SemaphoreType.DMA((4,))],
        input_output_aliases=aliases,
        compiler_params=params(6),
        cost_estimate=cost(rows * cols, 4 * rows * cols),
        name=name,
    )(*args)


def move(value, target):
    pairs = []
    for i in range(128):
        rest, c = divmod(i, 2)
        rest, zh = divmod(rest, 2)
        rest, x = divmod(rest, 4)
        y, zl = divmod(rest, 2)
        y, zl, x, zh = target(y, zl, x, zh)
        pairs.append((i, (((y * 2 + zl) * 4 + x) * 2 + zh) * 2 + c))
    return lax.ppermute(value, ALL, pairs)


def turn(flip):
    return lambda y, zl, x, zh: (x, zh, x ^ y ^ (2 * flip), zl ^ flip)


def sum_kernel(*refs):
    total = refs[0][...].astype(f32)
    for ref in refs[1:-1]:
        total = total + ref[...].astype(f32)
    refs[-1][...] = total.astype(bf16)


def add_up(values):
    return pl.pallas_call(
        sum_kernel,
        in_specs=[VMEM] * len(values),
        out_specs=VMEM,
        out_shape=jax.ShapeDtypeStruct(values[0].shape, bf16),
        compiler_params=params(4),
        cost_estimate=cost(4 * values[0].size, 10 * values[0].size),
        name="add_up",
    )(*values)


def scatter(even, odd):
    def along_y(share, dy):
        return move(share, lambda y, zl, x, zh: (y ^ dy, zl, x, zh))

    far = along_y(even[3], 2)
    own_two, far, odd = lax.optimization_barrier((even[2], far, odd))
    far = [far, along_y(odd[1], 1), along_y(odd[3], 3)]
    near = [along_y(own_two, 2), along_y(odd[0], 1), along_y(odd[2], 3)]
    for_twin = add_up([even[1], *far])
    return [even[0], *near, lax.ppermute(for_twin, "zl", SWAP)], for_twin


def spread(pair, axis):
    pairs = {0: pair}
    for d in (2, 1, 3):
        pairs[d] = lax.ppermute(pair, axis, [(i, (i + d) % 4) for i in range(4)])
    return [pairs[d] for d in range(4)]


def per_device(resident, memory, previous, inverse_part, pair_coupling):
    place = jnp.stack([lax.axis_index(name) for name in ("x", "zh", "c", "y", "zl")]).astype(jnp.int32)
    coupling = jnp.tile(pair_coupling, (1, 128 // ORB))

    resident, memory, previous = in_hbm(resident), in_hbm(memory), in_hbm(previous)
    even, lhs, odd_resident = first_product(place, memory, resident)
    lhs, even = lax.optimization_barrier((lhs, even))
    odd = half_product(place, lhs, odd_resident)
    parts, for_twin = scatter(even, odd)
    later, _ = lax.optimization_barrier((place, for_twin))
    memory, prior_one, prior_two, even_resident = bring_soon(later, memory, previous, resident)
    front_one, energy = solve(
        first_solve_kernel, place, parts, prior_one, inverse_part[0], [coupling], 2, "first_solve"
    )
    pair = [move(energy, turn(0)), move(energy, turn(1))]
    ones = spread(front_one, "y")
    later, _ = lax.optimization_barrier((place, energy))
    odd_resident = bring_late(later, resident)
    pair, ones, odd_resident = lax.optimization_barrier((pair, ones, odd_resident))
    own = spread(jnp.stack(pair), "x")
    ones = jnp.stack(ones)
    others = lax.ppermute(ones, "zl", SWAP)
    other = [lax.ppermute(pair, "c", SWAP) for pair in own]
    own_lhs = next_memory(0, place, memory, own)
    early = early_product(place, own_lhs, even_resident)
    other, others, early = lax.optimization_barrier((other, others, early))
    other_lhs = next_memory(1, place, memory, other)
    even = second_product(late_product_kernel, place, early, other_lhs, even_resident, "late_product")
    own_lhs, even = lax.optimization_barrier((own_lhs, even))
    odd = second_product(both_product_kernel, place, own_lhs, other_lhs, odd_resident, "both_product")
    parts, _ = scatter(even, odd)
    (front_two,) = solve(
        second_solve_kernel, place, parts, prior_two, inverse_part[1], [], 1, "second_solve"
    )
    twin = lax.ppermute(front_two, "zl", SWAP)
    chunks = [*spread(front_two, "y"), *spread(twin, "y")]
    fronts = join(join_one_kernel, (place, ones, others), [SMEM, VMEM, VMEM], previous.shape, {}, "join_one")
    return join(
        join_two_kernel, (place, *chunks, fronts), [SMEM] + [VMEM] * 8 + [HBM], previous.shape, {9: 0}, "join_two"
    )


def solution(mesh):
    fine = Mesh(mesh.devices.reshape(4, 2, 4, 2, 2), ALL)
    in_specs = (P(PASTS, SECONDS), P(None, None, PASTS), P(None, None, SECONDS), P(), P())
    out_specs = P(None, None, SECONDS)
    return jax.shard_map(
        per_device, mesh=fine, in_specs=in_specs, out_specs=out_specs, check_vma=False
    )
```

```python
import functools

import jax
import jax.numpy as jnp
from jax import lax
from jax.experimental import pallas as pl
from jax.experimental.pallas import tpu as pltpu
from jax.sharding import Mesh, PartitionSpec as P

step_size = 0.5
ORB = 32
f32 = jnp.float32
bf16 = jnp.bfloat16
PASTS = ("y", "zl")
SECONDS = ("x", "zh", "c")
ALL = PASTS + SECONDS
SWAP = [(0, 1), (1, 0)]
X, ZH, C, Y, ZL = range(5)


VMEM = pl.BlockSpec(memory_space=pltpu.VMEM)
SMEM = pl.BlockSpec(memory_space=pltpu.SMEM)
HBM = pl.BlockSpec(memory_space=pltpu.HBM)


def in_hbm(array):
    return pltpu.with_memory_space_constraint(array, pltpu.HBM)


def params(megabytes):
    return pltpu.CompilerParams(vmem_limit_bytes=megabytes << 20)


def cost(flops, nbytes):
    return pl.CostEstimate(flops=flops, bytes_accessed=nbytes, transcendentals=0)


def position(y):
    return (y & 1) * 2 + (y >> 1)


def store_shares(place_ref, turned_ref, out_refs):
    width = out_refs[0].shape[0]
    for k, out_ref in enumerate(out_refs):
        share = ((place_ref[Y] >> 1) ^ (k >> 1)) * 2 + (place_ref[ZL] ^ (k & 1))
        out_ref[...] = turned_ref[pl.ds(pl.multiple_of(share * width, width), width), :]


def half_product_kernel(place_ref, lhs_ref, resident_ref, *refs):
    out_refs, turned_ref = refs[:4], refs[4]
    product = jnp.dot(lhs_ref[...], resident_ref[...], preferred_element_type=f32)
    turned_ref[...] = product.T.astype(bf16)
    store_shares(place_ref, turned_ref, out_refs)


def half_product(place, lhs, resident):
    rows, depth = lhs.shape
    cols = resident.shape[1]
    width = cols // 4
    return pl.pallas_call(
        half_product_kernel,
        in_specs=[SMEM, VMEM, VMEM],
        out_specs=[VMEM] * 4,
        out_shape=[jax.ShapeDtypeStruct((width, rows), bf16)] * 4,
        scratch_shapes=[pltpu.VMEM((cols, rows), bf16)],
        compiler_params=params(6),
        cost_estimate=cost(2 * rows * depth * cols, 4 * width * rows),
        name="half_product",
    )(place, lhs, resident)


TILES = 3


def first_product_kernel(place_ref, memory_ref, resident_ref, *refs):
    out_refs, lhs_ref, even_ref, odd_ref, turned_ref, sems = refs[:4], *refs[4:]
    depth, cols = odd_ref.shape
    tile = cols // TILES
    parity = place_ref[Y] & 1

    def tile_copy(half_ref, side, i):
        start = pl.multiple_of((parity ^ side) * cols + i * tile, tile)
        return pltpu.make_async_copy(
            resident_ref.at[:, pl.ds(start, tile)],
            half_ref.at[:, i * tile : (i + 1) * tile],
            sems.at[side * TILES + i],
        )

    memory_copy = pltpu.make_async_copy(memory_ref.at[0], lhs_ref, sems.at[2 * TILES])
    odd = [tile_copy(odd_ref, 1, i) for i in range(TILES)]
    even = [tile_copy(even_ref, 0, i) for i in range(TILES)]
    for copy in (memory_copy, *odd):
        copy.start()
    memory_copy.wait()
    for i, copy in enumerate(odd):
        copy.wait()
        even[i].start()
        at = slice(i * tile, (i + 1) * tile)
        product = jnp.dot(lhs_ref[...], odd_ref[:, at], preferred_element_type=f32)
        turned_ref[at, :] = product.T.astype(bf16)
    store_shares(place_ref, turned_ref, out_refs)
    for copy in even:
        copy.wait()


def first_product(place, memory, resident):
    _, rows, depth = memory.shape
    cols = resident.shape[1]
    width = cols // 8
    outs = [((width, rows), 4), ((rows, depth), 1), ((depth, cols // 2), 1)]
    shapes = [jax.ShapeDtypeStruct(shape, bf16) for shape, count in outs for _ in range(count)]
    *odd, lhs, even_resident = pl.pallas_call(
        first_product_kernel,
        in_specs=[SMEM] + [pl.BlockSpec(memory_space=pltpu.HBM)] * 2,
        out_specs=[VMEM] * 6,
        out_shape=shapes,
        scratch_shapes=[
            pltpu.VMEM((depth, cols // 2), bf16),
            pltpu.VMEM((cols // 2, rows), bf16),
            pltpu.SemaphoreType.DMA((2 * TILES + 1,)),
        ],
        compiler_params=params(12),
        cost_estimate=cost(rows * depth * cols, 4 * depth * cols),
        name="first_product",
    )(place, memory, resident)
    return odd, lhs, even_resident


def depth_half(place_ref, side, resident_ref):
    half = resident_ref.shape[0] // 2
    return pl.ds(pl.multiple_of((place_ref[C] ^ side) * half, half), half)


def early_product_kernel(place_ref, lhs_ref, resident_ref, out_ref):
    right = resident_ref[depth_half(place_ref, 0, resident_ref), :]
    out_ref[...] = jnp.dot(lhs_ref[...], right, preferred_element_type=f32)


def early_product(place, lhs, resident):
    rows, depth = lhs.shape
    cols = resident.shape[1]
    return pl.pallas_call(
        early_product_kernel,
        in_specs=[SMEM, VMEM, VMEM],
        out_specs=VMEM,
        out_shape=jax.ShapeDtypeStruct((rows, cols), f32),
        compiler_params=params(6),
        cost_estimate=cost(2 * rows * depth * cols, 4 * rows * cols),
        name="early_product",
    )(place, lhs, resident)


def late_product_kernel(place_ref, early_ref, lhs_ref, resident_ref, *refs):
    out_refs, turned_ref = refs[:4], refs[4]
    right = resident_ref[depth_half(place_ref, 1, resident_ref), :]
    product = early_ref[...] + jnp.dot(lhs_ref[...], right, preferred_element_type=f32)
    turned_ref[...] = product.T.astype(bf16)
    store_shares(place_ref, turned_ref, out_refs)


def both_product_kernel(place_ref, own_ref, other_ref, resident_ref, *refs):
    out_refs, turned_ref = refs[:4], refs[4]
    product = None
    for side, lhs_ref in enumerate((own_ref, other_ref)):
        right = resident_ref[depth_half(place_ref, side, resident_ref), :]
        term = jnp.dot(lhs_ref[...], right, preferred_element_type=f32)
        product = term if product is None else product + term
    turned_ref[...] = product.T.astype(bf16)
    store_shares(place_ref, turned_ref, out_refs)


def second_product(kernel, place, left, lhs, resident, name):
    rows, depth = lhs.shape
    cols = resident.shape[1]
    return pl.pallas_call(
        kernel,
        in_specs=[SMEM] + [VMEM] * 3,
        out_specs=[VMEM] * 4,
        out_shape=[jax.ShapeDtypeStruct((cols // 4, rows), bf16)] * 4,
        scratch_shapes=[pltpu.VMEM((cols, rows), bf16)],
        compiler_params=params(6),
        cost_estimate=cost(2 * rows * depth * cols, 4 * cols * rows),
        name=name,
    )(place, left, lhs, resident)


def half_copy(side, place_ref, resident_ref, out_ref, sem):
    half = out_ref.shape[1]
    at = pl.ds(pl.multiple_of(((place_ref[Y] & 1) ^ side) * half, half), half)
    return pltpu.make_async_copy(resident_ref.at[:, at], out_ref, sem)


def bring_odd_kernel(
    place_ref, memory_ref, previous_ref, resident_ref, memory_out, one_out, two_out, odd_out, prior_ref, turned_ref, sems
):
    width, rows = one_out.shape
    start = position(place_ref[Y]) * 2 * width
    cols = pl.ds(pl.multiple_of(start, 128), 2 * width)
    copies = [
        pltpu.make_async_copy(previous_ref.at[:, :, cols], prior_ref, sems.at[0]),
        pltpu.make_async_copy(memory_ref.at[1], memory_out, sems.at[1]),
        half_copy(1, place_ref, resident_ref, odd_out, sems.at[2]),
    ]
    for copy in copies:
        copy.start()
    copies[0].wait()
    for front, out_ref in enumerate((one_out, two_out)):
        turned_ref[...] = prior_ref[front].astype(f32).T
        share = turned_ref[pl.ds(pl.multiple_of(place_ref[ZL] * width, width), width), :]
        out_ref[...] = share.astype(bf16)
    for copy in copies[1:]:
        copy.wait()


def bring_odd(place, memory, previous, resident):
    _, rows, depth = memory.shape
    cols = resident.shape[1]
    width = previous.shape[2] // 8
    shapes = [(rows, depth), (width, rows), (width, rows), (depth, cols // 2)]
    return pl.pallas_call(
        bring_odd_kernel,
        in_specs=[SMEM] + [HBM] * 3,
        out_specs=[VMEM] * 4,
        out_shape=[jax.ShapeDtypeStruct(shape, bf16) for shape in shapes],
        scratch_shapes=[
            pltpu.VMEM((2, rows, 2 * width), bf16),
            pltpu.VMEM((2 * width, rows), f32),
            pltpu.SemaphoreType.DMA((3,)),
        ],
        compiler_params=params(6),
        cost_estimate=cost(0, depth * (2 * rows + cols)),
        name="bring_odd",
    )(place, memory, previous, resident)


def bring_even_kernel(place_ref, resident_ref, even_out, sem):
    copy = half_copy(0, place_ref, resident_ref, even_out, sem)
    copy.start()
    copy.wait()


def bring_even(place, resident):
    depth, cols = resident.shape
    return pl.pallas_call(
        bring_even_kernel,
        in_specs=[SMEM, HBM],
        out_specs=VMEM,
        out_shape=jax.ShapeDtypeStruct((depth, cols // 2), bf16),
        scratch_shapes=[pltpu.SemaphoreType.DMA],
        compiler_params=params(4),
        cost_estimate=cost(0, depth * cols),
        name="bring_even",
    )(place, resident)


def place_pair(own, other, first, out_ref):
    near, far = own.astype(f32), other.astype(f32)
    low = jnp.where(first == 0, near, far)
    high = jnp.where(first == 0, far, near)
    out_ref[...] = jnp.concatenate([low, high], axis=0).T.astype(bf16)


def next_memory_kernel(side, place_ref, memory_ref, *refs):
    pair_refs, out_ref = refs[:4], refs[4]
    half = out_ref.shape[1]
    width = half // 4
    for dx in range(4):
        near, far = pair_refs[dx][0].astype(f32), pair_refs[dx ^ 2][1].astype(f32)
        start = position(((place_ref[X] - dx) & 3) ^ place_ref[Y]) * width
        low = jnp.where(place_ref[ZH] == 0, near, far)
        high = jnp.where(place_ref[ZH] == 0, far, near)
        pair = jnp.concatenate([low, high], axis=0).T
        at = pl.ds(pl.multiple_of((place_ref[C] ^ side) * half + start, 128), width)
        to = pl.ds(pl.multiple_of(start, 128), width)
        out_ref[:, to] = (memory_ref[:, at].astype(f32) + pair).astype(bf16)


def next_memory(side, place, memory, pairs):
    rows, depth = memory.shape
    return pl.pallas_call(
        functools.partial(next_memory_kernel, side),
        in_specs=[SMEM] + [VMEM] * 5,
        out_specs=VMEM,
        out_shape=jax.ShapeDtypeStruct((rows, depth // 2), bf16),
        compiler_params=params(6),
        cost_estimate=cost(rows * depth, 3 * rows * depth),
        name="next_memory",
    )(place, memory, *pairs)


def solve_into(part_refs, prior_ref, inverse_ref):
    summed = part_refs[0][...].astype(f32)
    for part_ref in part_refs[1:]:
        summed = summed + part_ref[...].astype(f32)
    source = prior_ref[...].astype(f32) - step_size * summed
    mixed = lax.dot_general(
        source,
        inverse_ref[...],
        (((1,), (1,)), ((), ())),
        precision=lax.Precision.HIGHEST,
        preferred_element_type=f32,
    )
    return (source + mixed).astype(bf16)


def flipped(values):
    rows, cols = values.shape
    strips = []
    pad = jnp.zeros((128 - ORB, 128), f32)
    for s in range(rows // ORB):
        pieces = []
        for q in range(cols // 128):
            block = values[s * ORB : (s + 1) * ORB, q * 128 : (q + 1) * 128]
            turned = jnp.concatenate([block, pad], axis=0).T
            piece = turned[:ORB]
            for t in range(1, 128 // ORB):
                piece = piece + pltpu.roll(turned[t * ORB : (t + 1) * ORB], t * ORB, 1)
            pieces.append(piece)
        strips.append(jnp.concatenate(pieces, axis=1))
    return jnp.concatenate(strips, axis=0)


def first_solve_kernel(place_ref, *refs):
    front_ref, energy_ref = refs[11:]
    front = solve_into(refs[:8], refs[8], refs[9])
    front_ref[...] = front
    values = front.astype(f32)
    mirror = flipped(values)
    rows, cols = values.shape
    coupling = jnp.tile(refs[10][...], (rows // ORB, cols // 128))
    energy_ref[...] = (mirror * mirror * values * coupling).astype(bf16)


def second_solve_kernel(place_ref, *refs):
    refs[10][...] = solve_into(refs[:8], refs[8], refs[9])


def solve(kernel, place, parts, prior, inverse, extra, outputs, name):
    width, rows = prior.shape
    return pl.pallas_call(
        kernel,
        in_specs=[SMEM] + [VMEM] * (len(parts) + 2 + len(extra)),
        out_specs=[VMEM] * outputs,
        out_shape=[jax.ShapeDtypeStruct((width, rows), bf16)] * outputs,
        compiler_params=params(8),
        cost_estimate=cost(12 * rows * rows * width, 24 * rows * width),
        name=name,
    )(place, *parts, prior, inverse, *extra)


def put_blocks(blocks, block_ref, sems, out_ref, front):
    width = block_ref.shape[2]
    copies = []
    for i, (start, write) in enumerate(blocks):
        write(block_ref.at[i])
        at = pl.ds(pl.multiple_of(start, 128), width)
        copies.append(pltpu.make_async_copy(block_ref.at[i], out_ref.at[front, :, at], sems.at[i]))
        copies[i].start()
    for copy in copies:
        copy.wait()


def join_one_kernel(place_ref, own_ref, other_ref, out_ref, block_ref, sems):
    def block(dy):
        def write(ref):
            place_pair(own_ref[dy], other_ref[dy], place_ref[ZL], ref)

        return position((place_ref[Y] - dy) & 3) * block_ref.shape[2], write

    put_blocks([block(dy) for dy in range(4)], block_ref, sems, out_ref, 0)


def join_two_kernel(place_ref, *refs):
    own_refs, twin_refs, (out_ref, block_ref, sems) = refs[:4], refs[4:8], refs[9:]

    def block(dy):
        def write(ref):
            place_pair(own_refs[dy][...], twin_refs[dy][...], place_ref[ZL], ref)

        return position((place_ref[Y] - dy) & 3) * block_ref.shape[2], write

    put_blocks([block(dy) for dy in range(4)], block_ref, sems, out_ref, 1)


def join(kernel, args, in_specs, shape, aliases, name):
    _, rows, cols = shape
    return pl.pallas_call(
        kernel,
        in_specs=in_specs,
        out_specs=HBM,
        out_shape=jax.ShapeDtypeStruct(shape, bf16),
        scratch_shapes=[pltpu.VMEM((4, rows, cols // 4), bf16), pltpu.SemaphoreType.DMA((4,))],
        input_output_aliases=aliases,
        compiler_params=params(6),
        cost_estimate=cost(rows * cols, 4 * rows * cols),
        name=name,
    )(*args)


def move(value, target):
    pairs = []
    for i in range(128):
        rest, c = divmod(i, 2)
        rest, zh = divmod(rest, 2)
        rest, x = divmod(rest, 4)
        y, zl = divmod(rest, 2)
        y, zl, x, zh = target(y, zl, x, zh)
        pairs.append((i, (((y * 2 + zl) * 4 + x) * 2 + zh) * 2 + c))
    return lax.ppermute(value, ALL, pairs)


def turn(flip):
    return lambda y, zl, x, zh: (x, zh, x ^ y ^ (2 * flip), zl ^ flip)


def scatter(shares, first):
    parts = []
    for k in (3, 2, 1, 0) if first == 0 else (1, 0, 3, 2):
        dy, dz = first + 2 * (k >> 1), k & 1
        if (dy, dz) == (0, 0):
            parts.append(shares[k])
        else:
            parts.append(move(shares[k], lambda y, zl, x, zh: (y ^ dy, zl ^ dz, x, zh)))
    return parts


def spread(pair, axis):
    pairs = {0: pair}
    for d in (2, 1, 3):
        pairs[d] = lax.ppermute(pair, axis, [(i, (i + d) % 4) for i in range(4)])
    return [pairs[d] for d in range(4)]


def per_device(resident, memory, previous, inverse_part, pair_coupling):
    place = jnp.stack([lax.axis_index(name) for name in ("x", "zh", "c", "y", "zl")]).astype(jnp.int32)
    coupling = jnp.tile(pair_coupling, (1, 128 // ORB))

    resident, memory, previous = in_hbm(resident), in_hbm(memory), in_hbm(previous)
    odd, lhs, even_resident = first_product(place, memory, resident)
    odd_parts = scatter(odd, 1)
    lhs, odd = lax.optimization_barrier((lhs, odd))
    even = half_product(place, lhs, even_resident)
    even_parts = scatter(even, 0)
    place, _, odd_parts = lax.optimization_barrier((place, even[0], odd_parts))
    memory, prior_one, prior_two, odd_resident = bring_odd(place, memory, previous, resident)
    parts = odd_parts + even_parts
    front_one, energy = solve(
        first_solve_kernel, place, parts, prior_one, inverse_part[0], [coupling], 2, "first_solve"
    )
    pair = [move(energy, turn(0)), move(energy, turn(1))]
    ones = spread(front_one, "y")
    later, _ = lax.optimization_barrier((place, energy))
    even_resident = bring_even(later, resident)
    pair, ones, even_resident = lax.optimization_barrier((pair, ones, even_resident))
    own = spread(jnp.stack(pair), "x")
    ones = jnp.stack(ones)
    others = lax.ppermute(ones, "zl", SWAP)
    other = [lax.ppermute(pair, "c", SWAP) for pair in own]
    own_lhs = next_memory(0, place, memory, own)
    early = early_product(place, own_lhs, odd_resident)
    other, others, early = lax.optimization_barrier((other, others, early))
    other_lhs = next_memory(1, place, memory, other)
    odd = second_product(late_product_kernel, place, early, other_lhs, odd_resident, "late_product")
    own_lhs, odd = lax.optimization_barrier((own_lhs, odd))
    even = second_product(both_product_kernel, place, own_lhs, other_lhs, even_resident, "both_product")
    parts = scatter(odd, 1) + scatter(even, 0)
    (front_two,) = solve(
        second_solve_kernel, place, parts, prior_two, inverse_part[1], [], 1, "second_solve"
    )
    twin = lax.ppermute(front_two, "zl", SWAP)
    chunks = [*spread(front_two, "y"), *spread(twin, "y")]
    fronts = join(join_one_kernel, (place, ones, others), [SMEM, VMEM, VMEM], previous.shape, {}, "join_one")
    return join(
        join_two_kernel, (place, *chunks, fronts), [SMEM] + [VMEM] * 8 + [HBM], previous.shape, {9: 0}, "join_two"
    )


def solution(mesh):
    fine = Mesh(mesh.devices.reshape(4, 2, 4, 2, 2), ALL)
    in_specs = (P(PASTS, SECONDS), P(None, None, PASTS), P(None, None, SECONDS), P(), P())
    out_specs = P(None, None, SECONDS)
    return jax.shard_map(
        per_device, mesh=fine, in_specs=in_specs, out_specs=out_specs, check_vma=False
    )
```

```python
import functools

import jax
import jax.numpy as jnp
from jax import lax
from jax.experimental import pallas as pl
from jax.experimental.pallas import tpu as pltpu
from jax.sharding import Mesh, PartitionSpec as P

step_size = 0.5
ORB = 32
f32 = jnp.float32
bf16 = jnp.bfloat16
PASTS = ("y", "zl")
SECONDS = ("x", "zh", "c")
ALL = PASTS + SECONDS
SWAP = [(0, 1), (1, 0)]
X, ZH, C, Y, ZL = range(5)


VMEM = pl.BlockSpec(memory_space=pltpu.VMEM)
SMEM = pl.BlockSpec(memory_space=pltpu.SMEM)
HBM = pl.BlockSpec(memory_space=pltpu.HBM)


def in_hbm(array):
    return pltpu.with_memory_space_constraint(array, pltpu.HBM)


def params(megabytes):
    return pltpu.CompilerParams(vmem_limit_bytes=megabytes << 20)


def cost(flops, nbytes):
    return pl.CostEstimate(flops=flops, bytes_accessed=nbytes, transcendentals=0)


def position(y):
    return (y & 1) * 2 + (y >> 1)


def store_shares(place_ref, turned_ref, out_refs):
    width = out_refs[0].shape[0]
    for k, out_ref in enumerate(out_refs):
        share = ((place_ref[Y] >> 1) ^ (k >> 1)) * 2 + (place_ref[ZL] ^ (k & 1))
        out_ref[...] = turned_ref[pl.ds(pl.multiple_of(share * width, width), width), :]


def half_product_kernel(place_ref, lhs_ref, resident_ref, *refs):
    out_refs, turned_ref = refs[:4], refs[4]
    product = jnp.dot(lhs_ref[...], resident_ref[...], preferred_element_type=f32)
    turned_ref[...] = product.T.astype(bf16)
    store_shares(place_ref, turned_ref, out_refs)


def half_product(place, lhs, resident):
    rows, depth = lhs.shape
    cols = resident.shape[1]
    width = cols // 4
    return pl.pallas_call(
        half_product_kernel,
        in_specs=[SMEM, VMEM, VMEM],
        out_specs=[VMEM] * 4,
        out_shape=[jax.ShapeDtypeStruct((width, rows), bf16)] * 4,
        scratch_shapes=[pltpu.VMEM((cols, rows), bf16)],
        compiler_params=params(6),
        cost_estimate=cost(2 * rows * depth * cols, 4 * width * rows),
        name="half_product",
    )(place, lhs, resident)


TILES = 3


def first_product_kernel(place_ref, memory_ref, resident_ref, *refs):
    out_refs, lhs_ref, even_ref, odd_ref, turned_ref, sems = refs[:4], *refs[4:]
    depth, cols = odd_ref.shape
    tile = cols // TILES
    parity = place_ref[Y] & 1

    def tile_copy(half_ref, side, i):
        start = pl.multiple_of((parity ^ side) * cols + i * tile, tile)
        return pltpu.make_async_copy(
            resident_ref.at[:, pl.ds(start, tile)],
            half_ref.at[:, i * tile : (i + 1) * tile],
            sems.at[side * TILES + i],
        )

    memory_copy = pltpu.make_async_copy(memory_ref.at[0], lhs_ref, sems.at[2 * TILES])
    odd = [tile_copy(odd_ref, 1, i) for i in range(TILES)]
    even = [tile_copy(even_ref, 0, i) for i in range(TILES)]
    for copy in (memory_copy, *odd):
        copy.start()
    memory_copy.wait()
    for i, copy in enumerate(odd):
        copy.wait()
        even[i].start()
        at = slice(i * tile, (i + 1) * tile)
        product = jnp.dot(lhs_ref[...], odd_ref[:, at], preferred_element_type=f32)
        turned_ref[at, :] = product.T.astype(bf16)
    store_shares(place_ref, turned_ref, out_refs)
    for copy in even:
        copy.wait()


def first_product(place, memory, resident):
    _, rows, depth = memory.shape
    cols = resident.shape[1]
    width = cols // 8
    outs = [((width, rows), 4), ((rows, depth), 1), ((depth, cols // 2), 1)]
    shapes = [jax.ShapeDtypeStruct(shape, bf16) for shape, count in outs for _ in range(count)]
    *odd, lhs, even_resident = pl.pallas_call(
        first_product_kernel,
        in_specs=[SMEM] + [pl.BlockSpec(memory_space=pltpu.HBM)] * 2,
        out_specs=[VMEM] * 6,
        out_shape=shapes,
        scratch_shapes=[
            pltpu.VMEM((depth, cols // 2), bf16),
            pltpu.VMEM((cols // 2, rows), bf16),
            pltpu.SemaphoreType.DMA((2 * TILES + 1,)),
        ],
        compiler_params=params(12),
        cost_estimate=cost(rows * depth * cols, 4 * depth * cols),
        name="first_product",
    )(place, memory, resident)
    return odd, lhs, even_resident


def depth_half(place_ref, side, resident_ref):
    half = resident_ref.shape[0] // 2
    return pl.ds(pl.multiple_of((place_ref[C] ^ side) * half, half), half)


def early_product_kernel(place_ref, lhs_ref, resident_ref, out_ref):
    right = resident_ref[depth_half(place_ref, 0, resident_ref), :]
    out_ref[...] = jnp.dot(lhs_ref[...], right, preferred_element_type=f32)


def early_product(place, lhs, resident):
    rows, depth = lhs.shape
    cols = resident.shape[1]
    return pl.pallas_call(
        early_product_kernel,
        in_specs=[SMEM, VMEM, VMEM],
        out_specs=VMEM,
        out_shape=jax.ShapeDtypeStruct((rows, cols), f32),
        compiler_params=params(6),
        cost_estimate=cost(2 * rows * depth * cols, 4 * rows * cols),
        name="early_product",
    )(place, lhs, resident)


def late_product_kernel(place_ref, early_ref, lhs_ref, resident_ref, *refs):
    out_refs, turned_ref = refs[:4], refs[4]
    right = resident_ref[depth_half(place_ref, 1, resident_ref), :]
    product = early_ref[...] + jnp.dot(lhs_ref[...], right, preferred_element_type=f32)
    turned_ref[...] = product.T.astype(bf16)
    store_shares(place_ref, turned_ref, out_refs)


def both_product_kernel(place_ref, own_ref, other_ref, resident_ref, *refs):
    out_refs, turned_ref = refs[:4], refs[4]
    product = None
    for side, lhs_ref in enumerate((own_ref, other_ref)):
        right = resident_ref[depth_half(place_ref, side, resident_ref), :]
        term = jnp.dot(lhs_ref[...], right, preferred_element_type=f32)
        product = term if product is None else product + term
    turned_ref[...] = product.T.astype(bf16)
    store_shares(place_ref, turned_ref, out_refs)


def second_product(kernel, place, left, lhs, resident, name):
    rows, depth = lhs.shape
    cols = resident.shape[1]
    return pl.pallas_call(
        kernel,
        in_specs=[SMEM] + [VMEM] * 3,
        out_specs=[VMEM] * 4,
        out_shape=[jax.ShapeDtypeStruct((cols // 4, rows), bf16)] * 4,
        scratch_shapes=[pltpu.VMEM((cols, rows), bf16)],
        compiler_params=params(6),
        cost_estimate=cost(2 * rows * depth * cols, 4 * cols * rows),
        name=name,
    )(place, left, lhs, resident)


def half_copy(side, place_ref, resident_ref, out_ref, sem):
    half = out_ref.shape[1]
    at = pl.ds(pl.multiple_of(((place_ref[Y] & 1) ^ side) * half, half), half)
    return pltpu.make_async_copy(resident_ref.at[:, at], out_ref, sem)


def bring_odd_kernel(
    place_ref, memory_ref, previous_ref, resident_ref, memory_out, one_out, two_out, odd_out, prior_ref, turned_ref, sems
):
    width, rows = one_out.shape
    start = position(place_ref[Y]) * 2 * width
    cols = pl.ds(pl.multiple_of(start, 128), 2 * width)
    copies = [
        pltpu.make_async_copy(previous_ref.at[:, :, cols], prior_ref, sems.at[0]),
        pltpu.make_async_copy(memory_ref.at[1], memory_out, sems.at[1]),
        half_copy(1, place_ref, resident_ref, odd_out, sems.at[2]),
    ]
    for copy in copies:
        copy.start()
    copies[0].wait()
    for front, out_ref in enumerate((one_out, two_out)):
        turned_ref[...] = prior_ref[front].astype(f32).T
        share = turned_ref[pl.ds(pl.multiple_of(place_ref[ZL] * width, width), width), :]
        out_ref[...] = share.astype(bf16)
    for copy in copies[1:]:
        copy.wait()


def bring_odd(place, memory, previous, resident):
    _, rows, depth = memory.shape
    cols = resident.shape[1]
    width = previous.shape[2] // 8
    shapes = [(rows, depth), (width, rows), (width, rows), (depth, cols // 2)]
    return pl.pallas_call(
        bring_odd_kernel,
        in_specs=[SMEM] + [HBM] * 3,
        out_specs=[VMEM] * 4,
        out_shape=[jax.ShapeDtypeStruct(shape, bf16) for shape in shapes],
        scratch_shapes=[
            pltpu.VMEM((2, rows, 2 * width), bf16),
            pltpu.VMEM((2 * width, rows), f32),
            pltpu.SemaphoreType.DMA((3,)),
        ],
        compiler_params=params(6),
        cost_estimate=cost(0, depth * (2 * rows + cols)),
        name="bring_odd",
    )(place, memory, previous, resident)


def bring_even_kernel(place_ref, resident_ref, even_out, sem):
    copy = half_copy(0, place_ref, resident_ref, even_out, sem)
    copy.start()
    copy.wait()


def bring_even(place, resident):
    depth, cols = resident.shape
    return pl.pallas_call(
        bring_even_kernel,
        in_specs=[SMEM, HBM],
        out_specs=VMEM,
        out_shape=jax.ShapeDtypeStruct((depth, cols // 2), bf16),
        scratch_shapes=[pltpu.SemaphoreType.DMA],
        compiler_params=params(4),
        cost_estimate=cost(0, depth * cols),
        name="bring_even",
    )(place, resident)


def place_pair(own, other, first, out_ref):
    near, far = own.astype(f32), other.astype(f32)
    low = jnp.where(first == 0, near, far)
    high = jnp.where(first == 0, far, near)
    out_ref[...] = jnp.concatenate([low, high], axis=0).T.astype(bf16)


def next_memory_kernel(side, place_ref, memory_ref, *refs):
    near_refs, far_refs, out_ref = refs[:4], refs[4:8], refs[8]
    half = out_ref.shape[1]
    width = half // 4
    for dx in range(4):
        near, far = near_refs[dx][...].astype(f32), far_refs[dx ^ 2][...].astype(f32)
        start = position(((place_ref[X] - dx) & 3) ^ place_ref[Y]) * width
        low = jnp.where(place_ref[ZH] == 0, near, far)
        high = jnp.where(place_ref[ZH] == 0, far, near)
        pair = jnp.concatenate([low, high], axis=0).T
        at = pl.ds(pl.multiple_of((place_ref[C] ^ side) * half + start, 128), width)
        to = pl.ds(pl.multiple_of(start, 128), width)
        out_ref[:, to] = (memory_ref[:, at].astype(f32) + pair).astype(bf16)


def next_memory(side, place, memory, energies):
    rows, depth = memory.shape
    return pl.pallas_call(
        functools.partial(next_memory_kernel, side),
        in_specs=[SMEM] + [VMEM] * 9,
        out_specs=VMEM,
        out_shape=jax.ShapeDtypeStruct((rows, depth // 2), bf16),
        compiler_params=params(6),
        cost_estimate=cost(rows * depth, 3 * rows * depth),
        name="next_memory",
    )(place, memory, *energies)


def solve_into(part_refs, prior_ref, inverse_ref):
    summed = part_refs[0][...].astype(f32)
    for part_ref in part_refs[1:]:
        summed = summed + part_ref[...].astype(f32)
    source = prior_ref[...].astype(f32) - step_size * summed
    mixed = lax.dot_general(
        source,
        inverse_ref[...],
        (((1,), (1,)), ((), ())),
        precision=lax.Precision.HIGHEST,
        preferred_element_type=f32,
    )
    return (source + mixed).astype(bf16)


def flipped(values):
    rows, cols = values.shape
    strips = []
    pad = jnp.zeros((128 - ORB, 128), f32)
    for s in range(rows // ORB):
        pieces = []
        for q in range(cols // 128):
            block = values[s * ORB : (s + 1) * ORB, q * 128 : (q + 1) * 128]
            turned = jnp.concatenate([block, pad], axis=0).T
            piece = turned[:ORB]
            for t in range(1, 128 // ORB):
                piece = piece + pltpu.roll(turned[t * ORB : (t + 1) * ORB], t * ORB, 1)
            pieces.append(piece)
        strips.append(jnp.concatenate(pieces, axis=1))
    return jnp.concatenate(strips, axis=0)


def first_solve_kernel(place_ref, *refs):
    front_ref, energy_ref = refs[11:]
    front = solve_into(refs[:8], refs[8], refs[9])
    front_ref[...] = front
    values = front.astype(f32)
    mirror = flipped(values)
    rows, cols = values.shape
    coupling = jnp.tile(refs[10][...], (rows // ORB, cols // 128))
    energy_ref[...] = (mirror * mirror * values * coupling).astype(bf16)


def second_solve_kernel(place_ref, *refs):
    refs[10][...] = solve_into(refs[:8], refs[8], refs[9])


def solve(kernel, place, parts, prior, inverse, extra, outputs, name):
    width, rows = prior.shape
    return pl.pallas_call(
        kernel,
        in_specs=[SMEM] + [VMEM] * (len(parts) + 2 + len(extra)),
        out_specs=[VMEM] * outputs,
        out_shape=[jax.ShapeDtypeStruct((width, rows), bf16)] * outputs,
        compiler_params=params(8),
        cost_estimate=cost(12 * rows * rows * width, 24 * rows * width),
        name=name,
    )(place, *parts, prior, inverse, *extra)


def put_blocks(blocks, block_ref, sems, out_ref, front):
    width = block_ref.shape[2]
    copies = []
    for i, (start, write) in enumerate(blocks):
        write(block_ref.at[i])
        at = pl.ds(pl.multiple_of(start, 128), width)
        copies.append(pltpu.make_async_copy(block_ref.at[i], out_ref.at[front, :, at], sems.at[i]))
        copies[i].start()
    for copy in copies:
        copy.wait()


def join_one_kernel(place_ref, own_ref, other_ref, out_ref, block_ref, sems):
    def block(dy):
        def write(ref):
            place_pair(own_ref[dy], other_ref[dy], place_ref[ZL], ref)

        return position((place_ref[Y] - dy) & 3) * block_ref.shape[2], write

    put_blocks([block(dy) for dy in range(4)], block_ref, sems, out_ref, 0)


def join_two_kernel(place_ref, *refs):
    own_refs, twin_refs, (out_ref, block_ref, sems) = refs[:4], refs[4:8], refs[9:]

    def block(dy):
        def write(ref):
            place_pair(own_refs[dy][...], twin_refs[dy][...], place_ref[ZL], ref)

        return position((place_ref[Y] - dy) & 3) * block_ref.shape[2], write

    put_blocks([block(dy) for dy in range(4)], block_ref, sems, out_ref, 1)


def join(kernel, args, in_specs, shape, aliases, name):
    _, rows, cols = shape
    return pl.pallas_call(
        kernel,
        in_specs=in_specs,
        out_specs=HBM,
        out_shape=jax.ShapeDtypeStruct(shape, bf16),
        scratch_shapes=[pltpu.VMEM((4, rows, cols // 4), bf16), pltpu.SemaphoreType.DMA((4,))],
        input_output_aliases=aliases,
        compiler_params=params(6),
        cost_estimate=cost(rows * cols, 4 * rows * cols),
        name=name,
    )(*args)


def move(value, target):
    pairs = []
    for i in range(128):
        rest, c = divmod(i, 2)
        rest, zh = divmod(rest, 2)
        rest, x = divmod(rest, 4)
        y, zl = divmod(rest, 2)
        y, zl, x, zh = target(y, zl, x, zh)
        pairs.append((i, (((y * 2 + zl) * 4 + x) * 2 + zh) * 2 + c))
    return lax.ppermute(value, ALL, pairs)


def turn(flip):
    return lambda y, zl, x, zh: (x, zh, x ^ y ^ (2 * flip), zl ^ flip)


def scatter(shares, first):
    parts = []
    for k in (3, 2, 1, 0) if first == 0 else (1, 0, 3, 2):
        dy, dz = first + 2 * (k >> 1), k & 1
        if (dy, dz) == (0, 0):
            parts.append(shares[k])
        else:
            parts.append(move(shares[k], lambda y, zl, x, zh: (y ^ dy, zl ^ dz, x, zh)))
    return parts


def spread(pair, axis):
    pairs = {0: pair}
    for d in (2, 1, 3):
        pairs[d] = lax.ppermute(pair, axis, [(i, (i + d) % 4) for i in range(4)])
    return [pairs[d] for d in range(4)]


def relayed(value, onward):
    step = lambda value, d: lax.ppermute(value, "x", [(i, (i + d) % 4) for i in range(4)])
    values = {0: value, 1: step(value, 1), 3: step(value, 3)}
    values[2] = step(values[onward], onward)
    return [values[d] for d in range(4)]


def per_device(resident, memory, previous, inverse_part, pair_coupling):
    place = jnp.stack([lax.axis_index(name) for name in ("x", "zh", "c", "y", "zl")]).astype(jnp.int32)
    coupling = jnp.tile(pair_coupling, (1, 128 // ORB))

    resident, memory, previous = in_hbm(resident), in_hbm(memory), in_hbm(previous)
    odd, lhs, even_resident = first_product(place, memory, resident)
    odd_parts = scatter(odd, 1)
    lhs, odd = lax.optimization_barrier((lhs, odd))
    even = half_product(place, lhs, even_resident)
    even_parts = scatter(even, 0)
    place, _, odd_parts = lax.optimization_barrier((place, even[0], odd_parts))
    memory, prior_one, prior_two, odd_resident = bring_odd(place, memory, previous, resident)
    parts = odd_parts + even_parts
    front_one, energy = solve(
        first_solve_kernel, place, parts, prior_one, inverse_part[0], [coupling], 2, "first_solve"
    )
    near, far = move(energy, turn(0)), move(energy, turn(1))
    ones = spread(front_one, "y")
    later, _ = lax.optimization_barrier((place, energy))
    even_resident = bring_even(later, resident)
    near, far, ones, even_resident = lax.optimization_barrier((near, far, ones, even_resident))
    near, far = relayed(near, 1), relayed(far, 3)
    own = near + far
    gated = lax.optimization_barrier((near[0], far[0], jnp.stack(ones), near[1], far[3]))
    near[0], far[0], ones, near[1], far[3] = gated
    others = lax.ppermute(ones, "zl", SWAP)
    other = [lax.ppermute(value, "c", SWAP) for value in near + far]
    own_lhs = next_memory(0, place, memory, own)
    early = early_product(place, own_lhs, odd_resident)
    other, others, early = lax.optimization_barrier((other, others, early))
    other_lhs = next_memory(1, place, memory, other)
    odd = second_product(late_product_kernel, place, early, other_lhs, odd_resident, "late_product")
    own_lhs, odd = lax.optimization_barrier((own_lhs, odd))
    even = second_product(both_product_kernel, place, own_lhs, other_lhs, even_resident, "both_product")
    parts = scatter(odd, 1) + scatter(even, 0)
    (front_two,) = solve(
        second_solve_kernel, place, parts, prior_two, inverse_part[1], [], 1, "second_solve"
    )
    twin = lax.ppermute(front_two, "zl", SWAP)
    chunks = [*spread(front_two, "y"), *spread(twin, "y")]
    fronts = join(join_one_kernel, (place, ones, others), [SMEM, VMEM, VMEM], previous.shape, {}, "join_one")
    return join(
        join_two_kernel, (place, *chunks, fronts), [SMEM] + [VMEM] * 8 + [HBM], previous.shape, {9: 0}, "join_two"
    )


def solution(mesh):
    fine = Mesh(mesh.devices.reshape(4, 2, 4, 2, 2), ALL)
    in_specs = (P(PASTS, SECONDS), P(None, None, PASTS), P(None, None, SECONDS), P(), P())
    out_specs = P(None, None, SECONDS)
    return jax.shard_map(
        per_device, mesh=fine, in_specs=in_specs, out_specs=out_specs, check_vma=False
    )
```

```python
import functools

import jax
import jax.numpy as jnp
from jax import lax
from jax.experimental import pallas as pl
from jax.experimental.pallas import tpu as pltpu
from jax.sharding import Mesh, PartitionSpec as P

step_size = 0.5
ORB = 32
f32 = jnp.float32
bf16 = jnp.bfloat16
PASTS = ("y", "zl")
SECONDS = ("x", "zh", "c")
ALL = PASTS + SECONDS
SWAP = [(0, 1), (1, 0)]
X, ZH, C, Y, ZL = range(5)


VMEM = pl.BlockSpec(memory_space=pltpu.VMEM)
SMEM = pl.BlockSpec(memory_space=pltpu.SMEM)
HBM = pl.BlockSpec(memory_space=pltpu.HBM)


def in_hbm(array):
    return pltpu.with_memory_space_constraint(array, pltpu.HBM)


def params(megabytes):
    return pltpu.CompilerParams(vmem_limit_bytes=megabytes << 20)


def cost(flops, nbytes):
    return pl.CostEstimate(flops=flops, bytes_accessed=nbytes, transcendentals=0)


def position(y):
    return (y & 1) * 2 + (y >> 1)


def store_shares(place_ref, turned_ref, out_refs):
    width = out_refs[0].shape[0]
    for k, out_ref in enumerate(out_refs):
        share = ((place_ref[Y] >> 1) ^ (k >> 1)) * 2 + (place_ref[ZL] ^ (k & 1))
        out_ref[...] = turned_ref[pl.ds(pl.multiple_of(share * width, width), width), :]


def half_product_kernel(place_ref, lhs_ref, resident_ref, *refs):
    out_refs, turned_ref = refs[:4], refs[4]
    product = jnp.dot(lhs_ref[...], resident_ref[...], preferred_element_type=f32)
    turned_ref[...] = product.T.astype(bf16)
    store_shares(place_ref, turned_ref, out_refs)


def half_product(place, lhs, resident):
    rows, depth = lhs.shape
    cols = resident.shape[1]
    width = cols // 4
    return pl.pallas_call(
        half_product_kernel,
        in_specs=[SMEM, VMEM, VMEM],
        out_specs=[VMEM] * 4,
        out_shape=[jax.ShapeDtypeStruct((width, rows), bf16)] * 4,
        scratch_shapes=[pltpu.VMEM((cols, rows), bf16)],
        compiler_params=params(6),
        cost_estimate=cost(2 * rows * depth * cols, 4 * width * rows),
        name="half_product",
    )(place, lhs, resident)


TILES = 3


def first_product_kernel(place_ref, memory_ref, resident_ref, *refs):
    out_refs, lhs_ref, even_ref, odd_ref, turned_ref, sems = refs[:4], *refs[4:]
    depth, cols = odd_ref.shape
    tile = cols // TILES
    parity = place_ref[Y] & 1

    def tile_copy(half_ref, side, i):
        start = pl.multiple_of((parity ^ side) * cols + i * tile, tile)
        return pltpu.make_async_copy(
            resident_ref.at[:, pl.ds(start, tile)],
            half_ref.at[:, i * tile : (i + 1) * tile],
            sems.at[side * TILES + i],
        )

    memory_copy = pltpu.make_async_copy(memory_ref.at[0], lhs_ref, sems.at[2 * TILES])
    odd = [tile_copy(odd_ref, 1, i) for i in range(TILES)]
    even = [tile_copy(even_ref, 0, i) for i in range(TILES)]
    for copy in (memory_copy, *odd):
        copy.start()
    memory_copy.wait()
    for i, copy in enumerate(odd):
        copy.wait()
        even[i].start()
        at = slice(i * tile, (i + 1) * tile)
        product = jnp.dot(lhs_ref[...], odd_ref[:, at], preferred_element_type=f32)
        turned_ref[at, :] = product.T.astype(bf16)
    store_shares(place_ref, turned_ref, out_refs)
    for copy in even:
        copy.wait()


def first_product(place, memory, resident):
    _, rows, depth = memory.shape
    cols = resident.shape[1]
    width = cols // 8
    outs = [((width, rows), 4), ((rows, depth), 1), ((depth, cols // 2), 1)]
    shapes = [jax.ShapeDtypeStruct(shape, bf16) for shape, count in outs for _ in range(count)]
    *odd, lhs, even_resident = pl.pallas_call(
        first_product_kernel,
        in_specs=[SMEM] + [pl.BlockSpec(memory_space=pltpu.HBM)] * 2,
        out_specs=[VMEM] * 6,
        out_shape=shapes,
        scratch_shapes=[
            pltpu.VMEM((depth, cols // 2), bf16),
            pltpu.VMEM((cols // 2, rows), bf16),
            pltpu.SemaphoreType.DMA((2 * TILES + 1,)),
        ],
        compiler_params=params(12),
        cost_estimate=cost(rows * depth * cols, 4 * depth * cols),
        name="first_product",
    )(place, memory, resident)
    return odd, lhs, even_resident


def depth_half(place_ref, side, resident_ref):
    half = resident_ref.shape[0] // 2
    return pl.ds(pl.multiple_of((place_ref[C] ^ side) * half, half), half)


def early_product_kernel(place_ref, lhs_ref, resident_ref, out_ref):
    right = resident_ref[depth_half(place_ref, 0, resident_ref), :]
    out_ref[...] = jnp.dot(lhs_ref[...], right, preferred_element_type=f32)


def early_product(place, lhs, resident):
    rows, depth = lhs.shape
    cols = resident.shape[1]
    return pl.pallas_call(
        early_product_kernel,
        in_specs=[SMEM, VMEM, VMEM],
        out_specs=VMEM,
        out_shape=jax.ShapeDtypeStruct((rows, cols), f32),
        compiler_params=params(6),
        cost_estimate=cost(2 * rows * depth * cols, 4 * rows * cols),
        name="early_product",
    )(place, lhs, resident)


def late_product_kernel(place_ref, early_ref, lhs_ref, resident_ref, *refs):
    out_refs, turned_ref = refs[:4], refs[4]
    right = resident_ref[depth_half(place_ref, 1, resident_ref), :]
    product = early_ref[...] + jnp.dot(lhs_ref[...], right, preferred_element_type=f32)
    turned_ref[...] = product.T.astype(bf16)
    store_shares(place_ref, turned_ref, out_refs)


def both_product_kernel(place_ref, own_ref, other_ref, resident_ref, *refs):
    out_refs, turned_ref = refs[:4], refs[4]
    product = None
    for side, lhs_ref in enumerate((own_ref, other_ref)):
        right = resident_ref[depth_half(place_ref, side, resident_ref), :]
        term = jnp.dot(lhs_ref[...], right, preferred_element_type=f32)
        product = term if product is None else product + term
    turned_ref[...] = product.T.astype(bf16)
    store_shares(place_ref, turned_ref, out_refs)


def second_product(kernel, place, left, lhs, resident, name):
    rows, depth = lhs.shape
    cols = resident.shape[1]
    return pl.pallas_call(
        kernel,
        in_specs=[SMEM] + [VMEM] * 3,
        out_specs=[VMEM] * 4,
        out_shape=[jax.ShapeDtypeStruct((cols // 4, rows), bf16)] * 4,
        scratch_shapes=[pltpu.VMEM((cols, rows), bf16)],
        compiler_params=params(6),
        cost_estimate=cost(2 * rows * depth * cols, 4 * cols * rows),
        name=name,
    )(place, left, lhs, resident)


def half_copy(side, place_ref, resident_ref, out_ref, sem):
    half = out_ref.shape[1]
    at = pl.ds(pl.multiple_of(((place_ref[Y] & 1) ^ side) * half, half), half)
    return pltpu.make_async_copy(resident_ref.at[:, at], out_ref, sem)


def bring_odd_kernel(
    place_ref, memory_ref, previous_ref, resident_ref, memory_out, one_out, two_out, odd_out, prior_ref, turned_ref, sems
):
    width, rows = one_out.shape
    start = position(place_ref[Y]) * 2 * width
    cols = pl.ds(pl.multiple_of(start, 128), 2 * width)
    copies = [
        pltpu.make_async_copy(previous_ref.at[:, :, cols], prior_ref, sems.at[0]),
        pltpu.make_async_copy(memory_ref.at[1], memory_out, sems.at[1]),
        half_copy(1, place_ref, resident_ref, odd_out, sems.at[2]),
    ]
    for copy in copies:
        copy.start()
    copies[0].wait()
    for front, out_ref in enumerate((one_out, two_out)):
        turned_ref[...] = prior_ref[front].astype(f32).T
        share = turned_ref[pl.ds(pl.multiple_of(place_ref[ZL] * width, width), width), :]
        out_ref[...] = share.astype(bf16)
    for copy in copies[1:]:
        copy.wait()


def bring_odd(place, memory, previous, resident):
    _, rows, depth = memory.shape
    cols = resident.shape[1]
    width = previous.shape[2] // 8
    shapes = [(rows, depth), (width, rows), (width, rows), (depth, cols // 2)]
    return pl.pallas_call(
        bring_odd_kernel,
        in_specs=[SMEM] + [HBM] * 3,
        out_specs=[VMEM] * 4,
        out_shape=[jax.ShapeDtypeStruct(shape, bf16) for shape in shapes],
        scratch_shapes=[
            pltpu.VMEM((2, rows, 2 * width), bf16),
            pltpu.VMEM((2 * width, rows), f32),
            pltpu.SemaphoreType.DMA((3,)),
        ],
        compiler_params=params(6),
        cost_estimate=cost(0, depth * (2 * rows + cols)),
        name="bring_odd",
    )(place, memory, previous, resident)


def bring_even_kernel(place_ref, resident_ref, even_out, sem):
    copy = half_copy(0, place_ref, resident_ref, even_out, sem)
    copy.start()
    copy.wait()


def bring_even(place, resident):
    depth, cols = resident.shape
    return pl.pallas_call(
        bring_even_kernel,
        in_specs=[SMEM, HBM],
        out_specs=VMEM,
        out_shape=jax.ShapeDtypeStruct((depth, cols // 2), bf16),
        scratch_shapes=[pltpu.SemaphoreType.DMA],
        compiler_params=params(4),
        cost_estimate=cost(0, depth * cols),
        name="bring_even",
    )(place, resident)


def place_pair(own, other, first, out_ref):
    near, far = own.astype(f32), other.astype(f32)
    low = jnp.where(first == 0, near, far)
    high = jnp.where(first == 0, far, near)
    out_ref[...] = jnp.concatenate([low, high], axis=0).T.astype(bf16)


def next_memory_kernel(side, place_ref, memory_ref, *refs):
    pair_refs, out_ref = refs[:4], refs[4]
    half = out_ref.shape[1]
    width = half // 4
    for dx in range(4):
        near, far = pair_refs[dx][0].astype(f32), pair_refs[dx ^ 2][1].astype(f32)
        start = position(((place_ref[X] - dx) & 3) ^ place_ref[Y]) * width
        low = jnp.where(place_ref[ZH] == 0, near, far)
        high = jnp.where(place_ref[ZH] == 0, far, near)
        pair = jnp.concatenate([low, high], axis=0).T
        at = pl.ds(pl.multiple_of((place_ref[C] ^ side) * half + start, 128), width)
        to = pl.ds(pl.multiple_of(start, 128), width)
        out_ref[:, to] = (memory_ref[:, at].astype(f32) + pair).astype(bf16)


def next_memory(side, place, memory, pairs):
    rows, depth = memory.shape
    return pl.pallas_call(
        functools.partial(next_memory_kernel, side),
        in_specs=[SMEM] + [VMEM] * 5,
        out_specs=VMEM,
        out_shape=jax.ShapeDtypeStruct((rows, depth // 2), bf16),
        compiler_params=params(6),
        cost_estimate=cost(rows * depth, 3 * rows * depth),
        name="next_memory",
    )(place, memory, *pairs)


def solve_into(part_refs, prior_ref, inverse_ref):
    summed = part_refs[0][...].astype(f32)
    for part_ref in part_refs[1:]:
        summed = summed + part_ref[...].astype(f32)
    source = prior_ref[...].astype(f32) - step_size * summed
    mixed = lax.dot_general(
        source,
        inverse_ref[...],
        (((1,), (1,)), ((), ())),
        precision=lax.Precision.HIGHEST,
        preferred_element_type=f32,
    )
    return (source + mixed).astype(bf16)


def flipped(values):
    rows, cols = values.shape
    strips = []
    pad = jnp.zeros((128 - ORB, 128), f32)
    for s in range(rows // ORB):
        pieces = []
        for q in range(cols // 128):
            block = values[s * ORB : (s + 1) * ORB, q * 128 : (q + 1) * 128]
            turned = jnp.concatenate([block, pad], axis=0).T
            piece = turned[:ORB]
            for t in range(1, 128 // ORB):
                piece = piece + pltpu.roll(turned[t * ORB : (t + 1) * ORB], t * ORB, 1)
            pieces.append(piece)
        strips.append(jnp.concatenate(pieces, axis=1))
    return jnp.concatenate(strips, axis=0)


def first_solve_kernel(place_ref, *refs):
    front_ref, energy_ref = refs[11:]
    front = solve_into(refs[:8], refs[8], refs[9])
    front_ref[...] = front
    values = front.astype(f32)
    mirror = flipped(values)
    rows, cols = values.shape
    coupling = jnp.tile(refs[10][...], (rows // ORB, cols // 128))
    energy_ref[...] = (mirror * mirror * values * coupling).astype(bf16)


def second_solve_kernel(place_ref, *refs):
    refs[10][...] = solve_into(refs[:8], refs[8], refs[9])


def solve(kernel, place, parts, prior, inverse, extra, outputs, name):
    width, rows = prior.shape
    return pl.pallas_call(
        kernel,
        in_specs=[SMEM] + [VMEM] * (len(parts) + 2 + len(extra)),
        out_specs=[VMEM] * outputs,
        out_shape=[jax.ShapeDtypeStruct((width, rows), bf16)] * outputs,
        compiler_params=params(8),
        cost_estimate=cost(12 * rows * rows * width, 24 * rows * width),
        name=name,
    )(place, *parts, prior, inverse, *extra)


def put_blocks(blocks, block_ref, sems, out_ref, front):
    width = block_ref.shape[2]
    copies = []
    for i, (start, write) in enumerate(blocks):
        write(block_ref.at[i])
        at = pl.ds(pl.multiple_of(start, 128), width)
        copies.append(pltpu.make_async_copy(block_ref.at[i], out_ref.at[front, :, at], sems.at[i]))
        copies[i].start()
    for copy in copies:
        copy.wait()


def join_one_kernel(place_ref, own_ref, other_ref, out_ref, block_ref, sems):
    def block(dy):
        def write(ref):
            place_pair(own_ref[dy], other_ref[dy], place_ref[ZL], ref)

        return position((place_ref[Y] - dy) & 3) * block_ref.shape[2], write

    put_blocks([block(dy) for dy in range(4)], block_ref, sems, out_ref, 0)


def join_two_kernel(place_ref, *refs):
    own_refs, twin_refs, (out_ref, block_ref, sems) = refs[:4], refs[4:8], refs[9:]

    def block(dy):
        def write(ref):
            place_pair(own_refs[dy][...], twin_refs[dy][...], place_ref[ZL], ref)

        return position((place_ref[Y] - dy) & 3) * block_ref.shape[2], write

    put_blocks([block(dy) for dy in range(4)], block_ref, sems, out_ref, 1)


def join(kernel, args, in_specs, shape, aliases, name):
    _, rows, cols = shape
    return pl.pallas_call(
        kernel,
        in_specs=in_specs,
        out_specs=HBM,
        out_shape=jax.ShapeDtypeStruct(shape, bf16),
        scratch_shapes=[pltpu.VMEM((4, rows, cols // 4), bf16), pltpu.SemaphoreType.DMA((4,))],
        input_output_aliases=aliases,
        compiler_params=params(6),
        cost_estimate=cost(rows * cols, 4 * rows * cols),
        name=name,
    )(*args)


def move(value, target):
    pairs = []
    for i in range(128):
        rest, c = divmod(i, 2)
        rest, zh = divmod(rest, 2)
        rest, x = divmod(rest, 4)
        y, zl = divmod(rest, 2)
        y, zl, x, zh = target(y, zl, x, zh)
        pairs.append((i, (((y * 2 + zl) * 4 + x) * 2 + zh) * 2 + c))
    return lax.ppermute(value, ALL, pairs)


def turn(flip):
    return lambda y, zl, x, zh: (x, zh, x ^ y ^ (2 * flip), zl ^ flip)


def scatter(shares, first):
    parts = []
    for k in (3, 2, 1, 0) if first == 0 else (1, 0, 3, 2):
        dy, dz = first + 2 * (k >> 1), k & 1
        if (dy, dz) == (0, 0):
            parts.append(shares[k])
        else:
            parts.append(move(shares[k], lambda y, zl, x, zh: (y ^ dy, zl ^ dz, x, zh)))
    return parts


def spread(pair, axis):
    pairs = {0: pair}
    for d in (2, 1, 3):
        pairs[d] = lax.ppermute(pair, axis, [(i, (i + d) % 4) for i in range(4)])
    return [pairs[d] for d in range(4)]


def per_device(resident, memory, previous, inverse_part, pair_coupling):
    place = jnp.stack([lax.axis_index(name) for name in ("x", "zh", "c", "y", "zl")]).astype(jnp.int32)
    coupling = jnp.tile(pair_coupling, (1, 128 // ORB))

    resident, memory, previous = in_hbm(resident), in_hbm(memory), in_hbm(previous)
    odd, lhs, even_resident = first_product(place, memory, resident)
    odd_parts = scatter(odd, 1)
    lhs, odd = lax.optimization_barrier((lhs, odd))
    even = half_product(place, lhs, even_resident)
    even_parts = scatter(even, 0)
    place, _, odd_parts = lax.optimization_barrier((place, even[0], odd_parts))
    memory, prior_one, prior_two, odd_resident = bring_odd(place, memory, previous, resident)
    parts = odd_parts + even_parts
    front_one, energy = solve(
        first_solve_kernel, place, parts, prior_one, inverse_part[0], [coupling], 2, "first_solve"
    )
    pair = [move(energy, turn(0)), move(energy, turn(1))]
    ones = spread(front_one, "y")
    later, _ = lax.optimization_barrier((place, energy))
    even_resident = bring_even(later, resident)
    pair, even_resident = lax.optimization_barrier((pair, even_resident))
    own = spread(jnp.stack(pair), "x")
    ones = jnp.stack(ones)
    others = lax.ppermute(ones, "zl", SWAP)
    other = [lax.ppermute(pair, "c", SWAP) for pair in own]
    own_lhs = next_memory(0, place, memory, own)
    early = early_product(place, own_lhs, odd_resident)
    other, others, early = lax.optimization_barrier((other, others, early))
    other_lhs = next_memory(1, place, memory, other)
    odd = second_product(late_product_kernel, place, early, other_lhs, odd_resident, "late_product")
    own_lhs, odd = lax.optimization_barrier((own_lhs, odd))
    even = second_product(both_product_kernel, place, own_lhs, other_lhs, even_resident, "both_product")
    parts = scatter(odd, 1) + scatter(even, 0)
    (front_two,) = solve(
        second_solve_kernel, place, parts, prior_two, inverse_part[1], [], 1, "second_solve"
    )
    twin = lax.ppermute(front_two, "zl", SWAP)
    chunks = [*spread(front_two, "y"), *spread(twin, "y")]
    fronts = join(join_one_kernel, (place, ones, others), [SMEM, VMEM, VMEM], previous.shape, {}, "join_one")
    return join(
        join_two_kernel, (place, *chunks, fronts), [SMEM] + [VMEM] * 8 + [HBM], previous.shape, {9: 0}, "join_two"
    )


def solution(mesh):
    fine = Mesh(mesh.devices.reshape(4, 2, 4, 2, 2), ALL)
    in_specs = (P(PASTS, SECONDS), P(None, None, PASTS), P(None, None, SECONDS), P(), P())
    out_specs = P(None, None, SECONDS)
    return jax.shard_map(
        per_device, mesh=fine, in_specs=in_specs, out_specs=out_specs, check_vma=False
    )
```

```python
import functools

import jax
import jax.numpy as jnp
from jax import lax
from jax.experimental import pallas as pl
from jax.experimental.pallas import tpu as pltpu
from jax.sharding import Mesh, PartitionSpec as P

step_size = 0.5
ORB = 32
f32 = jnp.float32
bf16 = jnp.bfloat16
PASTS = ("y", "zl")
SECONDS = ("x", "zh", "c")
ALL = PASTS + SECONDS
SWAP = [(0, 1), (1, 0)]
X, ZH, C, Y, ZL = range(5)


VMEM = pl.BlockSpec(memory_space=pltpu.VMEM)
SMEM = pl.BlockSpec(memory_space=pltpu.SMEM)
HBM = pl.BlockSpec(memory_space=pltpu.HBM)


def in_hbm(array):
    return pltpu.with_memory_space_constraint(array, pltpu.HBM)


def params(megabytes):
    return pltpu.CompilerParams(vmem_limit_bytes=megabytes << 20)


def cost(flops, nbytes):
    return pl.CostEstimate(flops=flops, bytes_accessed=nbytes, transcendentals=0)


def position(y):
    return (y & 1) * 2 + (y >> 1)


def store_shares(place_ref, turned_ref, out_refs):
    width = out_refs[0].shape[0]
    for k, out_ref in enumerate(out_refs):
        share = ((place_ref[Y] >> 1) ^ (k >> 1)) * 2 + (place_ref[ZL] ^ (k & 1))
        out_ref[...] = turned_ref[pl.ds(pl.multiple_of(share * width, width), width), :]


def half_product_kernel(place_ref, lhs_ref, resident_ref, *refs):
    out_refs, turned_ref = refs[:4], refs[4]
    product = jnp.dot(lhs_ref[...], resident_ref[...], preferred_element_type=f32)
    turned_ref[...] = product.T.astype(bf16)
    store_shares(place_ref, turned_ref, out_refs)


def half_product(place, lhs, resident):
    rows, depth = lhs.shape
    cols = resident.shape[1]
    width = cols // 4
    return pl.pallas_call(
        half_product_kernel,
        in_specs=[SMEM, VMEM, VMEM],
        out_specs=[VMEM] * 4,
        out_shape=[jax.ShapeDtypeStruct((width, rows), bf16)] * 4,
        scratch_shapes=[pltpu.VMEM((cols, rows), bf16)],
        compiler_params=params(6),
        cost_estimate=cost(2 * rows * depth * cols, 4 * width * rows),
        name="half_product",
    )(place, lhs, resident)


TILES = 3


def first_product_kernel(place_ref, memory_ref, resident_ref, *refs):
    out_refs, lhs_ref, even_ref, odd_ref, turned_ref, sems = refs[:4], *refs[4:]
    depth, cols = odd_ref.shape
    tile = cols // TILES
    parity = place_ref[Y] & 1

    def tile_copy(half_ref, side, i):
        start = pl.multiple_of((parity ^ side) * cols + i * tile, tile)
        return pltpu.make_async_copy(
            resident_ref.at[:, pl.ds(start, tile)],
            half_ref.at[:, i * tile : (i + 1) * tile],
            sems.at[side * TILES + i],
        )

    memory_copy = pltpu.make_async_copy(memory_ref.at[0], lhs_ref, sems.at[2 * TILES])
    odd = [tile_copy(odd_ref, 1, i) for i in range(TILES)]
    even = [tile_copy(even_ref, 0, i) for i in range(TILES)]
    for copy in (memory_copy, *odd):
        copy.start()
    memory_copy.wait()
    for i, copy in enumerate(odd):
        copy.wait()
        even[i].start()
        at = slice(i * tile, (i + 1) * tile)
        product = jnp.dot(lhs_ref[...], odd_ref[:, at], preferred_element_type=f32)
        turned_ref[at, :] = product.T.astype(bf16)
    store_shares(place_ref, turned_ref, out_refs)
    for copy in even:
        copy.wait()


def first_product(place, memory, resident):
    _, rows, depth = memory.shape
    cols = resident.shape[1]
    width = cols // 8
    outs = [((width, rows), 4), ((rows, depth), 1), ((depth, cols // 2), 1)]
    shapes = [jax.ShapeDtypeStruct(shape, bf16) for shape, count in outs for _ in range(count)]
    *odd, lhs, even_resident = pl.pallas_call(
        first_product_kernel,
        in_specs=[SMEM] + [pl.BlockSpec(memory_space=pltpu.HBM)] * 2,
        out_specs=[VMEM] * 6,
        out_shape=shapes,
        scratch_shapes=[
            pltpu.VMEM((depth, cols // 2), bf16),
            pltpu.VMEM((cols // 2, rows), bf16),
            pltpu.SemaphoreType.DMA((2 * TILES + 1,)),
        ],
        compiler_params=params(12),
        cost_estimate=cost(rows * depth * cols, 4 * depth * cols),
        name="first_product",
    )(place, memory, resident)
    return odd, lhs, even_resident


def depth_half(place_ref, side, resident_ref):
    half = resident_ref.shape[0] // 2
    return pl.ds(pl.multiple_of((place_ref[C] ^ side) * half, half), half)


def early_product_kernel(place_ref, lhs_ref, resident_ref, out_ref):
    right = resident_ref[depth_half(place_ref, 0, resident_ref), :]
    out_ref[...] = jnp.dot(lhs_ref[...], right, preferred_element_type=f32)


def early_product(place, lhs, resident):
    rows, depth = lhs.shape
    cols = resident.shape[1]
    return pl.pallas_call(
        early_product_kernel,
        in_specs=[SMEM, VMEM, VMEM],
        out_specs=VMEM,
        out_shape=jax.ShapeDtypeStruct((rows, cols), f32),
        compiler_params=params(6),
        cost_estimate=cost(2 * rows * depth * cols, 4 * rows * cols),
        name="early_product",
    )(place, lhs, resident)


def late_product_kernel(place_ref, early_ref, lhs_ref, resident_ref, *refs):
    out_refs, turned_ref = refs[:4], refs[4]
    right = resident_ref[depth_half(place_ref, 1, resident_ref), :]
    product = early_ref[...] + jnp.dot(lhs_ref[...], right, preferred_element_type=f32)
    turned_ref[...] = product.T.astype(bf16)
    store_shares(place_ref, turned_ref, out_refs)


def both_product_kernel(place_ref, own_ref, other_ref, resident_ref, *refs):
    out_refs, turned_ref = refs[:4], refs[4]
    product = None
    for side, lhs_ref in enumerate((own_ref, other_ref)):
        right = resident_ref[depth_half(place_ref, side, resident_ref), :]
        term = jnp.dot(lhs_ref[...], right, preferred_element_type=f32)
        product = term if product is None else product + term
    turned_ref[...] = product.T.astype(bf16)
    store_shares(place_ref, turned_ref, out_refs)


def second_product(kernel, place, left, lhs, resident, name):
    rows, depth = lhs.shape
    cols = resident.shape[1]
    return pl.pallas_call(
        kernel,
        in_specs=[SMEM] + [VMEM] * 3,
        out_specs=[VMEM] * 4,
        out_shape=[jax.ShapeDtypeStruct((cols // 4, rows), bf16)] * 4,
        scratch_shapes=[pltpu.VMEM((cols, rows), bf16)],
        compiler_params=params(6),
        cost_estimate=cost(2 * rows * depth * cols, 4 * cols * rows),
        name=name,
    )(place, left, lhs, resident)


def half_copy(side, place_ref, resident_ref, out_ref, sem):
    half = out_ref.shape[1]
    at = pl.ds(pl.multiple_of(((place_ref[Y] & 1) ^ side) * half, half), half)
    return pltpu.make_async_copy(resident_ref.at[:, at], out_ref, sem)


def bring_odd_kernel(
    place_ref, memory_ref, previous_ref, resident_ref, memory_out, one_out, two_out, odd_out, prior_ref, turned_ref, sems
):
    width, rows = one_out.shape
    start = position(place_ref[Y]) * 2 * width
    cols = pl.ds(pl.multiple_of(start, 128), 2 * width)
    copies = [
        pltpu.make_async_copy(previous_ref.at[:, :, cols], prior_ref, sems.at[0]),
        pltpu.make_async_copy(memory_ref.at[1], memory_out, sems.at[1]),
        half_copy(1, place_ref, resident_ref, odd_out, sems.at[2]),
    ]
    for copy in copies:
        copy.start()
    copies[0].wait()
    for front, out_ref in enumerate((one_out, two_out)):
        turned_ref[...] = prior_ref[front].astype(f32).T
        share = turned_ref[pl.ds(pl.multiple_of(place_ref[ZL] * width, width), width), :]
        out_ref[...] = share.astype(bf16)
    for copy in copies[1:]:
        copy.wait()


def bring_odd(place, memory, previous, resident):
    _, rows, depth = memory.shape
    cols = resident.shape[1]
    width = previous.shape[2] // 8
    shapes = [(rows, depth), (width, rows), (width, rows), (depth, cols // 2)]
    return pl.pallas_call(
        bring_odd_kernel,
        in_specs=[SMEM] + [HBM] * 3,
        out_specs=[VMEM] * 4,
        out_shape=[jax.ShapeDtypeStruct(shape, bf16) for shape in shapes],
        scratch_shapes=[
            pltpu.VMEM((2, rows, 2 * width), bf16),
            pltpu.VMEM((2 * width, rows), f32),
            pltpu.SemaphoreType.DMA((3,)),
        ],
        compiler_params=params(6),
        cost_estimate=cost(0, depth * (2 * rows + cols)),
        name="bring_odd",
    )(place, memory, previous, resident)


def bring_even_kernel(place_ref, resident_ref, even_out, sem):
    copy = half_copy(0, place_ref, resident_ref, even_out, sem)
    copy.start()
    copy.wait()


def bring_even(place, resident):
    depth, cols = resident.shape
    return pl.pallas_call(
        bring_even_kernel,
        in_specs=[SMEM, HBM],
        out_specs=VMEM,
        out_shape=jax.ShapeDtypeStruct((depth, cols // 2), bf16),
        scratch_shapes=[pltpu.SemaphoreType.DMA],
        compiler_params=params(4),
        cost_estimate=cost(0, depth * cols),
        name="bring_even",
    )(place, resident)


def place_pair(own, other, first, out_ref):
    near, far = own.astype(f32), other.astype(f32)
    low = jnp.where(first == 0, near, far)
    high = jnp.where(first == 0, far, near)
    out_ref[...] = jnp.concatenate([low, high], axis=0).T.astype(bf16)


def next_memory_kernel(side, place_ref, memory_ref, *refs):
    pair_refs, out_ref = refs[:4], refs[4]
    half = out_ref.shape[1]
    width = half // 4
    for dx in range(4):
        near, far = pair_refs[dx][0].astype(f32), pair_refs[dx ^ 2][1].astype(f32)
        start = position(((place_ref[X] - dx) & 3) ^ place_ref[Y]) * width
        low = jnp.where(place_ref[ZH] == 0, near, far)
        high = jnp.where(place_ref[ZH] == 0, far, near)
        pair = jnp.concatenate([low, high], axis=0).T
        at = pl.ds(pl.multiple_of((place_ref[C] ^ side) * half + start, 128), width)
        to = pl.ds(pl.multiple_of(start, 128), width)
        out_ref[:, to] = (memory_ref[:, at].astype(f32) + pair).astype(bf16)


def next_memory(side, place, memory, pairs):
    rows, depth = memory.shape
    return pl.pallas_call(
        functools.partial(next_memory_kernel, side),
        in_specs=[SMEM] + [VMEM] * 5,
        out_specs=VMEM,
        out_shape=jax.ShapeDtypeStruct((rows, depth // 2), bf16),
        compiler_params=params(6),
        cost_estimate=cost(rows * depth, 3 * rows * depth),
        name="next_memory",
    )(place, memory, *pairs)


def solve_into(part_refs, prior_ref, inverse_ref):
    summed = part_refs[0][...].astype(f32)
    for part_ref in part_refs[1:]:
        summed = summed + part_ref[...].astype(f32)
    source = prior_ref[...].astype(f32) - step_size * summed
    mixed = lax.dot_general(
        source,
        inverse_ref[...],
        (((1,), (1,)), ((), ())),
        precision=lax.Precision.HIGHEST,
        preferred_element_type=f32,
    )
    return (source + mixed).astype(bf16)


def flipped(values):
    rows, cols = values.shape
    strips = []
    pad = jnp.zeros((128 - ORB, 128), f32)
    for s in range(rows // ORB):
        pieces = []
        for q in range(cols // 128):
            block = values[s * ORB : (s + 1) * ORB, q * 128 : (q + 1) * 128]
            turned = jnp.concatenate([block, pad], axis=0).T
            piece = turned[:ORB]
            for t in range(1, 128 // ORB):
                piece = piece + pltpu.roll(turned[t * ORB : (t + 1) * ORB], t * ORB, 1)
            pieces.append(piece)
        strips.append(jnp.concatenate(pieces, axis=1))
    return jnp.concatenate(strips, axis=0)


def first_solve_kernel(place_ref, *refs):
    front_ref, energy_ref = refs[11:]
    front = solve_into(refs[:8], refs[8], refs[9])
    front_ref[...] = front
    values = front.astype(f32)
    mirror = flipped(values)
    rows, cols = values.shape
    coupling = jnp.tile(refs[10][...], (rows // ORB, cols // 128))
    energy_ref[...] = (mirror * mirror * values * coupling).astype(bf16)


def second_solve_kernel(place_ref, *refs):
    refs[10][...] = solve_into(refs[:8], refs[8], refs[9])


def solve(kernel, place, parts, prior, inverse, extra, outputs, name):
    width, rows = prior.shape
    return pl.pallas_call(
        kernel,
        in_specs=[SMEM] + [VMEM] * (len(parts) + 2 + len(extra)),
        out_specs=[VMEM] * outputs,
        out_shape=[jax.ShapeDtypeStruct((width, rows), bf16)] * outputs,
        compiler_params=params(8),
        cost_estimate=cost(12 * rows * rows * width, 24 * rows * width),
        name=name,
    )(place, *parts, prior, inverse, *extra)


def put_blocks(blocks, block_ref, sems, out_ref, front):
    width = block_ref.shape[2]
    copies = []
    for i, (start, write) in enumerate(blocks):
        write(block_ref.at[i])
        at = pl.ds(pl.multiple_of(start, 128), width)
        copies.append(pltpu.make_async_copy(block_ref.at[i], out_ref.at[front, :, at], sems.at[i]))
        copies[i].start()
    for copy in copies:
        copy.wait()


def join_one_kernel(place_ref, own_ref, other_ref, out_ref, block_ref, sems):
    def block(dy):
        def write(ref):
            place_pair(own_ref[dy], other_ref[dy], place_ref[ZL], ref)

        return position((place_ref[Y] - dy) & 3) * block_ref.shape[2], write

    put_blocks([block(dy) for dy in range(4)], block_ref, sems, out_ref, 0)


def join_two_kernel(place_ref, *refs):
    own_refs, twin_refs, (out_ref, block_ref, sems) = refs[:4], refs[4:8], refs[9:]

    def block(dy):
        def write(ref):
            place_pair(own_refs[dy][...], twin_refs[dy][...], place_ref[ZL], ref)

        return position((place_ref[Y] - dy) & 3) * block_ref.shape[2], write

    put_blocks([block(dy) for dy in range(4)], block_ref, sems, out_ref, 1)


def join(kernel, args, in_specs, shape, aliases, name):
    _, rows, cols = shape
    return pl.pallas_call(
        kernel,
        in_specs=in_specs,
        out_specs=HBM,
        out_shape=jax.ShapeDtypeStruct(shape, bf16),
        scratch_shapes=[pltpu.VMEM((4, rows, cols // 4), bf16), pltpu.SemaphoreType.DMA((4,))],
        input_output_aliases=aliases,
        compiler_params=params(6),
        cost_estimate=cost(rows * cols, 4 * rows * cols),
        name=name,
    )(*args)


def move(value, target):
    pairs = []
    for i in range(128):
        rest, c = divmod(i, 2)
        rest, zh = divmod(rest, 2)
        rest, x = divmod(rest, 4)
        y, zl = divmod(rest, 2)
        y, zl, x, zh = target(y, zl, x, zh)
        pairs.append((i, (((y * 2 + zl) * 4 + x) * 2 + zh) * 2 + c))
    return lax.ppermute(value, ALL, pairs)


def turn(flip):
    return lambda y, zl, x, zh: (x, zh, x ^ y ^ (2 * flip), zl ^ flip)


def scatter(shares, first):
    parts = []
    for k in (3, 2, 1, 0) if first == 0 else (1, 0, 3, 2):
        dy, dz = first + 2 * (k >> 1), k & 1
        if (dy, dz) == (0, 0):
            parts.append(shares[k])
        else:
            parts.append(move(shares[k], lambda y, zl, x, zh: (y ^ dy, zl ^ dz, x, zh)))
    return parts


def spread(pair, axis):
    pairs = {0: pair}
    for d in (2, 1, 3):
        pairs[d] = lax.ppermute(pair, axis, [(i, (i + d) % 4) for i in range(4)])
    return [pairs[d] for d in range(4)]


def per_device(resident, memory, previous, inverse_part, pair_coupling):
    place = jnp.stack([lax.axis_index(name) for name in ("x", "zh", "c", "y", "zl")]).astype(jnp.int32)
    coupling = jnp.tile(pair_coupling, (1, 128 // ORB))

    resident, memory, previous = in_hbm(resident), in_hbm(memory), in_hbm(previous)
    odd, lhs, even_resident = first_product(place, memory, resident)
    odd_parts = scatter(odd, 1)
    lhs, odd = lax.optimization_barrier((lhs, odd))
    even = half_product(place, lhs, even_resident)
    even_parts = scatter(even, 0)
    place, _, odd_parts = lax.optimization_barrier((place, even[0], odd_parts))
    memory, prior_one, prior_two, odd_resident = bring_odd(place, memory, previous, resident)
    parts = odd_parts + even_parts
    front_one, energy = solve(
        first_solve_kernel, place, parts, prior_one, inverse_part[0], [coupling], 2, "first_solve"
    )
    pair = [move(energy, turn(0)), move(energy, turn(1))]
    ones = spread(front_one, "y")
    later, _ = lax.optimization_barrier((place, energy))
    even_resident = bring_even(later, resident)
    pair, even_resident = lax.optimization_barrier((pair, even_resident))
    own = spread(jnp.stack(pair), "x")
    ones = jnp.stack(ones)
    others = lax.ppermute(ones, "zl", SWAP)
    other = [lax.ppermute(pair, "c", SWAP) for pair in own]
    own_lhs = next_memory(0, place, memory, own)
    early = early_product(place, own_lhs, odd_resident)
    other, early = lax.optimization_barrier((other, early))
    other_lhs = next_memory(1, place, memory, other)
    odd = second_product(late_product_kernel, place, early, other_lhs, odd_resident, "late_product")
    own_lhs, odd, others = lax.optimization_barrier((own_lhs, odd, others))
    even = second_product(both_product_kernel, place, own_lhs, other_lhs, even_resident, "both_product")
    parts = scatter(odd, 1) + scatter(even, 0)
    (front_two,) = solve(
        second_solve_kernel, place, parts, prior_two, inverse_part[1], [], 1, "second_solve"
    )
    twin = lax.ppermute(front_two, "zl", SWAP)
    chunks = [*spread(front_two, "y"), *spread(twin, "y")]
    fronts = join(join_one_kernel, (place, ones, others), [SMEM, VMEM, VMEM], previous.shape, {}, "join_one")
    return join(
        join_two_kernel, (place, *chunks, fronts), [SMEM] + [VMEM] * 8 + [HBM], previous.shape, {9: 0}, "join_two"
    )


def solution(mesh):
    fine = Mesh(mesh.devices.reshape(4, 2, 4, 2, 2), ALL)
    in_specs = (P(PASTS, SECONDS), P(None, None, PASTS), P(None, None, SECONDS), P(), P())
    out_specs = P(None, None, SECONDS)
    return jax.shard_map(
        per_device, mesh=fine, in_specs=in_specs, out_specs=out_specs, check_vma=False
    )
```

```python
import functools

import jax
import jax.numpy as jnp
from jax import lax
from jax.experimental import pallas as pl
from jax.experimental.pallas import tpu as pltpu
from jax.sharding import Mesh, PartitionSpec as P

step_size = 0.5
ORB = 32
f32 = jnp.float32
bf16 = jnp.bfloat16
PASTS = ("y", "zl")
SECONDS = ("x", "zh", "c")
ALL = PASTS + SECONDS
SWAP = [(0, 1), (1, 0)]
X, ZH, C, Y, ZL = range(5)


VMEM = pl.BlockSpec(memory_space=pltpu.VMEM)
SMEM = pl.BlockSpec(memory_space=pltpu.SMEM)
HBM = pl.BlockSpec(memory_space=pltpu.HBM)


def in_hbm(array):
    return pltpu.with_memory_space_constraint(array, pltpu.HBM)


def params(megabytes):
    return pltpu.CompilerParams(vmem_limit_bytes=megabytes << 20)


def cost(flops, nbytes):
    return pl.CostEstimate(flops=flops, bytes_accessed=nbytes, transcendentals=0)


def position(y):
    return (y & 1) * 2 + (y >> 1)


def store_shares(place_ref, turned_ref, out_refs):
    width = out_refs[0].shape[0]
    for k, out_ref in enumerate(out_refs):
        share = ((place_ref[Y] >> 1) ^ (k >> 1)) * 2 + (place_ref[ZL] ^ (k & 1))
        out_ref[...] = turned_ref[pl.ds(pl.multiple_of(share * width, width), width), :]


def half_product_kernel(place_ref, lhs_ref, resident_ref, *refs):
    out_refs, turned_ref = refs[:4], refs[4]
    product = jnp.dot(lhs_ref[...], resident_ref[...], preferred_element_type=f32)
    turned_ref[...] = product.T.astype(bf16)
    store_shares(place_ref, turned_ref, out_refs)


def half_product(place, lhs, resident):
    rows, depth = lhs.shape
    cols = resident.shape[1]
    width = cols // 4
    return pl.pallas_call(
        half_product_kernel,
        in_specs=[SMEM, VMEM, VMEM],
        out_specs=[VMEM] * 4,
        out_shape=[jax.ShapeDtypeStruct((width, rows), bf16)] * 4,
        scratch_shapes=[pltpu.VMEM((cols, rows), bf16)],
        compiler_params=params(6),
        cost_estimate=cost(2 * rows * depth * cols, 4 * width * rows),
        name="half_product",
    )(place, lhs, resident)


TILES = 3


def first_product_kernel(place_ref, memory_ref, resident_ref, *refs):
    out_refs, lhs_ref, even_ref, odd_ref, turned_ref, sems = refs[:4], *refs[4:]
    depth, cols = odd_ref.shape
    tile = cols // TILES
    parity = place_ref[Y] & 1

    def tile_copy(half_ref, side, i):
        start = pl.multiple_of((parity ^ side) * cols + i * tile, tile)
        return pltpu.make_async_copy(
            resident_ref.at[:, pl.ds(start, tile)],
            half_ref.at[:, i * tile : (i + 1) * tile],
            sems.at[side * TILES + i],
        )

    memory_copy = pltpu.make_async_copy(memory_ref.at[0], lhs_ref, sems.at[2 * TILES])
    odd = [tile_copy(odd_ref, 1, i) for i in range(TILES)]
    even = [tile_copy(even_ref, 0, i) for i in range(TILES)]
    for copy in (memory_copy, *odd):
        copy.start()
    memory_copy.wait()
    for i, copy in enumerate(odd):
        copy.wait()
        even[i].start()
        at = slice(i * tile, (i + 1) * tile)
        product = jnp.dot(lhs_ref[...], odd_ref[:, at], preferred_element_type=f32)
        turned_ref[at, :] = product.T.astype(bf16)
    store_shares(place_ref, turned_ref, out_refs)
    for copy in even:
        copy.wait()


def first_product(place, memory, resident):
    _, rows, depth = memory.shape
    cols = resident.shape[1]
    width = cols // 8
    outs = [((width, rows), 4), ((rows, depth), 1), ((depth, cols // 2), 1)]
    shapes = [jax.ShapeDtypeStruct(shape, bf16) for shape, count in outs for _ in range(count)]
    *odd, lhs, even_resident = pl.pallas_call(
        first_product_kernel,
        in_specs=[SMEM] + [pl.BlockSpec(memory_space=pltpu.HBM)] * 2,
        out_specs=[VMEM] * 6,
        out_shape=shapes,
        scratch_shapes=[
            pltpu.VMEM((depth, cols // 2), bf16),
            pltpu.VMEM((cols // 2, rows), bf16),
            pltpu.SemaphoreType.DMA((2 * TILES + 1,)),
        ],
        compiler_params=params(12),
        cost_estimate=cost(rows * depth * cols, 4 * depth * cols),
        name="first_product",
    )(place, memory, resident)
    return odd, lhs, even_resident


def depth_half(place_ref, side, resident_ref):
    half = resident_ref.shape[0] // 2
    return pl.ds(pl.multiple_of((place_ref[C] ^ side) * half, half), half)


def early_product_kernel(place_ref, lhs_ref, resident_ref, out_ref):
    right = resident_ref[depth_half(place_ref, 0, resident_ref), :]
    out_ref[...] = jnp.dot(lhs_ref[...], right, preferred_element_type=f32)


def early_product(place, lhs, resident):
    rows, depth = lhs.shape
    cols = resident.shape[1]
    return pl.pallas_call(
        early_product_kernel,
        in_specs=[SMEM, VMEM, VMEM],
        out_specs=VMEM,
        out_shape=jax.ShapeDtypeStruct((rows, cols), f32),
        compiler_params=params(6),
        cost_estimate=cost(2 * rows * depth * cols, 4 * rows * cols),
        name="early_product",
    )(place, lhs, resident)


def late_product_kernel(place_ref, early_ref, lhs_ref, resident_ref, *refs):
    out_refs, turned_ref = refs[:4], refs[4]
    right = resident_ref[depth_half(place_ref, 1, resident_ref), :]
    product = early_ref[...] + jnp.dot(lhs_ref[...], right, preferred_element_type=f32)
    turned_ref[...] = product.T.astype(bf16)
    store_shares(place_ref, turned_ref, out_refs)


def both_product_kernel(place_ref, own_ref, other_ref, resident_ref, *refs):
    out_refs, turned_ref = refs[:4], refs[4]
    product = None
    for side, lhs_ref in enumerate((own_ref, other_ref)):
        right = resident_ref[depth_half(place_ref, side, resident_ref), :]
        term = jnp.dot(lhs_ref[...], right, preferred_element_type=f32)
        product = term if product is None else product + term
    turned_ref[...] = product.T.astype(bf16)
    store_shares(place_ref, turned_ref, out_refs)


def second_product(kernel, place, left, lhs, resident, name):
    rows, depth = lhs.shape
    cols = resident.shape[1]
    return pl.pallas_call(
        kernel,
        in_specs=[SMEM] + [VMEM] * 3,
        out_specs=[VMEM] * 4,
        out_shape=[jax.ShapeDtypeStruct((cols // 4, rows), bf16)] * 4,
        scratch_shapes=[pltpu.VMEM((cols, rows), bf16)],
        compiler_params=params(6),
        cost_estimate=cost(2 * rows * depth * cols, 4 * cols * rows),
        name=name,
    )(place, left, lhs, resident)


def half_copy(side, place_ref, resident_ref, out_ref, sem):
    half = out_ref.shape[1]
    at = pl.ds(pl.multiple_of(((place_ref[Y] & 1) ^ side) * half, half), half)
    return pltpu.make_async_copy(resident_ref.at[:, at], out_ref, sem)


def bring_odd_kernel(
    place_ref, memory_ref, previous_ref, resident_ref, memory_out, one_out, two_out, odd_out, prior_ref, turned_ref, sems
):
    width, rows = one_out.shape
    start = position(place_ref[Y]) * 2 * width
    cols = pl.ds(pl.multiple_of(start, 128), 2 * width)
    copies = [
        pltpu.make_async_copy(previous_ref.at[:, :, cols], prior_ref, sems.at[0]),
        pltpu.make_async_copy(memory_ref.at[1], memory_out, sems.at[1]),
        half_copy(1, place_ref, resident_ref, odd_out, sems.at[2]),
    ]
    for copy in copies:
        copy.start()
    copies[0].wait()
    for front, out_ref in enumerate((one_out, two_out)):
        turned_ref[...] = prior_ref[front].astype(f32).T
        share = turned_ref[pl.ds(pl.multiple_of(place_ref[ZL] * width, width), width), :]
        out_ref[...] = share.astype(bf16)
    for copy in copies[1:]:
        copy.wait()


def bring_odd(place, memory, previous, resident):
    _, rows, depth = memory.shape
    cols = resident.shape[1]
    width = previous.shape[2] // 8
    shapes = [(rows, depth), (width, rows), (width, rows), (depth, cols // 2)]
    return pl.pallas_call(
        bring_odd_kernel,
        in_specs=[SMEM] + [HBM] * 3,
        out_specs=[VMEM] * 4,
        out_shape=[jax.ShapeDtypeStruct(shape, bf16) for shape in shapes],
        scratch_shapes=[
            pltpu.VMEM((2, rows, 2 * width), bf16),
            pltpu.VMEM((2 * width, rows), f32),
            pltpu.SemaphoreType.DMA((3,)),
        ],
        compiler_params=params(6),
        cost_estimate=cost(0, depth * (2 * rows + cols)),
        name="bring_odd",
    )(place, memory, previous, resident)


def bring_even_kernel(place_ref, resident_ref, even_out, sem):
    copy = half_copy(0, place_ref, resident_ref, even_out, sem)
    copy.start()
    copy.wait()


def bring_even(place, resident):
    depth, cols = resident.shape
    return pl.pallas_call(
        bring_even_kernel,
        in_specs=[SMEM, HBM],
        out_specs=VMEM,
        out_shape=jax.ShapeDtypeStruct((depth, cols // 2), bf16),
        scratch_shapes=[pltpu.SemaphoreType.DMA],
        compiler_params=params(4),
        cost_estimate=cost(0, depth * cols),
        name="bring_even",
    )(place, resident)


def place_pair(own, other, first, out_ref):
    near, far = own.astype(f32), other.astype(f32)
    low = jnp.where(first == 0, near, far)
    high = jnp.where(first == 0, far, near)
    out_ref[...] = jnp.concatenate([low, high], axis=0).T.astype(bf16)


def next_memory_kernel(side, place_ref, memory_ref, *refs):
    pair_refs, out_ref = refs[:4], refs[4]
    half = out_ref.shape[1]
    width = half // 4
    for dx in range(4):
        near, far = pair_refs[dx][0].astype(f32), pair_refs[dx ^ 2][1].astype(f32)
        start = position(((place_ref[X] - dx) & 3) ^ place_ref[Y]) * width
        low = jnp.where(place_ref[ZH] == 0, near, far)
        high = jnp.where(place_ref[ZH] == 0, far, near)
        pair = jnp.concatenate([low, high], axis=0).T
        at = pl.ds(pl.multiple_of((place_ref[C] ^ side) * half + start, 128), width)
        to = pl.ds(pl.multiple_of(start, 128), width)
        out_ref[:, to] = (memory_ref[:, at].astype(f32) + pair).astype(bf16)


def next_memory(side, place, memory, pairs):
    rows, depth = memory.shape
    return pl.pallas_call(
        functools.partial(next_memory_kernel, side),
        in_specs=[SMEM] + [VMEM] * 5,
        out_specs=VMEM,
        out_shape=jax.ShapeDtypeStruct((rows, depth // 2), bf16),
        compiler_params=params(6),
        cost_estimate=cost(rows * depth, 3 * rows * depth),
        name="next_memory",
    )(place, memory, *pairs)


def solve_into(part_refs, prior_ref, inverse_ref):
    summed = part_refs[0][...].astype(f32)
    for part_ref in part_refs[1:]:
        summed = summed + part_ref[...].astype(f32)
    source = prior_ref[...].astype(f32) - step_size * summed
    mixed = lax.dot_general(
        source,
        inverse_ref[...],
        (((1,), (1,)), ((), ())),
        precision=lax.Precision.HIGHEST,
        preferred_element_type=f32,
    )
    return (source + mixed).astype(bf16)


def flipped(values):
    rows, cols = values.shape
    strips = []
    pad = jnp.zeros((128 - ORB, 128), f32)
    for s in range(rows // ORB):
        pieces = []
        for q in range(cols // 128):
            block = values[s * ORB : (s + 1) * ORB, q * 128 : (q + 1) * 128]
            turned = jnp.concatenate([block, pad], axis=0).T
            piece = turned[:ORB]
            for t in range(1, 128 // ORB):
                piece = piece + pltpu.roll(turned[t * ORB : (t + 1) * ORB], t * ORB, 1)
            pieces.append(piece)
        strips.append(jnp.concatenate(pieces, axis=1))
    return jnp.concatenate(strips, axis=0)


def first_solve_kernel(place_ref, *refs):
    front_ref, energy_ref = refs[11:]
    front = solve_into(refs[:8], refs[8], refs[9])
    front_ref[...] = front
    values = front.astype(f32)
    mirror = flipped(values)
    rows, cols = values.shape
    coupling = jnp.tile(refs[10][...], (rows // ORB, cols // 128))
    energy_ref[...] = (mirror * mirror * values * coupling).astype(bf16)


def second_solve_kernel(place_ref, *refs):
    refs[10][...] = solve_into(refs[:8], refs[8], refs[9])


def solve(kernel, place, parts, prior, inverse, extra, outputs, name):
    width, rows = prior.shape
    return pl.pallas_call(
        kernel,
        in_specs=[SMEM] + [VMEM] * (len(parts) + 2 + len(extra)),
        out_specs=[VMEM] * outputs,
        out_shape=[jax.ShapeDtypeStruct((width, rows), bf16)] * outputs,
        compiler_params=params(8),
        cost_estimate=cost(12 * rows * rows * width, 24 * rows * width),
        name=name,
    )(place, *parts, prior, inverse, *extra)


def put_blocks(blocks, block_ref, sems, out_ref, front):
    width = block_ref.shape[2]
    copies = []
    for i, (start, write) in enumerate(blocks):
        write(block_ref.at[i])
        at = pl.ds(pl.multiple_of(start, 128), width)
        copies.append(pltpu.make_async_copy(block_ref.at[i], out_ref.at[front, :, at], sems.at[i]))
        copies[i].start()
    for copy in copies:
        copy.wait()


def join_one_kernel(place_ref, own_ref, other_ref, out_ref, block_ref, sems):
    def block(dy):
        def write(ref):
            place_pair(own_ref[dy], other_ref[dy], place_ref[ZL], ref)

        return position((place_ref[Y] - dy) & 3) * block_ref.shape[2], write

    put_blocks([block(dy) for dy in range(4)], block_ref, sems, out_ref, 0)


def join_two_kernel(place_ref, *refs):
    own_refs, twin_refs, (out_ref, block_ref, sems) = refs[:4], refs[4:8], refs[9:]

    def block(dy):
        def write(ref):
            place_pair(own_refs[dy][...], twin_refs[dy][...], place_ref[ZL], ref)

        return position((place_ref[Y] - dy) & 3) * block_ref.shape[2], write

    put_blocks([block(dy) for dy in range(4)], block_ref, sems, out_ref, 1)


def join(kernel, args, in_specs, shape, aliases, name):
    _, rows, cols = shape
    return pl.pallas_call(
        kernel,
        in_specs=in_specs,
        out_specs=HBM,
        out_shape=jax.ShapeDtypeStruct(shape, bf16),
        scratch_shapes=[pltpu.VMEM((4, rows, cols // 4), bf16), pltpu.SemaphoreType.DMA((4,))],
        input_output_aliases=aliases,
        compiler_params=params(6),
        cost_estimate=cost(rows * cols, 4 * rows * cols),
        name=name,
    )(*args)


def move(value, target):
    pairs = []
    for i in range(128):
        rest, c = divmod(i, 2)
        rest, zh = divmod(rest, 2)
        rest, x = divmod(rest, 4)
        y, zl = divmod(rest, 2)
        y, zl, x, zh = target(y, zl, x, zh)
        pairs.append((i, (((y * 2 + zl) * 4 + x) * 2 + zh) * 2 + c))
    return lax.ppermute(value, ALL, pairs)


def turn(flip):
    return lambda y, zl, x, zh: (x, zh, x ^ y ^ (2 * flip), zl ^ flip)


def scatter(shares, first):
    parts = []
    for k in (3, 2, 1, 0) if first == 0 else (1, 0, 3, 2):
        dy, dz = first + 2 * (k >> 1), k & 1
        if (dy, dz) == (0, 0):
            parts.append(shares[k])
        else:
            parts.append(move(shares[k], lambda y, zl, x, zh: (y ^ dy, zl ^ dz, x, zh)))
    return parts


def spread(pair, axis):
    pairs = {0: pair}
    for d in (2, 1, 3):
        pairs[d] = lax.ppermute(pair, axis, [(i, (i + d) % 4) for i in range(4)])
    return [pairs[d] for d in range(4)]


def per_device(resident, memory, previous, inverse_part, pair_coupling):
    place = jnp.stack([lax.axis_index(name) for name in ("x", "zh", "c", "y", "zl")]).astype(jnp.int32)
    coupling = jnp.tile(pair_coupling, (1, 128 // ORB))

    resident, memory, previous = in_hbm(resident), in_hbm(memory), in_hbm(previous)
    odd, lhs, even_resident = first_product(place, memory, resident)
    odd_parts = scatter(odd, 1)
    lhs, odd = lax.optimization_barrier((lhs, odd))
    even = half_product(place, lhs, even_resident)
    even_parts = scatter(even, 0)
    place, _, odd_parts = lax.optimization_barrier((place, even[0], odd_parts))
    memory, prior_one, prior_two, odd_resident = bring_odd(place, memory, previous, resident)
    parts = odd_parts + even_parts
    front_one, energy = solve(
        first_solve_kernel, place, parts, prior_one, inverse_part[0], [coupling], 2, "first_solve"
    )
    pair = [move(energy, turn(0)), move(energy, turn(1))]
    ones = spread(front_one, "y")
    own = spread(jnp.stack(pair), "x")
    later, _ = lax.optimization_barrier((place, pair))
    even_resident = bring_even(later, resident)
    for d in (1, 2, 3):
        own[d], _ = lax.optimization_barrier((own[d], even_resident))
    ones = jnp.stack(ones)
    others = lax.ppermute(ones, "zl", SWAP)
    other = [lax.ppermute(pair, "c", SWAP) for pair in own]
    own_lhs = next_memory(0, place, memory, own)
    early = early_product(place, own_lhs, odd_resident)
    other, early = lax.optimization_barrier((other, early))
    other_lhs = next_memory(1, place, memory, other)
    odd = second_product(late_product_kernel, place, early, other_lhs, odd_resident, "late_product")
    own_lhs, odd, others = lax.optimization_barrier((own_lhs, odd, others))
    even = second_product(both_product_kernel, place, own_lhs, other_lhs, even_resident, "both_product")
    parts = scatter(odd, 1) + scatter(even, 0)
    (front_two,) = solve(
        second_solve_kernel, place, parts, prior_two, inverse_part[1], [], 1, "second_solve"
    )
    twin = lax.ppermute(front_two, "zl", SWAP)
    chunks = [*spread(front_two, "y"), *spread(twin, "y")]
    fronts = join(join_one_kernel, (place, ones, others), [SMEM, VMEM, VMEM], previous.shape, {}, "join_one")
    return join(
        join_two_kernel, (place, *chunks, fronts), [SMEM] + [VMEM] * 8 + [HBM], previous.shape, {9: 0}, "join_two"
    )


def solution(mesh):
    fine = Mesh(mesh.devices.reshape(4, 2, 4, 2, 2), ALL)
    in_specs = (P(PASTS, SECONDS), P(None, None, PASTS), P(None, None, SECONDS), P(), P())
    out_specs = P(None, None, SECONDS)
    return jax.shard_map(
        per_device, mesh=fine, in_specs=in_specs, out_specs=out_specs, check_vma=False
    )
```
